32 devices in a mesh: groups: 2 (over y), basin: 4 (over z), member: 4 (over x, core).
Axes of the slice: x: 2, y: 2, z: 4, core: 2. Of those that a mesh axis runs over, the one named last changes fastest.
Arguments:
- runoff: bfloat16 [64, 32, 2048], P(('groups', 'basin'), 'member'), parts along dimension 0, may hold values from 0.099609375 to 3
- route_params: float32 [3, 64, 32], P(None, ('groups', 'basin'), 'member'), parts along dimension 1, may hold values from 0.1 to 0.5
- unit_shapes: float32 [3, 256], replicated, may hold values from 0 to 2
- level_map: int32 [64], P(('groups', 'basin')), parts along dimension 0, may hold values from 0 to 7, as said below
- down_map: int32 [64], P(('groups', 'basin')), parts along dimension 0, may hold values from 0 to 16, as said below
- gauge_reach: int32 [16], P(('groups', 'basin')), parts along dimension 0, may hold values from 0 to 7
- gauge_sigma: float32 [16], P(('groups', 'basin')), parts along dimension 0, may hold values from 0.5 to 5
- observed: float32 [16, 64], P(('groups', 'basin')), parts along dimension 0, may hold values from 0.5 to 5
- obs_noise: float32 [16, 32, 64], P(('groups', 'basin'), 'member'), parts along dimension 0, may hold values from -6 to 6
Outputs:
- flows: bfloat16 [64, 32, 2048], P(('groups', 'basin'), 'member'), parts along dimension 0
- new_params: float32 [3, 64, 32], P(None, ('groups', 'basin'), 'member'), parts along dimension 1
The draws below stay inside these ranges and needn't reach their ends.
There are 2 independent parts, one for each index of `groups`. The reference program is written for one: setup_inputs(seed, part) draws one part's arguments, and reference() takes and returns one part's arrays. A program takes and returns all parts, laid end to end along the dimension named above; an argument that names none is the same for every part. Nothing has to cross between parts.
Inputs may be any that keep to these rules, and one draw needn't show every extreme that they name: `level_map`: within one block of 8 reaches at most 2 reaches share a level, and some level of each block holds exactly 2. `down_map`: encodes the target as in the reference program; a target's level is always higher than its source's, and reaches of the last block never target a next block. `gauge_reach`: index of the gauged reach within its block of 8 reaches; gauge g lies in block g // 2.
All inputs are finite; a program needn't handle non-finite values.
Results may differ from the reference program's by a relative error of at most 0.0023.
Values may be sent and summed in bfloat16 or wider, within the bound.
No kernel may reach another device: no remote copies, remote signals or barrier semaphores. Data moves between devices by JAX's collectives and lax.ppermute only.
A program may use at most 192 MiB of HBM per device.

```python
import math
import jax
import jax.numpy as jnp
from jax import lax

STEPS = 2048
KERNEL = 256
SHAPES = 3
LEVELS = 8
WINDOWS = 64
G_DEV = 2
R_DEV = 8
CAP = 2
REACHES = 32
MEMBERS = 32
GAUGES = 8
N_BASIN = 4


def network(key):
    base_key = jax.random.fold_in(key, 11)
    sub_keys = jax.random.split(base_key, 5)
    slot_total = LEVELS * CAP
    busy_level = jax.random.randint(sub_keys[0], (N_BASIN, 1), 0, LEVELS)
    slot_ids = jnp.arange(slot_total, dtype=jnp.int32)[None, :]
    scores = jax.random.randint(sub_keys[1], (N_BASIN, slot_total), 0, 1 << 20) * slot_total + slot_ids
    scores = jnp.where(slot_ids // CAP == busy_level, slot_ids - slot_total, scores)
    chosen = jnp.argsort(scores, axis=1)[:, :R_DEV].astype(jnp.int32) // CAP
    mixing = jax.random.randint(sub_keys[2], (N_BASIN, R_DEV), 0, 1 << 20) * R_DEV + jnp.arange(R_DEV, dtype=jnp.int32)[None, :]
    placing = jnp.argsort(mixing, axis=1).astype(jnp.int32)
    levels = jnp.take_along_axis(chosen, placing, axis=1)
    options = 2 * R_DEV + 1
    next_levels = jnp.concatenate([levels[1:], jnp.full((1, R_DEV), -1, jnp.int32)], axis=0)
    candidate = jnp.concatenate([levels, next_levels], axis=1)
    allowed = candidate[:, None, :] > levels[:, :, None]
    allowed = jnp.concatenate([allowed, jnp.ones((N_BASIN, R_DEV, 1), dtype=bool)], axis=2)
    wanted_kind = jax.random.randint(sub_keys[3], (N_BASIN, R_DEV, 1), 0, 4)
    wanted = jnp.where(wanted_kind < 2, 0, wanted_kind - 1)
    category = jnp.concatenate([jnp.zeros((R_DEV,), jnp.int32), jnp.ones((R_DEV,), jnp.int32), jnp.full((1,), 2, jnp.int32)])
    random_rank = jax.random.randint(sub_keys[4], (N_BASIN, R_DEV, options), 0, 1 << 20) * options + jnp.arange(options, dtype=jnp.int32)
    option_score = random_rank + jnp.where(category[None, None, :] == wanted, 1 << 26, 0)
    option_score = jnp.where(allowed, option_score + 1, 0)
    targets = jnp.argmax(option_score, axis=2).astype(jnp.int32)
    return (levels.reshape(-1), targets.reshape(-1))


def draw_level_map(key, part):
    return network(key)[0]


def draw_down_map(key, part):
    return network(key)[1]


def touch_ends(drawn, rng, smallest, high):
    spot = [jax.random.randint(jax.random.fold_in(rng, axis), (), 0, length) for axis, length in enumerate(drawn.shape)]
    widest = drawn.shape.index(max(drawn.shape))
    beside = spot[:widest] + [(spot[widest] + 1) % drawn.shape[widest]] + spot[widest + 1:]
    return drawn.at[tuple(spot)].set(smallest).at[tuple(beside)].set(high)


def steps_of(rng, shape, cuts, low, largest):
    def one(axis_at, blocks):
        steps = jax.random.uniform(jax.random.fold_in(jax.random.fold_in(rng, 6), axis_at), (blocks,), jnp.float32, low / len(cuts), largest / len(cuts))
        return jnp.repeat(jnp.exp(steps), shape[axis_at] // blocks).reshape((-1,) + (1,) * (len(shape) - axis_at - 1))

    loudness = one(*cuts[0])
    for cut in cuts[1:]:
        loudness = loudness * one(*cut)
    return loudness


def noise(own_key, extent, scale, reach, cuts=(), kind=jnp.bfloat16):
    gain = steps_of(own_key, extent, cuts, -0.22, 0.18) if cuts else 1.0
    array = jax.random.normal(own_key, extent, jnp.float32) * scale * gain
    return jnp.minimum(jnp.maximum(array, -reach), reach).astype(kind)


def setup_inputs(seed: int = 0, part: int = 0) -> dict:
    keys = jax.random.split(jax.random.key(seed), 10)
    part_splits = jax.random.split(jax.random.fold_in(keys[9], part), 10)
    return {
        "runoff": jnp.clip(jnp.exp(math.log(3.0) - 3.4051113 * jax.random.uniform(part_splits[0], (REACHES, MEMBERS, STEPS), jnp.float32) ** steps_of(part_splits[0], (REACHES, MEMBERS, STEPS), ((0, 4), (1, 4)), -0.2, 0.2)), 0.099609375, 3.0).astype(jnp.bfloat16),
        "route_params": jnp.clip(0.1 + 0.4 * jax.random.uniform(part_splits[1], (SHAPES, REACHES, MEMBERS), jnp.float32) ** steps_of(part_splits[1], (SHAPES, REACHES, MEMBERS), ((1, 4), (2, 4)), -0.2, 0.2), 0.1, 0.5),
        "unit_shapes": jnp.clip(jax.random.uniform(keys[2], (SHAPES, KERNEL), jnp.float32, 0.0, 2.0), 0.0, 2.0),
        "level_map": draw_level_map(jax.random.fold_in(jax.random.fold_in(keys[9], part), 71), part),
        "down_map": draw_down_map(jax.random.fold_in(jax.random.fold_in(keys[9], part), 71), part),
        "gauge_reach": touch_ends(jax.random.randint(part_splits[5], (GAUGES,), 0, R_DEV), jax.random.fold_in(part_splits[5], 1), 0, R_DEV - 1).astype(jnp.int32),
        "gauge_sigma": jnp.clip(jnp.exp(math.log(5.0) - 2.3025851 * jax.random.uniform(part_splits[6], (GAUGES,), jnp.float32) ** steps_of(part_splits[6], (GAUGES,), ((0, 4),), -0.2, 0.2)), 0.5, 5.0),
        "observed": jnp.clip(0.5 + 4.5 * jax.random.uniform(part_splits[7], (GAUGES, WINDOWS), jnp.float32) ** steps_of(part_splits[7], (GAUGES, WINDOWS), ((0, 4),), -0.2, 0.2), 0.5, 5.0),
        "obs_noise": noise(part_splits[8], (GAUGES, MEMBERS, WINDOWS), 1.0, 6.0, ((0, 4), (1, 4)), jnp.float32),
    }


def kernel_table(unit_shapes):
    block_len = unit_shapes.shape[1]
    row_ids = jnp.arange(2 * block_len, dtype=jnp.int32)[:, None]
    col_ids = jnp.arange(block_len, dtype=jnp.int32)[None, :]
    lag_index = jnp.where(row_ids < block_len, col_ids - row_ids, 2 * block_len + col_ids - row_ids)
    usable = (lag_index >= 0) & (lag_index < block_len)
    shape_values = jnp.take(unit_shapes, jnp.clip(lag_index, 0, block_len - 1), axis=1)
    shape_values = jnp.where(usable[None], shape_values, 0.0) / block_len
    return jnp.transpose(shape_values, (1, 0, 2)).reshape(2 * block_len, -1).astype(jnp.bfloat16)

def route_rows(inflow_rows, slot_weights, conv_table):
    block_len = conv_table.shape[0] // 2
    row_count, series_len = inflow_rows.shape
    blocks = inflow_rows.reshape(row_count, series_len // block_len, block_len)
    earlier = jnp.concatenate([jnp.zeros_like(blocks[:, :1]), blocks[:, :-1]], axis=1)
    joined = jnp.concatenate([blocks, earlier], axis=2).reshape(-1, 2 * block_len)
    mixed_blocks = jnp.dot(joined.astype(jnp.float32), conv_table.astype(jnp.float32), preferred_element_type=jnp.float32)
    mixed_blocks = mixed_blocks.reshape(row_count, series_len // block_len, slot_weights.shape[1], block_len)
    return lax.optimization_barrier(jnp.sum(mixed_blocks * slot_weights[:, None, :, None], axis=2)).reshape(row_count, series_len)

def level_slots(level_block, level_now, slot_count):
    entry_count = level_block.shape[-1]
    sort_key = (level_block != level_now).astype(jnp.int32) * entry_count + jnp.arange(entry_count, dtype=jnp.int32)
    slot_order = jnp.argsort(sort_key, axis=-1)[..., :slot_count].astype(jnp.int32)
    slot_valid = jnp.take_along_axis(level_block, slot_order, axis=-1) == level_now
    return (slot_order, slot_valid)

def reference(runoff, route_params, unit_shapes, level_map, down_map, gauge_reach, gauge_sigma, observed, obs_noise):
    conv_table = kernel_table(unit_shapes)
    members = runoff.shape[1]
    series_len = runoff.shape[2]
    flat_len = members * series_len
    inflow = runoff.astype(jnp.float32).reshape(N_BASIN, R_DEV, flat_len)
    outflow = jnp.zeros_like(inflow)
    levels = level_map.reshape(N_BASIN, R_DEV)
    down_block = down_map.reshape(N_BASIN, R_DEV)
    params = route_params.reshape(SHAPES, N_BASIN, R_DEV, members)
    reach_ids = jnp.arange(R_DEV, dtype=jnp.int32)[None, :, None]
    for level_now in range(LEVELS):
        slot_order, slot_valid = level_slots(levels, level_now, CAP)
        gathered = jnp.take_along_axis(inflow, slot_order[:, :, None], axis=1).astype(jnp.bfloat16)
        slot_weights = jnp.take_along_axis(params, slot_order[None, :, :, None], axis=2)
        slot_weights = jnp.transpose(slot_weights, (1, 2, 3, 0)).reshape(-1, SHAPES)
        routed = route_rows(gathered.reshape(-1, series_len), slot_weights, conv_table)
        routed = routed.astype(jnp.bfloat16).reshape(N_BASIN, CAP, flat_len).astype(jnp.float32)
        slot_target = jnp.take_along_axis(down_block, slot_order, axis=1)[:, None, :]
        slot_mask = slot_valid[:, None, :]
        local_edges = ((slot_target == reach_ids) & slot_mask).astype(jnp.float32)
        onward = ((slot_target == reach_ids + R_DEV) & slot_mask).astype(jnp.float32)
        chosen = ((slot_order[:, None, :] == reach_ids) & slot_mask).astype(jnp.float32)
        inflow = inflow + jnp.einsum('nrc,ncw->nrw', local_edges, routed)
        passed = jnp.einsum('nrc,ncw->nrw', onward, routed)
        inflow = inflow + jnp.concatenate([jnp.zeros_like(passed[:1]), passed[:-1]], axis=0)
        outflow = outflow + jnp.einsum('nrc,ncw->nrw', chosen, routed)
    flows = outflow.astype(jnp.bfloat16).reshape(N_BASIN * R_DEV, members, series_len)
    owners = jnp.arange(N_BASIN * G_DEV, dtype=jnp.int32) // G_DEV
    gauged = flows[(owners * R_DEV + gauge_reach).astype(jnp.int32)].astype(jnp.float32)
    predicted = lax.optimization_barrier(jnp.mean(gauged.reshape(-1, members, WINDOWS, series_len // WINDOWS), axis=3))
    scaled = predicted / gauge_sigma[:, None, None]
    innovation = observed[:, None, :] / gauge_sigma[:, None, None] + obs_noise - scaled
    scaled = jnp.transpose(scaled, (0, 2, 1)).reshape(-1, members)
    innovation = jnp.transpose(innovation, (0, 2, 1)).reshape(-1, members)
    spread = (scaled - lax.optimization_barrier(jnp.mean(scaled, axis=1, keepdims=True))) / jnp.sqrt(members - 1.0)
    gram = jnp.eye(members, dtype=jnp.float32) + jnp.dot(spread.T, spread, precision=lax.Precision.HIGHEST)
    cross = jnp.dot(spread.T, innovation, precision=lax.Precision.HIGHEST)
    factor = jnp.linalg.cholesky(gram)
    kalman_gain = jax.scipy.linalg.cho_solve((factor, True), cross)
    flat_theta = route_params.reshape(-1, members)
    anomaly = flat_theta - lax.optimization_barrier(jnp.mean(flat_theta, axis=1, keepdims=True))
    updated = flat_theta + jnp.dot(anomaly, kalman_gain, precision=lax.Precision.HIGHEST) / jnp.sqrt(members - 1.0)
    return (flows, updated.reshape(route_params.shape))
```

```python
import functools

import jax
import jax.numpy as jnp
from jax import lax
from jax.experimental import pallas as pl
from jax.experimental.pallas import tpu as pltpu
from jax.sharding import PartitionSpec as P

LEVELS = 8
WINDOWS = 64
LANES = 128
EXTRA = 16
HIGHEST = lax.Precision.HIGHEST

def vmem():
    return pl.BlockSpec(memory_space=pltpu.VMEM)


def smem():
    return pl.BlockSpec(memory_space=pltpu.SMEM)


def table_body(shapes_ref, table_ref):
    shape_count, block_len = shapes_ref.shape
    for s in range(shape_count):
        lags = shapes_ref[s : s + 1, :] * (1.0 / block_len)
        lags = jnp.concatenate([lags, jnp.zeros_like(lags)], axis=1)
        skewed = pltpu.roll(
            jnp.broadcast_to(lags, (block_len, 2 * block_len)), 0, 1, stride=1, stride_axis=0
        ).astype(jnp.bfloat16)
        cols = slice(s * block_len, (s + 1) * block_len)
        table_ref[:block_len, cols] = skewed[:, :block_len]
        table_ref[block_len:, cols] = skewed[:, block_len:]


def kernel_table(unit_shapes):
    shape_count, block_len = unit_shapes.shape
    return pl.pallas_call(
        table_body,
        out_shape=jax.ShapeDtypeStruct((2 * block_len, shape_count * block_len), jnp.bfloat16),
        in_specs=[vmem()],
        out_specs=vmem(),
        name="table",
    )(unit_shapes)


def split_two(x):
    top = x.astype(jnp.bfloat16)
    rest = x - top.astype(jnp.float32)
    mid = rest.astype(jnp.bfloat16)
    return top, mid, rest - mid.astype(jnp.float32)


def pack_body(
    level_ref,
    down_ref,
    gauge_ref,
    sigma_ref,
    runoff_ref,
    params_ref,
    observed_ref,
    noise_ref,
    *rest,
):
    out_refs, (stage_ref, extra_ref) = rest[:-2], rest[-2:]
    reach_count, members_dev, series_len = runoff_ref.shape
    shape_count = params_ref.shape[0]
    gauge_count, windows = observed_ref.shape
    block_len = out_refs[0].shape[1]
    block_count = series_len // block_len
    share = members_dev // len(out_refs)
    rows = share * block_count
    here = lax.axis_index("basin")
    for r in range(reach_count):
        series = runoff_ref[r].astype(jnp.float32)
        for i in range(block_count):
            at = (r * block_count + i) * members_dev
            for h in range(block_len // LANES):
                lane = i * block_len + h * LANES
                stage_ref[h, at : at + members_dev, :] = series[:, lane : lane + LANES]
    extra_ref[...] = jnp.zeros(extra_ref.shape, jnp.float32)
    for g in range(gauge_count):
        extra_ref[:members_dev, g * windows : (g + 1) * windows] = (
            observed_ref[g : g + 1, :] / sigma_ref[g] + noise_ref[g]
        )
    lower = slice(members_dev, members_dev + reach_count)
    for s in range(shape_count):
        extra_ref[lower, s * members_dev : (s + 1) * members_dev] = params_ref[s]
    at_row = lax.broadcasted_iota(jnp.int32, (reach_count, LANES), 0)
    at_lane = lax.broadcasted_iota(jnp.int32, (reach_count, LANES), 1)
    base = shape_count * members_dev
    facts = extra_ref[lower, :]
    for r in range(reach_count):
        facts = jnp.where(
            (at_row == r) & (at_lane == base), level_ref[r].astype(jnp.float32), facts
        )
        facts = jnp.where(
            (at_row == r) & (at_lane == base + 1), down_ref[r].astype(jnp.float32), facts
        )
    for g in range(gauge_count):
        facts = jnp.where(
            (at_row == g) & (at_lane == base + 2), gauge_ref[g].astype(jnp.float32), facts
        )
        facts = jnp.where((at_row == g) & (at_lane == base + 3), sigma_ref[g], facts)
    upper_top, upper_mid, _ = split_two(extra_ref[:members_dev, :])
    lower_top, lower_mid, lower_low = split_two(facts)
    half = LANES // 2
    lower_top = jnp.where(
        at_lane < half, lower_top.astype(jnp.float32), pltpu.roll(lower_low, half, 1)
    )
    tops = jnp.concatenate([upper_top.astype(jnp.float32), lower_top], axis=0)
    mids = jnp.concatenate(
        [upper_mid.astype(jnp.float32), lower_mid.astype(jnp.float32)], axis=0
    )
    extras = jnp.concatenate([tops, mids], axis=1).astype(jnp.bfloat16)
    for k, out_ref in enumerate(out_refs):
        to = here ^ k
        for r in range(reach_count):
            for h in range(block_len // LANES):
                pieces = [
                    stage_ref[
                        h,
                        pl.ds(
                            r * block_count * members_dev + share * to + j,
                            block_count,
                            stride=members_dev,
                        ),
                        :,
                    ]
                    for j in range(share)
                ]
                out_ref[r * rows : (r + 1) * rows, h * LANES : (h + 1) * LANES] = jnp.concatenate(
                    pieces, axis=0
                ).astype(jnp.bfloat16)
        out_ref[reach_count * rows :, :] = extras


def route_body(table_ref, *rest, parts, reach_count, shape_count, gauge_count, members_dev):
    in_refs, rest = rest[:parts], rest[parts:]
    out_refs, rest = rest[:parts], rest[parts:]
    base_ref, state_ref, flows_ref, left_ref, facts_ref, facts_smem, slot_ref, count_ref, sem = rest
    block_len = table_ref.shape[0] // 2
    rows = state_ref.shape[1]
    share = members_dev // parts
    block_count = rows // share
    total = parts * reach_count
    cap = slot_ref.shape[0] // (LEVELS * parts)
    here = lax.axis_index("basin")
    half = LANES // 2
    base = shape_count * members_dev
    at_lane = lax.broadcasted_iota(jnp.int32, (reach_count, LANES), 1)
    facts_ref[total:, :] = jnp.zeros((facts_ref.shape[0] - total, LANES), jnp.float32)
    for k, in_ref in enumerate(in_refs):
        source = here ^ k
        extras = in_ref[reach_count * rows :, :].astype(jnp.float32)
        tops, mids = extras[:, :LANES], extras[:, LANES:]
        base_ref[source] = tops[:members_dev] + mids[:members_dev]
        low = pltpu.roll(tops[members_dev:], half, 1)
        facts_ref[pl.ds(pl.multiple_of(source * reach_count, reach_count), reach_count), :] = jnp.where(
            at_lane < half, tops[members_dev:] + (mids[members_dev:] + low), 0.0
        )
    copy = pltpu.make_async_copy(facts_ref, facts_smem, sem)
    copy.start()
    for k, in_ref in enumerate(in_refs):
        source = here ^ k
        for r in range(reach_count):
            state_ref[source * reach_count + r] = in_ref[r * rows : (r + 1) * rows, :].astype(
                jnp.float32
            )
    state_ref[total] = jnp.zeros(state_ref.shape[1:], jnp.float32)
    state_ref[total + 1] = jnp.zeros(state_ref.shape[1:], jnp.float32)
    copy.wait()

    def clear(i, carry):
        slot_ref[i] = total
        return carry

    lax.fori_loop(0, slot_ref.shape[0], clear, 0, unroll=True)

    def clear_count(i, carry):
        count_ref[i] = 0
        return carry

    lax.fori_loop(0, count_ref.shape[0], clear_count, 0, unroll=True)

    def enlist(i, carry):
        group = facts_smem[i, base].astype(jnp.int32) * parts + i // reach_count
        taken = count_ref[group]
        slot_ref[group * cap + jnp.minimum(taken, cap - 1)] = i
        count_ref[group] = taken + 1
        return carry

    lax.fori_loop(0, total, enlist, 0)
    first_row = lax.broadcasted_iota(jnp.int32, (block_count, block_len), 0) == 0
    slots = parts * cap

    def one_level(level_now, carry):
        picked = [slot_ref[level_now * slots + c] for c in range(slots)]
        for c in range(slots):
            rows_now = state_ref[picked[c]]
            left_ref[c * rows : (c + 1) * rows, :block_len] = rows_now.astype(jnp.bfloat16)
            earlier = [
                jnp.where(
                    first_row,
                    0.0,
                    pltpu.roll(rows_now[j * block_count : (j + 1) * block_count], 1, 0),
                )
                for j in range(share)
            ]
            left_ref[c * rows : (c + 1) * rows, block_len:] = jnp.concatenate(
                earlier, axis=0
            ).astype(jnp.bfloat16)
        left = left_ref[...]
        mixed = [
            jnp.dot(
                left,
                table_ref[:, s * block_len : (s + 1) * block_len],
                preferred_element_type=jnp.float32,
            )
            for s in range(shape_count)
        ]
        for c in range(slots):
            pieces = []
            for j in range(share):
                at = slice(c * rows + j * block_count, c * rows + (j + 1) * block_count)
                piece = None
                for s in range(shape_count):
                    weight = facts_smem[picked[c], s * members_dev + share * here + j]
                    term = mixed[s][at] * weight
                    piece = term if piece is None else piece + term
                pieces.append(piece)
            routed = jnp.concatenate(pieces, axis=0).astype(jnp.bfloat16)
            flows_ref[picked[c]] = routed
            jump = facts_smem[picked[c], base + 1].astype(jnp.int32)
            goal = (picked[c] // reach_count) * reach_count + jump
            kept = (jump < 2 * reach_count) & (goal < total) & (picked[c] < total)
            goal = jnp.where(kept, goal, total + 1)
            state_ref[goal] = state_ref[goal] + routed.astype(jnp.float32)
        return carry

    lax.fori_loop(0, LEVELS, one_level, 0)

    gauges = parts * gauge_count
    span = block_count * block_len // WINDOWS
    wide = gauges * WINDOWS
    per_block = WINDOWS // block_count
    lag_at = lax.broadcasted_iota(jnp.int32, (block_len, wide), 0)
    col_at = lax.broadcasted_iota(jnp.int32, (block_len, wide), 1)
    windowing = jnp.where(lag_at // span == col_at % per_block, 1.0 / span, 0.0).astype(
        jnp.bfloat16
    )
    for g in range(gauges):
        reach = (g // gauge_count) * reach_count + facts_smem[
            (g // gauge_count) * reach_count + g % gauge_count, base + 2
        ].astype(jnp.int32)
        left_ref[g * rows : (g + 1) * rows, :block_len] = flows_ref[reach]
    means = jnp.dot(
        left_ref[: gauges * rows, :block_len], windowing, preferred_element_type=jnp.float32
    )
    row_at = lax.broadcasted_iota(jnp.int32, (block_count, wide), 0)
    col_at = lax.broadcasted_iota(jnp.int32, (block_count, wide), 1)
    sigma_row = jnp.zeros((1, wide), jnp.float32)
    for g in range(gauges):
        sigma = facts_smem[(g // gauge_count) * reach_count + g % gauge_count, base + 3]
        sigma_row = jnp.where(col_at[:1] // WINDOWS == g, sigma, sigma_row)
    scaled = []
    for j in range(share):
        merged = jnp.zeros((block_count, wide), jnp.float32)
        for g in range(gauges):
            at = g * rows + j * block_count
            merged = jnp.where(
                (col_at // per_block) == g * block_count + row_at,
                means[at : at + block_count],
                merged,
            )
        scaled.append(jnp.sum(merged, axis=0, keepdims=True) / sigma_row)
    scaled = jnp.concatenate(scaled, axis=0)
    top, mid, low = split_two(scaled)
    chunks = []
    for part in (top.astype(jnp.float32), mid.astype(jnp.float32), low):
        chunks += [part[:, i * block_len : (i + 1) * block_len] for i in range(wide // block_len)]
    used = len(chunks) * share
    chunks.append(jnp.zeros((EXTRA - used, block_len), jnp.float32))
    extras = jnp.concatenate(chunks, axis=0).astype(jnp.bfloat16)
    for k, out_ref in enumerate(out_refs):
        to = here ^ k
        for r in range(reach_count):
            out_ref[r * rows : (r + 1) * rows, :] = flows_ref[to * reach_count + r]
        out_ref[reach_count * rows :, :] = extras


def gather_body(params_ref, *rest, wide):
    in_refs, (out_ref, tile_ref) = rest[:-2], rest[-2:]
    parts = len(in_refs)
    shape_count, reach_count, members_dev = params_ref.shape
    share = members_dev // parts
    block_len = in_refs[0].shape[1]
    here = lax.axis_index("basin")
    pieces = wide // block_len
    at_row = lax.broadcasted_iota(jnp.int32, (members_dev, block_len), 0)
    placed = [jnp.zeros((members_dev, block_len), jnp.float32)] * pieces
    for k, in_ref in enumerate(in_refs):
        extras = in_ref[...].astype(jnp.float32)
        for i in range(pieces):
            for j in range(share):
                value = sum(
                    extras[(p * pieces + i) * share + j : (p * pieces + i) * share + j + 1]
                    for p in range(3)
                )
                placed[i] = jnp.where(at_row == share * (here ^ k) + j, value, placed[i])
    for i in range(pieces):
        out_ref[:, i * block_len : (i + 1) * block_len] = placed[i]
    place_params(params_ref, tile_ref)
    out_ref[:, wide:] = tile_ref[...]


def place_params(params_ref, tile_ref):
    shape_count, _, members_dev = params_ref.shape
    members = members_dev * lax.axis_size("member")
    tile_ref[...] = jnp.zeros(tile_ref.shape, jnp.float32)
    for s in range(shape_count):
        tile_ref[:, s * members : s * members + members_dev] = params_ref[s]
    tile_ref[...] = pltpu.roll(tile_ref[...], lax.axis_index("member") * members_dev, 1)


def unpack_body(*refs, parts, reach_count):
    in_refs, (out_ref, stage_ref) = refs[:parts], refs[parts:]
    members_dev = out_ref.shape[1]
    block_len = in_refs[0].shape[1]
    share = members_dev // parts
    block_count = out_ref.shape[2] // block_len
    rows = share * block_count
    here = lax.axis_index("basin")
    for k, in_ref in enumerate(in_refs):
        source = here ^ k
        for r in range(reach_count):
            piece = in_ref[r * rows : (r + 1) * rows, :].astype(jnp.float32)
            for j in range(share):
                for h in range(block_len // LANES):
                    stage_ref[
                        h,
                        pl.ds(
                            r * block_count * members_dev + share * source + j,
                            block_count,
                            stride=members_dev,
                        ),
                        :,
                    ] = piece[j * block_count : (j + 1) * block_count, h * LANES : (h + 1) * LANES]
    for r in range(reach_count):
        for i in range(block_count):
            at = (r * block_count + i) * members_dev
            for h in range(block_len // LANES):
                lane = i * block_len + h * LANES
                out_ref[r, :, lane : lane + LANES] = stage_ref[
                    h, at : at + members_dev, :
                ].astype(jnp.bfloat16)


def solve_body(base_ref, params_ref, *rest):
    in_refs, (out_ref, all_ref, right_ref) = rest[:-3], rest[-3:]
    shape_count, reach_count, members_dev = params_ref.shape
    groups = len(in_refs)
    members = groups * members_dev
    wide = all_ref.shape[1]
    here = lax.axis_index("member")
    tiles = None
    for k, in_ref in enumerate(in_refs):
        at = pl.multiple_of((here ^ k) * members_dev, members_dev)
        all_ref[pl.ds(at, members_dev), :] = in_ref[:, :wide]
        tile = in_ref[:, wide:]
        tiles = tile if tiles is None else tiles + tile
    scaled = all_ref[...]
    root = jnp.sqrt(jnp.float32(members - 1))
    spread = (scaled - jnp.mean(scaled, axis=0, keepdims=True)) / root
    own = in_refs[0][:, :wide]
    right_ref[:members, :] = spread
    for n in range(base_ref.shape[0]):
        cols = slice(n * base_ref.shape[2], (n + 1) * base_ref.shape[2])
        right_ref[members : members + members_dev, cols] = base_ref[n] - own[:, cols]
    right_ref[members + members_dev :, :] = jnp.zeros(
        (right_ref.shape[0] - members - members_dev, wide), jnp.float32
    )
    system = lax.dot_general(
        spread,
        right_ref[...],
        (((1,), (1,)), ((), ())),
        precision=HIGHEST,
        preferred_element_type=jnp.float32,
    )
    row_at = lax.broadcasted_iota(jnp.int32, system.shape, 0)
    col_at = lax.broadcasted_iota(jnp.int32, system.shape, 1)
    system = system + jnp.where(row_at == col_at, 1.0, 0.0)
    for i in range(members):
        pivot_row = system[i : i + 1, :] / system[i : i + 1, i : i + 1]
        system = jnp.where(row_at == i, pivot_row, system - system[:, i : i + 1] * pivot_row)
    gain = system[:, members : members + members_dev]
    theta = jnp.concatenate(
        [tiles[:, s * members : (s + 1) * members] for s in range(shape_count)], axis=0
    )
    anomaly = theta - jnp.mean(theta, axis=1, keepdims=True)
    step = (
        jnp.dot(anomaly, gain, precision=HIGHEST, preferred_element_type=jnp.float32) / root
    )
    for s in range(shape_count):
        out_ref[s] = params_ref[s] + step[s * reach_count : (s + 1) * reach_count]


def exchanged(x, axis, by):
    length = lax.axis_size(axis)
    return lax.ppermute(x, axis, [(i, i ^ by) for i in range(length)])


def per_device_split(
    runoff,
    route_params,
    unit_shapes,
    level_map,
    down_map,
    gauge_reach,
    gauge_sigma,
    observed,
    obs_noise,
):
    f32, bf16 = jnp.float32, jnp.bfloat16
    parts, groups = lax.axis_size("basin"), lax.axis_size("member")
    reach_count, members_dev, series_len = runoff.shape
    shape_count, block_len = unit_shapes.shape
    gauge_count = observed.shape[0]
    block_count = series_len // block_len
    share = members_dev // parts
    rows = share * block_count
    total = parts * reach_count
    cap = reach_count // 4
    wide = parts * gauge_count * WINDOWS
    members = members_dev * groups
    sent = jax.ShapeDtypeStruct((reach_count * rows + EXTRA, block_len), bf16)
    packed = pl.pallas_call(
        pack_body,
        out_shape=[sent] * parts,
        in_specs=[smem()] * 4 + [vmem()] * 4,
        out_specs=[vmem()] * parts,
        scratch_shapes=[
            pltpu.VMEM((block_len // LANES, reach_count * members_dev * block_count, LANES), f32),
            pltpu.VMEM((members_dev + reach_count, LANES), f32),
        ],
        name="pack",
    )(level_map, down_map, gauge_reach, gauge_sigma, runoff, route_params, observed, obs_noise)
    arrived = [packed[0]] + [exchanged(packed[k], "basin", k) for k in range(1, parts)]
    conv_table = kernel_table(unit_shapes)
    *routed, noise_base = pl.pallas_call(
        functools.partial(
            route_body,
            parts=parts,
            reach_count=reach_count,
            shape_count=shape_count,
            gauge_count=gauge_count,
            members_dev=members_dev,
        ),
        out_shape=[sent] * parts
        + [jax.ShapeDtypeStruct((parts, members_dev, gauge_count * WINDOWS), f32)],
        in_specs=[vmem()] * (1 + parts),
        out_specs=[vmem()] * (parts + 1),
        scratch_shapes=[
            pltpu.VMEM((total + 2, rows, block_len), f32),
            pltpu.VMEM((total + 1, rows, block_len), bf16),
            pltpu.VMEM((parts * max(cap, gauge_count) * rows, 2 * block_len), bf16),
            pltpu.VMEM((total + 8, LANES), f32),
            pltpu.SMEM((total + 8, LANES), f32),
            pltpu.SMEM((LEVELS * parts * cap,), jnp.int32),
            pltpu.SMEM((LEVELS * parts,), jnp.int32),
            pltpu.SemaphoreType.DMA,
        ],
        name="route",
    )(conv_table, *arrived)
    returned = [routed[0]] + [exchanged(routed[k], "basin", k) for k in range(1, parts)]
    last = (reach_count * rows) // EXTRA
    local = pl.pallas_call(
        functools.partial(gather_body, wide=wide),
        grid=(1,),
        out_shape=jax.ShapeDtypeStruct((members_dev, wide + LANES), f32),
        in_specs=[pl.BlockSpec(route_params.shape, lambda i: (0, 0, 0))]
        + [pl.BlockSpec((EXTRA, block_len), lambda i: (last, 0))] * parts,
        out_specs=pl.BlockSpec((members_dev, wide + LANES), lambda i: (0, 0)),
        scratch_shapes=[pltpu.VMEM((reach_count, LANES), f32)],
        name="gather",
    )(route_params, *returned)
    everyone = [local] + [exchanged(local, "member", k) for k in range(1, groups)]
    flows = pl.pallas_call(
        functools.partial(unpack_body, parts=parts, reach_count=reach_count),
        out_shape=jax.ShapeDtypeStruct(runoff.shape, bf16),
        in_specs=[vmem()] * parts,
        out_specs=vmem(),
        scratch_shapes=[pltpu.VMEM((block_len // LANES, reach_count * members_dev * block_count, LANES), f32)],
        name="unpack",
    )(*returned)
    updated = pl.pallas_call(
        solve_body,
        out_shape=jax.ShapeDtypeStruct(route_params.shape, f32),
        in_specs=[vmem()] * (2 + groups),
        out_specs=vmem(),
        scratch_shapes=[pltpu.VMEM((members, wide), f32), pltpu.VMEM((LANES, wide), f32)],
        name="solve",
    )(noise_base, route_params, *everyone)
    return flows, updated


def power_of_two(x):
    return x & (x - 1) == 0


def per_device(*args):
    runoff, route_params, unit_shapes, _, _, _, _, observed, _ = args
    parts, groups = lax.axis_size("basin"), lax.axis_size("member")
    reach_count, members_dev, series_len = runoff.shape
    shape_count, block_len = unit_shapes.shape
    block_count = series_len // block_len
    gauge_count = observed.shape[0]
    wide = parts * gauge_count * WINDOWS
    share = max(members_dev // parts, 1)
    fits = (
        power_of_two(parts)
        and power_of_two(groups)
        and members_dev == share * parts
        and reach_count == 8
        and members_dev == 8
        and block_count == 8
        and series_len % block_len == 0
        and block_len == 2 * LANES
        and gauge_count * WINDOWS == LANES
        and wide % block_len == 0
        and 3 * share * (wide // block_len) <= EXTRA
        and (shape_count * members_dev + 4) * 2 <= LANES
        and shape_count * groups * members_dev <= LANES
        and groups * members_dev + members_dev <= LANES
    )
    if fits:
        return per_device_split(*args)
    return per_device_chain(*args)


def passed_along(x, axis, by):
    length = lax.axis_size(axis)
    pairs = [(i, i + by) for i in range(length) if 0 <= i + by < length]
    return lax.ppermute(x, axis, pairs)


def route_rows(inflow_rows, slot_weights, conv_table):
    block_len = conv_table.shape[0] // 2
    row_count, series_len = inflow_rows.shape
    blocks = inflow_rows.reshape(row_count, series_len // block_len, block_len)
    earlier = jnp.concatenate([jnp.zeros_like(blocks[:, :1]), blocks[:, :-1]], axis=1)
    joined = jnp.concatenate([blocks, earlier], axis=2).reshape(-1, 2 * block_len)
    mixed_blocks = jnp.dot(joined, conv_table, preferred_element_type=jnp.float32)
    mixed_blocks = mixed_blocks.reshape(
        row_count, series_len // block_len, slot_weights.shape[1], block_len
    )
    return jnp.sum(mixed_blocks * slot_weights[:, None, :, None], axis=2).reshape(
        row_count, series_len
    )


def level_select(level_block, down_block, level_now, slot_count):
    entry_count = level_block.shape[0]
    entry_ids = jnp.arange(entry_count, dtype=jnp.int32)
    in_level = level_block == level_now
    before = (entry_ids[None, :] < entry_ids[:, None]) & in_level[None, :]
    rank = jnp.sum(before.astype(jnp.int32), axis=1)
    slot_ids = jnp.arange(slot_count, dtype=jnp.int32)
    select = (rank[None, :] == slot_ids[:, None]) & in_level[None, :]
    slot_valid = slot_ids < jnp.sum(in_level.astype(jnp.int32))
    slot_target = jnp.sum(jnp.where(select, down_block[None, :], 0), axis=1)
    return (select, slot_valid, slot_target)


def per_device_chain(
    runoff,
    route_params,
    unit_shapes,
    level_map,
    down_map,
    gauge_reach,
    gauge_sigma,
    observed,
    obs_noise,
):
    conv_table = kernel_table(unit_shapes)
    reach_count, members_dev, series_len = runoff.shape
    flat_len = members_dev * series_len
    slot_count = reach_count // 4
    shape_count = route_params.shape[0]
    inflow = runoff.astype(jnp.float32).reshape(reach_count, flat_len)
    outflow = jnp.zeros_like(inflow)
    reach_ids = jnp.arange(reach_count, dtype=jnp.int32)[:, None]
    params_rows = jnp.transpose(route_params, (1, 2, 0))
    prev_level, prev_down = passed_along((level_map, down_map), "basin", 1)
    for level_now in range(LEVELS):
        select, slot_valid, slot_target_row = level_select(
            level_map, down_map, level_now, slot_count
        )
        gathered = jnp.dot(
            select.astype(jnp.bfloat16),
            inflow.astype(jnp.bfloat16),
            preferred_element_type=jnp.float32,
        )
        gathered = gathered.astype(jnp.bfloat16).reshape(slot_count * members_dev, series_len)
        slot_weights = jnp.einsum(
            "cr,rms->cms", select.astype(jnp.float32), params_rows, precision=lax.Precision.HIGHEST
        ).reshape(-1, shape_count)
        routed = (
            route_rows(gathered, slot_weights, conv_table)
            .astype(jnp.bfloat16)
            .reshape(slot_count, flat_len)
        )
        slot_target = slot_target_row[None, :]
        slot_mask = slot_valid[None, :]
        local_edges = (slot_target == reach_ids) & slot_mask
        chosen = jnp.transpose(select) & slot_mask
        edge_matrix = jnp.concatenate([local_edges, chosen], axis=0).astype(jnp.bfloat16)
        spread_flows = jnp.dot(edge_matrix, routed, preferred_element_type=jnp.float32)
        inflow = inflow + spread_flows[:reach_count]
        outflow = outflow + spread_flows[reach_count:]
        if level_now + 1 < LEVELS:
            arrived = passed_along(routed, "basin", 1)
            prev_select, prev_valid, prev_target = level_select(
                prev_level, prev_down, level_now, slot_count
            )
            incoming = (prev_target[None, :] == reach_ids + reach_count) & prev_valid[None, :]
            inflow = inflow + jnp.dot(
                incoming.astype(jnp.bfloat16), arrived, preferred_element_type=jnp.float32
            )
    flows = outflow.astype(jnp.bfloat16)
    gauge_pick = (gauge_reach[:, None] == jnp.arange(reach_count, dtype=jnp.int32)[None, :]).astype(
        jnp.bfloat16
    )
    gauged = jnp.dot(gauge_pick, flows, preferred_element_type=jnp.float32)
    predicted = jnp.mean(gauged.reshape(-1, members_dev, WINDOWS, series_len // WINDOWS), axis=3)
    scaled = predicted / gauge_sigma[:, None, None]
    innovation = observed[:, None, :] / gauge_sigma[:, None, None] + obs_noise - scaled
    scaled = jnp.transpose(scaled, (0, 2, 1))
    innovation = jnp.transpose(innovation, (0, 2, 1))
    scaled, innovation = (
        lax.all_gather(scaled, "member", axis=2, tiled=True),
        lax.all_gather(innovation, "member", axis=2, tiled=True),
    )
    members = scaled.shape[2]
    scaled = scaled.reshape(-1, members)
    innovation = innovation.reshape(-1, members)
    spread = (scaled - jnp.mean(scaled, axis=1, keepdims=True)) / jnp.sqrt(members - 1.0)
    gram_part = jnp.dot(spread.T, spread, precision=lax.Precision.HIGHEST)
    cross_part = jnp.dot(spread.T, innovation, precision=lax.Precision.HIGHEST)
    gram_part, cross_part = lax.psum((gram_part, cross_part), "basin")
    gram = jnp.eye(members, dtype=jnp.float32) + gram_part
    factor = jnp.linalg.cholesky(gram)
    kalman_gain = jax.scipy.linalg.cho_solve((factor, True), cross_part)
    col_start = lax.axis_index("member") * members_dev
    all_params = lax.all_gather(route_params, "member", axis=2, tiled=True).reshape(-1, members)
    anomaly = all_params - jnp.mean(all_params, axis=1, keepdims=True)
    columns = lax.dynamic_slice_in_dim(kalman_gain, col_start, members_dev, 1)
    increment = jnp.dot(anomaly, columns, precision=lax.Precision.HIGHEST)
    updated = route_params.reshape(-1, members_dev) + increment / jnp.sqrt(members - 1.0)
    return (
        flows.reshape(reach_count, members_dev, series_len),
        updated.reshape(route_params.shape),
    )


def solution(mesh):
    return jax.shard_map(
        per_device,
        mesh=mesh,
        in_specs=(
            P(("groups", "basin"), "member", None),
            P(None, ("groups", "basin"), "member"),
            P(),
            P(("groups", "basin")),
            P(("groups", "basin")),
            P(("groups", "basin")),
            P(("groups", "basin")),
            P(("groups", "basin"), None),
            P(("groups", "basin"), "member", None),
        ),
        out_specs=(P(("groups", "basin"), "member", None), P(None, ("groups", "basin"), "member")),
        check_vma=False,
    )
```

```python
import functools

import jax
import jax.numpy as jnp
from jax import lax
from jax.experimental import pallas as pl
from jax.experimental.pallas import tpu as pltpu
from jax.sharding import PartitionSpec as P

LEVELS = 8
WINDOWS = 64
LANES = 128
EXTRA = 16
HIGHEST = lax.Precision.HIGHEST

def vmem():
    return pl.BlockSpec(memory_space=pltpu.VMEM)


def smem():
    return pl.BlockSpec(memory_space=pltpu.SMEM)


def kept(x):
    return pltpu.with_memory_space_constraint(x, pltpu.VMEM)


def table_body(shapes_ref, table_ref):
    shape_count, block_len = shapes_ref.shape
    for s in range(shape_count):
        lags = shapes_ref[s : s + 1, :] * (1.0 / block_len)
        lags = jnp.concatenate([lags, jnp.zeros_like(lags)], axis=1)
        skewed = pltpu.roll(
            jnp.broadcast_to(lags, (block_len, 2 * block_len)), 0, 1, stride=1, stride_axis=0
        ).astype(jnp.bfloat16)
        cols = slice(s * block_len, (s + 1) * block_len)
        table_ref[:block_len, cols] = skewed[:, :block_len]
        table_ref[block_len:, cols] = skewed[:, block_len:]


def kernel_table(unit_shapes):
    shape_count, block_len = unit_shapes.shape
    return pl.pallas_call(
        table_body,
        out_shape=pltpu.VMEM((2 * block_len, shape_count * block_len), jnp.bfloat16),
        in_specs=[vmem()],
        out_specs=vmem(),
        name="table",
    )(unit_shapes)


def split_two(x):
    top = x.astype(jnp.bfloat16)
    rest = x - top.astype(jnp.float32)
    mid = rest.astype(jnp.bfloat16)
    return top, mid, rest - mid.astype(jnp.float32)


def pack_body(
    level_ref,
    down_ref,
    gauge_ref,
    sigma_ref,
    runoff_ref,
    params_ref,
    observed_ref,
    noise_ref,
    *rest,
):
    out_refs, (stage_ref, extra_ref) = rest[:-2], rest[-2:]
    reach_count, members_dev, series_len = runoff_ref.shape
    shape_count = params_ref.shape[0]
    gauge_count, windows = observed_ref.shape
    block_len = out_refs[0].shape[1]
    block_count = series_len // block_len
    share = members_dev // len(out_refs)
    rows = share * block_count
    here = lax.axis_index("basin")
    for r in range(reach_count):
        series = runoff_ref[r].astype(jnp.float32)
        for i in range(block_count):
            at = (r * block_count + i) * members_dev
            for h in range(block_len // LANES):
                lane = i * block_len + h * LANES
                stage_ref[h, at : at + members_dev, :] = series[:, lane : lane + LANES]
    extra_ref[...] = jnp.zeros(extra_ref.shape, jnp.float32)
    for g in range(gauge_count):
        extra_ref[:members_dev, g * windows : (g + 1) * windows] = (
            observed_ref[g : g + 1, :] / sigma_ref[g] + noise_ref[g]
        )
    lower = slice(members_dev, members_dev + reach_count)
    for s in range(shape_count):
        extra_ref[lower, s * members_dev : (s + 1) * members_dev] = params_ref[s]
    at_row = lax.broadcasted_iota(jnp.int32, (reach_count, LANES), 0)
    at_lane = lax.broadcasted_iota(jnp.int32, (reach_count, LANES), 1)
    base = shape_count * members_dev
    facts = extra_ref[lower, :]
    for r in range(reach_count):
        facts = jnp.where(
            (at_row == r) & (at_lane == base), level_ref[r].astype(jnp.float32), facts
        )
        facts = jnp.where(
            (at_row == r) & (at_lane == base + 1), down_ref[r].astype(jnp.float32), facts
        )
    for g in range(gauge_count):
        facts = jnp.where(
            (at_row == g) & (at_lane == base + 2), gauge_ref[g].astype(jnp.float32), facts
        )
        facts = jnp.where((at_row == g) & (at_lane == base + 3), sigma_ref[g], facts)
    upper_top, upper_mid, _ = split_two(extra_ref[:members_dev, :])
    lower_top, lower_mid, lower_low = split_two(facts)
    half = LANES // 2
    lower_top = jnp.where(
        at_lane < half, lower_top.astype(jnp.float32), pltpu.roll(lower_low, half, 1)
    )
    tops = jnp.concatenate([upper_top.astype(jnp.float32), lower_top], axis=0)
    mids = jnp.concatenate(
        [upper_mid.astype(jnp.float32), lower_mid.astype(jnp.float32)], axis=0
    )
    extras = jnp.concatenate([tops, mids], axis=1).astype(jnp.bfloat16)
    for k, out_ref in enumerate(out_refs):
        to = here ^ k
        for r in range(reach_count):
            for h in range(block_len // LANES):
                pieces = [
                    stage_ref[
                        h,
                        pl.ds(
                            r * block_count * members_dev + share * to + j,
                            block_count,
                            stride=members_dev,
                        ),
                        :,
                    ]
                    for j in range(share)
                ]
                out_ref[r * rows : (r + 1) * rows, h * LANES : (h + 1) * LANES] = jnp.concatenate(
                    pieces, axis=0
                ).astype(jnp.bfloat16)
        out_ref[reach_count * rows :, :] = extras


def route_body(table_ref, *rest, parts, reach_count, shape_count, gauge_count, members_dev):
    in_refs, rest = rest[:parts], rest[parts:]
    out_refs, rest = rest[:parts], rest[parts:]
    base_ref, state_ref, flows_ref, left_ref, facts_ref, facts_smem, slot_ref, count_ref, sem = rest
    block_len = table_ref.shape[0] // 2
    rows = state_ref.shape[1]
    share = members_dev // parts
    block_count = rows // share
    total = parts * reach_count
    cap = slot_ref.shape[0] // (LEVELS * parts)
    here = lax.axis_index("basin")
    half = LANES // 2
    base = shape_count * members_dev
    at_lane = lax.broadcasted_iota(jnp.int32, (reach_count, LANES), 1)
    facts_ref[total:, :] = jnp.zeros((facts_ref.shape[0] - total, LANES), jnp.float32)
    for k, in_ref in enumerate(in_refs):
        source = here ^ k
        extras = in_ref[reach_count * rows :, :].astype(jnp.float32)
        tops, mids = extras[:, :LANES], extras[:, LANES:]
        base_ref[source] = tops[:members_dev] + mids[:members_dev]
        low = pltpu.roll(tops[members_dev:], half, 1)
        facts_ref[pl.ds(pl.multiple_of(source * reach_count, reach_count), reach_count), :] = jnp.where(
            at_lane < half, tops[members_dev:] + (mids[members_dev:] + low), 0.0
        )
    copy = pltpu.make_async_copy(facts_ref, facts_smem, sem)
    copy.start()
    for k, in_ref in enumerate(in_refs):
        source = here ^ k
        for r in range(reach_count):
            state_ref[source * reach_count + r] = in_ref[r * rows : (r + 1) * rows, :].astype(
                jnp.float32
            )
    state_ref[total] = jnp.zeros(state_ref.shape[1:], jnp.float32)
    state_ref[total + 1] = jnp.zeros(state_ref.shape[1:], jnp.float32)
    copy.wait()

    def clear(i, carry):
        slot_ref[i] = total
        return carry

    lax.fori_loop(0, slot_ref.shape[0], clear, 0, unroll=True)

    def clear_count(i, carry):
        count_ref[i] = 0
        return carry

    lax.fori_loop(0, count_ref.shape[0], clear_count, 0, unroll=True)

    def enlist(i, carry):
        group = facts_smem[i, base].astype(jnp.int32) * parts + i // reach_count
        taken = count_ref[group]
        slot_ref[group * cap + jnp.minimum(taken, cap - 1)] = i
        count_ref[group] = taken + 1
        return carry

    lax.fori_loop(0, total, enlist, 0)
    first_row = lax.broadcasted_iota(jnp.int32, (block_count, block_len), 0) == 0
    slots = parts * cap

    def one_level(level_now, carry):
        picked = [slot_ref[level_now * slots + c] for c in range(slots)]
        for c in range(slots):
            rows_now = state_ref[picked[c]]
            left_ref[c * rows : (c + 1) * rows, :block_len] = rows_now.astype(jnp.bfloat16)
            earlier = [
                jnp.where(
                    first_row,
                    0.0,
                    pltpu.roll(rows_now[j * block_count : (j + 1) * block_count], 1, 0),
                )
                for j in range(share)
            ]
            left_ref[c * rows : (c + 1) * rows, block_len:] = jnp.concatenate(
                earlier, axis=0
            ).astype(jnp.bfloat16)
        left = left_ref[...]
        mixed = [
            jnp.dot(
                left,
                table_ref[:, s * block_len : (s + 1) * block_len],
                preferred_element_type=jnp.float32,
            )
            for s in range(shape_count)
        ]
        for c in range(slots):
            pieces = []
            for j in range(share):
                at = slice(c * rows + j * block_count, c * rows + (j + 1) * block_count)
                piece = None
                for s in range(shape_count):
                    weight = facts_smem[picked[c], s * members_dev + share * here + j]
                    term = mixed[s][at] * weight
                    piece = term if piece is None else piece + term
                pieces.append(piece)
            routed = jnp.concatenate(pieces, axis=0).astype(jnp.bfloat16)
            flows_ref[picked[c]] = routed
            jump = facts_smem[picked[c], base + 1].astype(jnp.int32)
            goal = (picked[c] // reach_count) * reach_count + jump
            kept = (jump < 2 * reach_count) & (goal < total) & (picked[c] < total)
            goal = jnp.where(kept, goal, total + 1)
            state_ref[goal] = state_ref[goal] + routed.astype(jnp.float32)
        return carry

    lax.fori_loop(0, LEVELS, one_level, 0)

    gauges = parts * gauge_count
    span = block_count * block_len // WINDOWS
    wide = gauges * WINDOWS
    per_block = WINDOWS // block_count
    lag_at = lax.broadcasted_iota(jnp.int32, (block_len, wide), 0)
    col_at = lax.broadcasted_iota(jnp.int32, (block_len, wide), 1)
    windowing = jnp.where(lag_at // span == col_at % per_block, 1.0 / span, 0.0).astype(
        jnp.bfloat16
    )
    for g in range(gauges):
        reach = (g // gauge_count) * reach_count + facts_smem[
            (g // gauge_count) * reach_count + g % gauge_count, base + 2
        ].astype(jnp.int32)
        left_ref[g * rows : (g + 1) * rows, :block_len] = flows_ref[reach]
    means = jnp.dot(
        left_ref[: gauges * rows, :block_len], windowing, preferred_element_type=jnp.float32
    )
    row_at = lax.broadcasted_iota(jnp.int32, (block_count, wide), 0)
    col_at = lax.broadcasted_iota(jnp.int32, (block_count, wide), 1)
    sigma_row = jnp.zeros((1, wide), jnp.float32)
    for g in range(gauges):
        sigma = facts_smem[(g // gauge_count) * reach_count + g % gauge_count, base + 3]
        sigma_row = jnp.where(col_at[:1] // WINDOWS == g, sigma, sigma_row)
    scaled = []
    for j in range(share):
        merged = jnp.zeros((block_count, wide), jnp.float32)
        for g in range(gauges):
            at = g * rows + j * block_count
            merged = jnp.where(
                (col_at // per_block) == g * block_count + row_at,
                means[at : at + block_count],
                merged,
            )
        scaled.append(jnp.sum(merged, axis=0, keepdims=True) / sigma_row)
    scaled = jnp.concatenate(scaled, axis=0)
    top, mid, low = split_two(scaled)
    chunks = []
    for part in (top.astype(jnp.float32), mid.astype(jnp.float32), low):
        chunks += [part[:, i * block_len : (i + 1) * block_len] for i in range(wide // block_len)]
    used = len(chunks) * share
    chunks.append(jnp.zeros((EXTRA - used, block_len), jnp.float32))
    extras = jnp.concatenate(chunks, axis=0).astype(jnp.bfloat16)
    for k, out_ref in enumerate(out_refs):
        to = here ^ k
        for r in range(reach_count):
            out_ref[r * rows : (r + 1) * rows, :] = flows_ref[to * reach_count + r]
        out_ref[reach_count * rows :, :] = extras


def gather_body(params_ref, *rest, wide):
    in_refs, (out_ref, tile_ref) = rest[:-2], rest[-2:]
    parts = len(in_refs)
    shape_count, reach_count, members_dev = params_ref.shape
    share = members_dev // parts
    block_len = in_refs[0].shape[1]
    here = lax.axis_index("basin")
    pieces = wide // block_len
    at_row = lax.broadcasted_iota(jnp.int32, (members_dev, block_len), 0)
    placed = [jnp.zeros((members_dev, block_len), jnp.float32)] * pieces
    for k, in_ref in enumerate(in_refs):
        extras = in_ref[in_ref.shape[0] - EXTRA :, :].astype(jnp.float32)
        for i in range(pieces):
            for j in range(share):
                value = sum(
                    extras[(p * pieces + i) * share + j : (p * pieces + i) * share + j + 1]
                    for p in range(3)
                )
                placed[i] = jnp.where(at_row == share * (here ^ k) + j, value, placed[i])
    for i in range(pieces):
        out_ref[:, i * block_len : (i + 1) * block_len] = placed[i]
    place_params(params_ref, tile_ref)
    out_ref[:, wide:] = tile_ref[...]


def place_params(params_ref, tile_ref):
    shape_count, _, members_dev = params_ref.shape
    members = members_dev * lax.axis_size("member")
    tile_ref[...] = jnp.zeros(tile_ref.shape, jnp.float32)
    for s in range(shape_count):
        tile_ref[:, s * members : s * members + members_dev] = params_ref[s]
    tile_ref[...] = pltpu.roll(tile_ref[...], lax.axis_index("member") * members_dev, 1)


def unpack_body(*refs, parts, reach_count):
    in_refs, (out_ref, stage_ref) = refs[:parts], refs[parts:]
    members_dev = out_ref.shape[1]
    block_len = in_refs[0].shape[1]
    share = members_dev // parts
    block_count = out_ref.shape[2] // block_len
    rows = share * block_count
    here = lax.axis_index("basin")
    for k, in_ref in enumerate(in_refs):
        source = here ^ k
        for r in range(reach_count):
            piece = in_ref[r * rows : (r + 1) * rows, :].astype(jnp.float32)
            for j in range(share):
                for h in range(block_len // LANES):
                    stage_ref[
                        h,
                        pl.ds(
                            r * block_count * members_dev + share * source + j,
                            block_count,
                            stride=members_dev,
                        ),
                        :,
                    ] = piece[j * block_count : (j + 1) * block_count, h * LANES : (h + 1) * LANES]
    for r in range(reach_count):
        for i in range(block_count):
            at = (r * block_count + i) * members_dev
            for h in range(block_len // LANES):
                lane = i * block_len + h * LANES
                out_ref[r, :, lane : lane + LANES] = stage_ref[
                    h, at : at + members_dev, :
                ].astype(jnp.bfloat16)


def solve_body(base_ref, params_ref, *rest):
    in_refs, (out_ref, all_ref, right_ref) = rest[:-3], rest[-3:]
    shape_count, reach_count, members_dev = params_ref.shape
    groups = len(in_refs)
    members = groups * members_dev
    wide = all_ref.shape[1]
    here = lax.axis_index("member")
    tiles = None
    for k, in_ref in enumerate(in_refs):
        at = pl.multiple_of((here ^ k) * members_dev, members_dev)
        all_ref[pl.ds(at, members_dev), :] = in_ref[:, :wide]
        tile = in_ref[:, wide:]
        tiles = tile if tiles is None else tiles + tile
    scaled = all_ref[...]
    root = jnp.sqrt(jnp.float32(members - 1))
    spread = (scaled - jnp.mean(scaled, axis=0, keepdims=True)) / root
    own = in_refs[0][:, :wide]
    right_ref[:members, :] = spread
    for n in range(base_ref.shape[0]):
        cols = slice(n * base_ref.shape[2], (n + 1) * base_ref.shape[2])
        right_ref[members : members + members_dev, cols] = base_ref[n] - own[:, cols]
    right_ref[members + members_dev :, :] = jnp.zeros(
        (right_ref.shape[0] - members - members_dev, wide), jnp.float32
    )
    system = lax.dot_general(
        spread,
        right_ref[...],
        (((1,), (1,)), ((), ())),
        precision=HIGHEST,
        preferred_element_type=jnp.float32,
    )
    row_at = lax.broadcasted_iota(jnp.int32, system.shape, 0)
    col_at = lax.broadcasted_iota(jnp.int32, system.shape, 1)
    system = system + jnp.where(row_at == col_at, 1.0, 0.0)
    for i in range(members):
        pivot_row = system[i : i + 1, :] / system[i : i + 1, i : i + 1]
        system = jnp.where(row_at == i, pivot_row, system - system[:, i : i + 1] * pivot_row)
    gain = system[:, members : members + members_dev]
    theta = jnp.concatenate(
        [tiles[:, s * members : (s + 1) * members] for s in range(shape_count)], axis=0
    )
    anomaly = theta - jnp.mean(theta, axis=1, keepdims=True)
    step = (
        jnp.dot(anomaly, gain, precision=HIGHEST, preferred_element_type=jnp.float32) / root
    )
    for s in range(shape_count):
        out_ref[s] = params_ref[s] + step[s * reach_count : (s + 1) * reach_count]


def exchanged(x, axis, by):
    length = lax.axis_size(axis)
    return lax.ppermute(x, axis, [(i, i ^ by) for i in range(length)])


def per_device_split(
    runoff,
    route_params,
    unit_shapes,
    level_map,
    down_map,
    gauge_reach,
    gauge_sigma,
    observed,
    obs_noise,
):
    f32, bf16 = jnp.float32, jnp.bfloat16
    parts, groups = lax.axis_size("basin"), lax.axis_size("member")
    reach_count, members_dev, series_len = runoff.shape
    shape_count, block_len = unit_shapes.shape
    gauge_count = observed.shape[0]
    block_count = series_len // block_len
    share = members_dev // parts
    rows = share * block_count
    total = parts * reach_count
    cap = reach_count // 4
    wide = parts * gauge_count * WINDOWS
    members = members_dev * groups
    sent = pltpu.VMEM((reach_count * rows + EXTRA, block_len), bf16)
    packed = pl.pallas_call(
        pack_body,
        out_shape=[sent] * parts,
        in_specs=[smem()] * 4 + [vmem()] * 4,
        out_specs=[vmem()] * parts,
        scratch_shapes=[
            pltpu.VMEM((block_len // LANES, reach_count * members_dev * block_count, LANES), f32),
            pltpu.VMEM((members_dev + reach_count, LANES), f32),
        ],
        name="pack",
    )(level_map, down_map, gauge_reach, gauge_sigma, runoff, route_params, observed, obs_noise)
    arrived = [packed[0]] + [exchanged(packed[k], "basin", k) for k in range(1, parts)]
    conv_table = kernel_table(unit_shapes)
    *routed, noise_base = pl.pallas_call(
        functools.partial(
            route_body,
            parts=parts,
            reach_count=reach_count,
            shape_count=shape_count,
            gauge_count=gauge_count,
            members_dev=members_dev,
        ),
        out_shape=[sent] * parts
        + [pltpu.VMEM((parts, members_dev, gauge_count * WINDOWS), f32)],
        in_specs=[vmem()] * (1 + parts),
        out_specs=[vmem()] * (parts + 1),
        scratch_shapes=[
            pltpu.VMEM((total + 2, rows, block_len), f32),
            pltpu.VMEM((total + 1, rows, block_len), bf16),
            pltpu.VMEM((parts * max(cap, gauge_count) * rows, 2 * block_len), bf16),
            pltpu.VMEM((total + 8, LANES), f32),
            pltpu.SMEM((total + 8, LANES), f32),
            pltpu.SMEM((LEVELS * parts * cap,), jnp.int32),
            pltpu.SMEM((LEVELS * parts,), jnp.int32),
            pltpu.SemaphoreType.DMA,
        ],
        name="route",
    )(kept(conv_table), *map(kept, arrived))
    returned = [routed[0]] + [exchanged(routed[k], "basin", k) for k in range(1, parts)]
    local = pl.pallas_call(
        functools.partial(gather_body, wide=wide),
        out_shape=pltpu.VMEM((members_dev, wide + LANES), f32),
        in_specs=[vmem()] * (1 + parts),
        out_specs=vmem(),
        scratch_shapes=[pltpu.VMEM((reach_count, LANES), f32)],
        name="gather",
    )(route_params, *map(kept, returned))
    everyone = [local] + [exchanged(local, "member", k) for k in range(1, groups)]
    flows = pl.pallas_call(
        functools.partial(unpack_body, parts=parts, reach_count=reach_count),
        out_shape=jax.ShapeDtypeStruct(runoff.shape, bf16),
        in_specs=[vmem()] * parts,
        out_specs=vmem(),
        scratch_shapes=[pltpu.VMEM((block_len // LANES, reach_count * members_dev * block_count, LANES), f32)],
        name="unpack",
    )(*map(kept, returned))
    updated = pl.pallas_call(
        solve_body,
        out_shape=jax.ShapeDtypeStruct(route_params.shape, f32),
        in_specs=[vmem()] * (2 + groups),
        out_specs=vmem(),
        scratch_shapes=[pltpu.VMEM((members, wide), f32), pltpu.VMEM((LANES, wide), f32)],
        name="solve",
    )(kept(noise_base), route_params, *map(kept, everyone))
    return flows, updated


def power_of_two(x):
    return x & (x - 1) == 0


def per_device(*args):
    runoff, route_params, unit_shapes, _, _, _, _, observed, _ = args
    parts, groups = lax.axis_size("basin"), lax.axis_size("member")
    reach_count, members_dev, series_len = runoff.shape
    shape_count, block_len = unit_shapes.shape
    block_count = series_len // block_len
    gauge_count = observed.shape[0]
    wide = parts * gauge_count * WINDOWS
    share = max(members_dev // parts, 1)
    fits = (
        power_of_two(parts)
        and power_of_two(groups)
        and members_dev == share * parts
        and reach_count == 8
        and members_dev == 8
        and block_count == 8
        and series_len % block_len == 0
        and block_len == 2 * LANES
        and gauge_count * WINDOWS == LANES
        and wide % block_len == 0
        and 3 * share * (wide // block_len) <= EXTRA
        and (shape_count * members_dev + 4) * 2 <= LANES
        and shape_count * groups * members_dev <= LANES
        and groups * members_dev + members_dev <= LANES
    )
    if fits:
        return per_device_split(*args)
    return per_device_chain(*args)


def passed_along(x, axis, by):
    length = lax.axis_size(axis)
    pairs = [(i, i + by) for i in range(length) if 0 <= i + by < length]
    return lax.ppermute(x, axis, pairs)


def route_rows(inflow_rows, slot_weights, conv_table):
    block_len = conv_table.shape[0] // 2
    row_count, series_len = inflow_rows.shape
    blocks = inflow_rows.reshape(row_count, series_len // block_len, block_len)
    earlier = jnp.concatenate([jnp.zeros_like(blocks[:, :1]), blocks[:, :-1]], axis=1)
    joined = jnp.concatenate([blocks, earlier], axis=2).reshape(-1, 2 * block_len)
    mixed_blocks = jnp.dot(joined, conv_table, preferred_element_type=jnp.float32)
    mixed_blocks = mixed_blocks.reshape(
        row_count, series_len // block_len, slot_weights.shape[1], block_len
    )
    return jnp.sum(mixed_blocks * slot_weights[:, None, :, None], axis=2).reshape(
        row_count, series_len
    )


def level_select(level_block, down_block, level_now, slot_count):
    entry_count = level_block.shape[0]
    entry_ids = jnp.arange(entry_count, dtype=jnp.int32)
    in_level = level_block == level_now
    before = (entry_ids[None, :] < entry_ids[:, None]) & in_level[None, :]
    rank = jnp.sum(before.astype(jnp.int32), axis=1)
    slot_ids = jnp.arange(slot_count, dtype=jnp.int32)
    select = (rank[None, :] == slot_ids[:, None]) & in_level[None, :]
    slot_valid = slot_ids < jnp.sum(in_level.astype(jnp.int32))
    slot_target = jnp.sum(jnp.where(select, down_block[None, :], 0), axis=1)
    return (select, slot_valid, slot_target)


def per_device_chain(
    runoff,
    route_params,
    unit_shapes,
    level_map,
    down_map,
    gauge_reach,
    gauge_sigma,
    observed,
    obs_noise,
):
    conv_table = kernel_table(unit_shapes)
    reach_count, members_dev, series_len = runoff.shape
    flat_len = members_dev * series_len
    slot_count = reach_count // 4
    shape_count = route_params.shape[0]
    inflow = runoff.astype(jnp.float32).reshape(reach_count, flat_len)
    outflow = jnp.zeros_like(inflow)
    reach_ids = jnp.arange(reach_count, dtype=jnp.int32)[:, None]
    params_rows = jnp.transpose(route_params, (1, 2, 0))
    prev_level, prev_down = passed_along((level_map, down_map), "basin", 1)
    for level_now in range(LEVELS):
        select, slot_valid, slot_target_row = level_select(
            level_map, down_map, level_now, slot_count
        )
        gathered = jnp.dot(
            select.astype(jnp.bfloat16),
            inflow.astype(jnp.bfloat16),
            preferred_element_type=jnp.float32,
        )
        gathered = gathered.astype(jnp.bfloat16).reshape(slot_count * members_dev, series_len)
        slot_weights = jnp.einsum(
            "cr,rms->cms", select.astype(jnp.float32), params_rows, precision=lax.Precision.HIGHEST
        ).reshape(-1, shape_count)
        routed = (
            route_rows(gathered, slot_weights, conv_table)
            .astype(jnp.bfloat16)
            .reshape(slot_count, flat_len)
        )
        slot_target = slot_target_row[None, :]
        slot_mask = slot_valid[None, :]
        local_edges = (slot_target == reach_ids) & slot_mask
        chosen = jnp.transpose(select) & slot_mask
        edge_matrix = jnp.concatenate([local_edges, chosen], axis=0).astype(jnp.bfloat16)
        spread_flows = jnp.dot(edge_matrix, routed, preferred_element_type=jnp.float32)
        inflow = inflow + spread_flows[:reach_count]
        outflow = outflow + spread_flows[reach_count:]
        if level_now + 1 < LEVELS:
            arrived = passed_along(routed, "basin", 1)
            prev_select, prev_valid, prev_target = level_select(
                prev_level, prev_down, level_now, slot_count
            )
            incoming = (prev_target[None, :] == reach_ids + reach_count) & prev_valid[None, :]
            inflow = inflow + jnp.dot(
                incoming.astype(jnp.bfloat16), arrived, preferred_element_type=jnp.float32
            )
    flows = outflow.astype(jnp.bfloat16)
    gauge_pick = (gauge_reach[:, None] == jnp.arange(reach_count, dtype=jnp.int32)[None, :]).astype(
        jnp.bfloat16
    )
    gauged = jnp.dot(gauge_pick, flows, preferred_element_type=jnp.float32)
    predicted = jnp.mean(gauged.reshape(-1, members_dev, WINDOWS, series_len // WINDOWS), axis=3)
    scaled = predicted / gauge_sigma[:, None, None]
    innovation = observed[:, None, :] / gauge_sigma[:, None, None] + obs_noise - scaled
    scaled = jnp.transpose(scaled, (0, 2, 1))
    innovation = jnp.transpose(innovation, (0, 2, 1))
    scaled, innovation = (
        lax.all_gather(scaled, "member", axis=2, tiled=True),
        lax.all_gather(innovation, "member", axis=2, tiled=True),
    )
    members = scaled.shape[2]
    scaled = scaled.reshape(-1, members)
    innovation = innovation.reshape(-1, members)
    spread = (scaled - jnp.mean(scaled, axis=1, keepdims=True)) / jnp.sqrt(members - 1.0)
    gram_part = jnp.dot(spread.T, spread, precision=lax.Precision.HIGHEST)
    cross_part = jnp.dot(spread.T, innovation, precision=lax.Precision.HIGHEST)
    gram_part, cross_part = lax.psum((gram_part, cross_part), "basin")
    gram = jnp.eye(members, dtype=jnp.float32) + gram_part
    factor = jnp.linalg.cholesky(gram)
    kalman_gain = jax.scipy.linalg.cho_solve((factor, True), cross_part)
    col_start = lax.axis_index("member") * members_dev
    all_params = lax.all_gather(route_params, "member", axis=2, tiled=True).reshape(-1, members)
    anomaly = all_params - jnp.mean(all_params, axis=1, keepdims=True)
    columns = lax.dynamic_slice_in_dim(kalman_gain, col_start, members_dev, 1)
    increment = jnp.dot(anomaly, columns, precision=lax.Precision.HIGHEST)
    updated = route_params.reshape(-1, members_dev) + increment / jnp.sqrt(members - 1.0)
    return (
        flows.reshape(reach_count, members_dev, series_len),
        updated.reshape(route_params.shape),
    )


def solution(mesh):
    return jax.shard_map(
        per_device,
        mesh=mesh,
        in_specs=(
            P(("groups", "basin"), "member", None),
            P(None, ("groups", "basin"), "member"),
            P(),
            P(("groups", "basin")),
            P(("groups", "basin")),
            P(("groups", "basin")),
            P(("groups", "basin")),
            P(("groups", "basin"), None),
            P(("groups", "basin"), "member", None),
        ),
        out_specs=(P(("groups", "basin"), "member", None), P(None, ("groups", "basin"), "member")),
        check_vma=False,
    )
```

```python
import functools

import jax
import jax.numpy as jnp
from jax import lax
from jax.experimental import pallas as pl
from jax.experimental.pallas import tpu as pltpu
from jax.sharding import PartitionSpec as P

LEVELS = 8
WINDOWS = 64
LANES = 128
EXTRA = 16
HIGHEST = lax.Precision.HIGHEST

def vmem():
    return pl.BlockSpec(memory_space=pltpu.VMEM)


def smem():
    return pl.BlockSpec(memory_space=pltpu.SMEM)


AHEAD = 8


def kept(x):
    return pltpu.with_memory_space_constraint(x, pltpu.VMEM)


def table_body(shapes_ref, table_ref):
    shape_count, block_len = shapes_ref.shape
    for s in range(shape_count):
        lags = shapes_ref[s : s + 1, :] * (1.0 / block_len)
        lags = jnp.concatenate([lags, jnp.zeros_like(lags)], axis=1)
        skewed = pltpu.roll(
            jnp.broadcast_to(lags, (block_len, 2 * block_len)), 0, 1, stride=1, stride_axis=0
        ).astype(jnp.bfloat16)
        cols = slice(s * block_len, (s + 1) * block_len)
        table_ref[:block_len, cols] = skewed[:, :block_len]
        table_ref[block_len:, cols] = skewed[:, block_len:]


def kernel_table(unit_shapes):
    shape_count, block_len = unit_shapes.shape
    return pl.pallas_call(
        table_body,
        out_shape=pltpu.VMEM((2 * block_len, shape_count * block_len), jnp.bfloat16),
        in_specs=[vmem()],
        out_specs=vmem(),
        name="table",
    )(unit_shapes)


def split_two(x):
    top = x.astype(jnp.bfloat16)
    rest = x - top.astype(jnp.float32)
    mid = rest.astype(jnp.bfloat16)
    return top, mid, rest - mid.astype(jnp.float32)


def pack_body(
    level_ref,
    down_ref,
    gauge_ref,
    sigma_ref,
    runoff_ref,
    params_ref,
    observed_ref,
    noise_ref,
    *rest,
):
    out_refs, (own_ref, tile_ref, stage_ref, extra_ref) = rest[:-4], rest[-4:]
    reach_count, members_dev, series_len = runoff_ref.shape
    shape_count = params_ref.shape[0]
    gauge_count, windows = observed_ref.shape
    block_len = out_refs[0].shape[1]
    block_count = series_len // block_len
    share = members_dev // len(out_refs)
    rows = share * block_count
    here = lax.axis_index("basin")
    for r in range(reach_count):
        series = runoff_ref[r].astype(jnp.float32)
        for i in range(block_count):
            at = (r * block_count + i) * members_dev
            for h in range(block_len // LANES):
                lane = i * block_len + h * LANES
                stage_ref[h, at : at + members_dev, :] = series[:, lane : lane + LANES]
    extra_ref[...] = jnp.zeros(extra_ref.shape, jnp.float32)
    for g in range(gauge_count):
        extra_ref[:members_dev, g * windows : (g + 1) * windows] = (
            observed_ref[g : g + 1, :] / sigma_ref[g] + noise_ref[g]
        )
    lower = slice(members_dev, members_dev + reach_count)
    for s in range(shape_count):
        extra_ref[lower, s * members_dev : (s + 1) * members_dev] = params_ref[s]
    at_row = lax.broadcasted_iota(jnp.int32, (reach_count, LANES), 0)
    at_lane = lax.broadcasted_iota(jnp.int32, (reach_count, LANES), 1)
    base = shape_count * members_dev
    facts = extra_ref[lower, :]
    cap = reach_count // 4
    facts = jnp.where(at_lane // cap == base // cap, jnp.float32(reach_count), facts)
    for r in range(reach_count):
        rank = jnp.int32(0)
        for q in range(r):
            rank = rank + (level_ref[q] == level_ref[r]).astype(jnp.int32)
        here_slot = (at_row == level_ref[r]) & (at_lane == base + rank)
        facts = jnp.where(here_slot, jnp.float32(r), facts)
        goal_slot = (at_row == level_ref[r]) & (at_lane == base + cap + rank)
        facts = jnp.where(goal_slot, down_ref[r].astype(jnp.float32), facts)
    for g in range(gauge_count):
        facts = jnp.where(
            (at_row == g) & (at_lane == base + 2 * cap), gauge_ref[g].astype(jnp.float32), facts
        )
        facts = jnp.where((at_row == g) & (at_lane == base + 2 * cap + 1), sigma_ref[g], facts)
    upper_top, upper_mid, _ = split_two(extra_ref[:members_dev, :])
    lower_top, lower_mid, lower_low = split_two(facts)
    half = LANES // 2
    lower_top = jnp.where(
        at_lane < half, lower_top.astype(jnp.float32), pltpu.roll(lower_low, half, 1)
    )
    tops = jnp.concatenate([upper_top.astype(jnp.float32), lower_top], axis=0)
    mids = jnp.concatenate(
        [upper_mid.astype(jnp.float32), lower_mid.astype(jnp.float32)], axis=0
    )
    extras = jnp.concatenate([tops, mids], axis=1).astype(jnp.bfloat16)
    for k, out_ref in enumerate(out_refs):
        to = here ^ k
        for r in range(reach_count):
            for h in range(block_len // LANES):
                pieces = [
                    stage_ref[
                        h,
                        pl.ds(
                            r * block_count * members_dev + share * to + j,
                            block_count,
                            stride=members_dev,
                        ),
                        :,
                    ]
                    for j in range(share)
                ]
                out_ref[r * rows : (r + 1) * rows, h * LANES : (h + 1) * LANES] = jnp.concatenate(
                    pieces, axis=0
                ).astype(jnp.bfloat16)
        out_ref[reach_count * rows :, :] = extras
    own_ref[...] = params_ref[...]
    place_params(params_ref, tile_ref)


def route_body(table_ref, *rest, parts, reach_count, shape_count, gauge_count, members_dev):
    in_refs, rest = rest[:parts], rest[parts:]
    out_refs, rest = rest[:parts], rest[parts:]
    base_ref, state_ref, flows_ref, left_ref, facts_ref, facts_smem, sem = rest
    block_len = table_ref.shape[0] // 2
    rows = state_ref.shape[1]
    share = members_dev // parts
    block_count = rows // share
    total = parts * reach_count
    cap = reach_count // 4
    here = lax.axis_index("basin")
    half = LANES // 2
    base = shape_count * members_dev
    at_lane = lax.broadcasted_iota(jnp.int32, (reach_count, LANES), 1)
    facts_ref[total:, :] = jnp.zeros((facts_ref.shape[0] - total, LANES), jnp.float32)
    for k, in_ref in enumerate(in_refs):
        source = here ^ k
        extras = in_ref[reach_count * rows :, :].astype(jnp.float32)
        tops, mids = extras[:, :LANES], extras[:, LANES:]
        base_ref[source] = tops[:members_dev] + mids[:members_dev]
        low = pltpu.roll(tops[members_dev:], half, 1)
        facts_ref[pl.ds(pl.multiple_of(source * reach_count, reach_count), reach_count), :] = jnp.where(
            at_lane < half, tops[members_dev:] + (mids[members_dev:] + low), 0.0
        )
    copy = pltpu.make_async_copy(facts_ref, facts_smem, sem)
    copy.start()
    for k, in_ref in enumerate(in_refs):
        source = here ^ k
        for r in range(reach_count):
            state_ref[source * reach_count + r] = in_ref[r * rows : (r + 1) * rows, :].astype(
                jnp.float32
            )
    state_ref[total] = jnp.zeros(state_ref.shape[1:], jnp.float32)
    state_ref[total + 1] = jnp.zeros(state_ref.shape[1:], jnp.float32)
    copy.wait()

    first_row = lax.broadcasted_iota(jnp.int32, (block_count, block_len), 0) == 0
    slots = parts * cap

    def one_level(level_now, carry):
        picked, goals = [], []
        for c in range(slots):
            at = (c // cap) * reach_count + level_now
            lane = base + c % cap
            reach = facts_smem[at, lane].astype(jnp.int32)
            goal = (c // cap) * reach_count + facts_smem[at, lane + cap].astype(jnp.int32)
            real = reach < reach_count
            kept_goal = (goal < (c // cap + 2) * reach_count) & (goal < total) & real
            picked.append(jnp.where(real, (c // cap) * reach_count + reach, total))
            goals.append(jnp.where(kept_goal, goal, total + 1))
        for c in range(slots):
            rows_now = state_ref[picked[c]]
            left_ref[c * rows : (c + 1) * rows, :block_len] = rows_now.astype(jnp.bfloat16)
            earlier = [
                jnp.where(
                    first_row,
                    0.0,
                    pltpu.roll(rows_now[j * block_count : (j + 1) * block_count], 1, 0),
                )
                for j in range(share)
            ]
            left_ref[c * rows : (c + 1) * rows, block_len:] = jnp.concatenate(
                earlier, axis=0
            ).astype(jnp.bfloat16)
        left = left_ref[...]
        mixed = [
            jnp.dot(
                left,
                table_ref[:, s * block_len : (s + 1) * block_len],
                preferred_element_type=jnp.float32,
            )
            for s in range(shape_count)
        ]
        for c in range(slots):
            pieces = []
            for j in range(share):
                at = slice(c * rows + j * block_count, c * rows + (j + 1) * block_count)
                piece = None
                for s in range(shape_count):
                    weight = facts_smem[picked[c], s * members_dev + share * here + j]
                    term = mixed[s][at] * weight
                    piece = term if piece is None else piece + term
                pieces.append(piece)
            routed = jnp.concatenate(pieces, axis=0).astype(jnp.bfloat16)
            flows_ref[picked[c]] = routed
            state_ref[goals[c]] = state_ref[goals[c]] + routed.astype(jnp.float32)
        return carry

    lax.fori_loop(0, LEVELS, one_level, 0)

    gauges = parts * gauge_count
    span = block_count * block_len // WINDOWS
    wide = gauges * WINDOWS
    per_block = WINDOWS // block_count
    lag_at = lax.broadcasted_iota(jnp.int32, (block_len, wide), 0)
    col_at = lax.broadcasted_iota(jnp.int32, (block_len, wide), 1)
    windowing = jnp.where(lag_at // span == col_at % per_block, 1.0 / span, 0.0).astype(
        jnp.bfloat16
    )
    for g in range(gauges):
        reach = (g // gauge_count) * reach_count + facts_smem[
            (g // gauge_count) * reach_count + g % gauge_count, base + 2 * cap
        ].astype(jnp.int32)
        left_ref[g * rows : (g + 1) * rows, :block_len] = flows_ref[reach]
    means = jnp.dot(
        left_ref[: gauges * rows, :block_len], windowing, preferred_element_type=jnp.float32
    )
    row_at = lax.broadcasted_iota(jnp.int32, (block_count, wide), 0)
    col_at = lax.broadcasted_iota(jnp.int32, (block_count, wide), 1)
    sigma_row = jnp.zeros((1, wide), jnp.float32)
    for g in range(gauges):
        sigma = facts_smem[(g // gauge_count) * reach_count + g % gauge_count, base + 2 * cap + 1]
        sigma_row = jnp.where(col_at[:1] // WINDOWS == g, sigma, sigma_row)
    scaled = []
    for j in range(share):
        merged = jnp.zeros((block_count, wide), jnp.float32)
        for g in range(gauges):
            at = g * rows + j * block_count
            merged = jnp.where(
                (col_at // per_block) == g * block_count + row_at,
                means[at : at + block_count],
                merged,
            )
        scaled.append(jnp.sum(merged, axis=0, keepdims=True) / sigma_row)
    scaled = jnp.concatenate(scaled, axis=0)
    top, mid, low = split_two(scaled)
    chunks = []
    for part in (top.astype(jnp.float32), mid.astype(jnp.float32), low):
        chunks += [part[:, i * block_len : (i + 1) * block_len] for i in range(wide // block_len)]
    used = len(chunks) * share
    chunks.append(jnp.zeros((EXTRA - used, block_len), jnp.float32))
    extras = jnp.concatenate(chunks, axis=0).astype(jnp.bfloat16)
    for k, out_ref in enumerate(out_refs):
        to = here ^ k
        for r in range(reach_count):
            out_ref[r * rows : (r + 1) * rows, :] = flows_ref[to * reach_count + r]
        out_ref[reach_count * rows :, :] = extras


def gather_body(tile_ref, *rest, wide):
    in_refs, out_ref = rest[:-1], rest[-1]
    parts = len(in_refs)
    members_dev = out_ref.shape[0]
    share = members_dev // parts
    block_len = in_refs[0].shape[1]
    here = lax.axis_index("basin")
    pieces = wide // block_len
    at_row = lax.broadcasted_iota(jnp.int32, (members_dev, block_len), 0)
    placed = [jnp.zeros((members_dev, block_len), jnp.float32)] * pieces
    for k, in_ref in enumerate(in_refs):
        extras = in_ref[in_ref.shape[0] - EXTRA :, :].astype(jnp.float32)
        for i in range(pieces):
            for j in range(share):
                value = sum(
                    extras[(p * pieces + i) * share + j : (p * pieces + i) * share + j + 1]
                    for p in range(3)
                )
                placed[i] = jnp.where(at_row == share * (here ^ k) + j, value, placed[i])
    for i in range(pieces):
        out_ref[:, i * block_len : (i + 1) * block_len] = placed[i]
    out_ref[:, wide:] = tile_ref[...]


def place_params(params_ref, tile_ref):
    shape_count, _, members_dev = params_ref.shape
    members = members_dev * lax.axis_size("member")
    tile_ref[...] = jnp.zeros(tile_ref.shape, jnp.float32)
    for s in range(shape_count):
        tile_ref[:, s * members : s * members + members_dev] = params_ref[s]
    tile_ref[...] = pltpu.roll(tile_ref[...], lax.axis_index("member") * members_dev, 1)


def unpack_body(*refs, parts, reach_count):
    in_refs, (out_ref, stage_ref) = refs[:parts], refs[parts:]
    members_dev = out_ref.shape[1]
    block_len = in_refs[0].shape[1]
    share = members_dev // parts
    block_count = out_ref.shape[2] // block_len
    rows = share * block_count
    here = lax.axis_index("basin")
    for k, in_ref in enumerate(in_refs):
        source = here ^ k
        for r in range(reach_count):
            piece = in_ref[r * rows : (r + 1) * rows, :].astype(jnp.float32)
            for j in range(share):
                for h in range(block_len // LANES):
                    stage_ref[
                        h,
                        pl.ds(
                            r * block_count * members_dev + share * source + j,
                            block_count,
                            stride=members_dev,
                        ),
                        :,
                    ] = piece[j * block_count : (j + 1) * block_count, h * LANES : (h + 1) * LANES]
    for r in range(reach_count):
        for i in range(block_count):
            at = (r * block_count + i) * members_dev
            for h in range(block_len // LANES):
                lane = i * block_len + h * LANES
                out_ref[r, :, lane : lane + LANES] = stage_ref[
                    h, at : at + members_dev, :
                ].astype(jnp.bfloat16)


def solve_body(base_ref, params_ref, *rest):
    in_refs, (out_ref, all_ref, right_ref) = rest[:-3], rest[-3:]
    shape_count, reach_count, members_dev = params_ref.shape
    groups = len(in_refs)
    members = groups * members_dev
    wide = all_ref.shape[1]
    here = lax.axis_index("member")
    tiles = None
    for k, in_ref in enumerate(in_refs):
        at = pl.multiple_of((here ^ k) * members_dev, members_dev)
        all_ref[pl.ds(at, members_dev), :] = in_ref[:, :wide]
        tile = in_ref[:, wide:]
        tiles = tile if tiles is None else tiles + tile
    scaled = all_ref[...]
    root = jnp.sqrt(jnp.float32(members - 1))
    spread = (scaled - jnp.mean(scaled, axis=0, keepdims=True)) / root
    own = in_refs[0][:, :wide]
    right_ref[:members, :] = spread
    for n in range(base_ref.shape[0]):
        cols = slice(n * base_ref.shape[2], (n + 1) * base_ref.shape[2])
        right_ref[members : members + members_dev, cols] = base_ref[n] - own[:, cols]
    right_ref[members + members_dev :, :] = jnp.zeros(
        (right_ref.shape[0] - members - members_dev, wide), jnp.float32
    )
    system = lax.dot_general(
        spread,
        right_ref[...],
        (((1,), (1,)), ((), ())),
        precision=HIGHEST,
        preferred_element_type=jnp.float32,
    )
    row_at = lax.broadcasted_iota(jnp.int32, system.shape, 0)
    col_at = lax.broadcasted_iota(jnp.int32, system.shape, 1)
    system = system + jnp.where(row_at == col_at, 1.0, 0.0)
    for first in range(0, members, AHEAD):
        cols = [
            jnp.broadcast_to(system[:, i : i + 1], system.shape)
            for i in range(first, first + AHEAD)
        ]
        for t in range(AHEAD):
            i = first + t
            own_row = row_at == i
            inverse = 1.0 / cols[t][i : i + 1, :]
            pivot_row = system[i : i + 1, :] * inverse
            system = jnp.where(own_row, pivot_row, system - cols[t] * pivot_row)
            for u in range(t + 1, AHEAD):
                pivot_row = cols[u][i : i + 1, :] * inverse
                cols[u] = jnp.where(own_row, pivot_row, cols[u] - cols[t] * pivot_row)
    gain = system[:, members : members + members_dev]
    theta = jnp.concatenate(
        [tiles[:, s * members : (s + 1) * members] for s in range(shape_count)], axis=0
    )
    anomaly = theta - jnp.mean(theta, axis=1, keepdims=True)
    step = (
        jnp.dot(anomaly, gain, precision=HIGHEST, preferred_element_type=jnp.float32) / root
    )
    for s in range(shape_count):
        out_ref[s] = params_ref[s] + step[s * reach_count : (s + 1) * reach_count]


def exchanged(x, axis, by):
    length = lax.axis_size(axis)
    return lax.ppermute(x, axis, [(i, i ^ by) for i in range(length)])


def per_device_split(
    runoff,
    route_params,
    unit_shapes,
    level_map,
    down_map,
    gauge_reach,
    gauge_sigma,
    observed,
    obs_noise,
):
    f32, bf16 = jnp.float32, jnp.bfloat16
    parts, groups = lax.axis_size("basin"), lax.axis_size("member")
    reach_count, members_dev, series_len = runoff.shape
    shape_count, block_len = unit_shapes.shape
    gauge_count = observed.shape[0]
    block_count = series_len // block_len
    share = members_dev // parts
    rows = share * block_count
    total = parts * reach_count
    cap = reach_count // 4
    wide = parts * gauge_count * WINDOWS
    members = members_dev * groups
    sent = pltpu.VMEM((reach_count * rows + EXTRA, block_len), bf16)
    *packed, own_params, tile = pl.pallas_call(
        pack_body,
        out_shape=[sent] * parts
        + [pltpu.VMEM(route_params.shape, f32), pltpu.VMEM((reach_count, LANES), f32)],
        in_specs=[smem()] * 4 + [vmem()] * 4,
        out_specs=[vmem()] * (parts + 2),
        scratch_shapes=[
            pltpu.VMEM((block_len // LANES, reach_count * members_dev * block_count, LANES), f32),
            pltpu.VMEM((members_dev + reach_count, LANES), f32),
        ],
        name="pack",
    )(level_map, down_map, gauge_reach, gauge_sigma, runoff, route_params, observed, obs_noise)
    arrived = [packed[0]] + [exchanged(packed[k], "basin", k) for k in range(1, parts)]
    conv_table = kernel_table(unit_shapes)
    *routed, noise_base = pl.pallas_call(
        functools.partial(
            route_body,
            parts=parts,
            reach_count=reach_count,
            shape_count=shape_count,
            gauge_count=gauge_count,
            members_dev=members_dev,
        ),
        out_shape=[sent] * parts
        + [pltpu.VMEM((parts, members_dev, gauge_count * WINDOWS), f32)],
        in_specs=[vmem()] * (1 + parts),
        out_specs=[vmem()] * (parts + 1),
        scratch_shapes=[
            pltpu.VMEM((total + 2, rows, block_len), f32),
            pltpu.VMEM((total + 1, rows, block_len), bf16),
            pltpu.VMEM((parts * max(cap, gauge_count) * rows, 2 * block_len), bf16),
            pltpu.VMEM((total + 8, LANES), f32),
            pltpu.SMEM((total + 8, LANES), f32),
            pltpu.SemaphoreType.DMA,
        ],
        name="route",
    )(kept(conv_table), *map(kept, arrived))
    returned = [routed[0]] + [exchanged(routed[k], "basin", k) for k in range(1, parts)]
    local = pl.pallas_call(
        functools.partial(gather_body, wide=wide),
        out_shape=pltpu.VMEM((members_dev, wide + LANES), f32),
        in_specs=[vmem()] * (1 + parts),
        out_specs=vmem(),
        name="gather",
    )(kept(tile), *map(kept, returned))
    everyone = [local] + [exchanged(local, "member", k) for k in range(1, groups)]
    flows = pl.pallas_call(
        functools.partial(unpack_body, parts=parts, reach_count=reach_count),
        out_shape=jax.ShapeDtypeStruct(runoff.shape, bf16),
        in_specs=[vmem()] * parts,
        out_specs=vmem(),
        scratch_shapes=[pltpu.VMEM((block_len // LANES, reach_count * members_dev * block_count, LANES), f32)],
        name="unpack",
    )(*map(kept, returned))
    updated = pl.pallas_call(
        solve_body,
        out_shape=jax.ShapeDtypeStruct(route_params.shape, f32),
        in_specs=[vmem()] * (2 + groups),
        out_specs=vmem(),
        scratch_shapes=[pltpu.VMEM((members, wide), f32), pltpu.VMEM((LANES, wide), f32)],
        name="solve",
    )(kept(noise_base), kept(own_params), *map(kept, everyone))
    return flows, updated


def power_of_two(x):
    return x & (x - 1) == 0


def per_device(*args):
    runoff, route_params, unit_shapes, _, _, _, _, observed, _ = args
    parts, groups = lax.axis_size("basin"), lax.axis_size("member")
    reach_count, members_dev, series_len = runoff.shape
    shape_count, block_len = unit_shapes.shape
    block_count = series_len // block_len
    gauge_count = observed.shape[0]
    wide = parts * gauge_count * WINDOWS
    share = max(members_dev // parts, 1)
    fits = (
        power_of_two(parts)
        and power_of_two(groups)
        and members_dev == share * parts
        and reach_count == 8
        and members_dev == 8
        and block_count == 8
        and series_len % block_len == 0
        and block_len == 2 * LANES
        and gauge_count * WINDOWS == LANES
        and wide % block_len == 0
        and 3 * share * (wide // block_len) <= EXTRA
        and (shape_count * members_dev + 8) * 2 <= LANES
        and reach_count == LEVELS
        and shape_count * groups * members_dev <= LANES
        and groups * members_dev + members_dev <= LANES
    )
    if fits:
        return per_device_split(*args)
    return per_device_chain(*args)


def passed_along(x, axis, by):
    length = lax.axis_size(axis)
    pairs = [(i, i + by) for i in range(length) if 0 <= i + by < length]
    return lax.ppermute(x, axis, pairs)


def route_rows(inflow_rows, slot_weights, conv_table):
    block_len = conv_table.shape[0] // 2
    row_count, series_len = inflow_rows.shape
    blocks = inflow_rows.reshape(row_count, series_len // block_len, block_len)
    earlier = jnp.concatenate([jnp.zeros_like(blocks[:, :1]), blocks[:, :-1]], axis=1)
    joined = jnp.concatenate([blocks, earlier], axis=2).reshape(-1, 2 * block_len)
    mixed_blocks = jnp.dot(joined, conv_table, preferred_element_type=jnp.float32)
    mixed_blocks = mixed_blocks.reshape(
        row_count, series_len // block_len, slot_weights.shape[1], block_len
    )
    return jnp.sum(mixed_blocks * slot_weights[:, None, :, None], axis=2).reshape(
        row_count, series_len
    )


def level_select(level_block, down_block, level_now, slot_count):
    entry_count = level_block.shape[0]
    entry_ids = jnp.arange(entry_count, dtype=jnp.int32)
    in_level = level_block == level_now
    before = (entry_ids[None, :] < entry_ids[:, None]) & in_level[None, :]
    rank = jnp.sum(before.astype(jnp.int32), axis=1)
    slot_ids = jnp.arange(slot_count, dtype=jnp.int32)
    select = (rank[None, :] == slot_ids[:, None]) & in_level[None, :]
    slot_valid = slot_ids < jnp.sum(in_level.astype(jnp.int32))
    slot_target = jnp.sum(jnp.where(select, down_block[None, :], 0), axis=1)
    return (select, slot_valid, slot_target)


def per_device_chain(
    runoff,
    route_params,
    unit_shapes,
    level_map,
    down_map,
    gauge_reach,
    gauge_sigma,
    observed,
    obs_noise,
):
    conv_table = kernel_table(unit_shapes)
    reach_count, members_dev, series_len = runoff.shape
    flat_len = members_dev * series_len
    slot_count = reach_count // 4
    shape_count = route_params.shape[0]
    inflow = runoff.astype(jnp.float32).reshape(reach_count, flat_len)
    outflow = jnp.zeros_like(inflow)
    reach_ids = jnp.arange(reach_count, dtype=jnp.int32)[:, None]
    params_rows = jnp.transpose(route_params, (1, 2, 0))
    prev_level, prev_down = passed_along((level_map, down_map), "basin", 1)
    for level_now in range(LEVELS):
        select, slot_valid, slot_target_row = level_select(
            level_map, down_map, level_now, slot_count
        )
        gathered = jnp.dot(
            select.astype(jnp.bfloat16),
            inflow.astype(jnp.bfloat16),
            preferred_element_type=jnp.float32,
        )
        gathered = gathered.astype(jnp.bfloat16).reshape(slot_count * members_dev, series_len)
        slot_weights = jnp.einsum(
            "cr,rms->cms", select.astype(jnp.float32), params_rows, precision=lax.Precision.HIGHEST
        ).reshape(-1, shape_count)
        routed = (
            route_rows(gathered, slot_weights, conv_table)
            .astype(jnp.bfloat16)
            .reshape(slot_count, flat_len)
        )
        slot_target = slot_target_row[None, :]
        slot_mask = slot_valid[None, :]
        local_edges = (slot_target == reach_ids) & slot_mask
        chosen = jnp.transpose(select) & slot_mask
        edge_matrix = jnp.concatenate([local_edges, chosen], axis=0).astype(jnp.bfloat16)
        spread_flows = jnp.dot(edge_matrix, routed, preferred_element_type=jnp.float32)
        inflow = inflow + spread_flows[:reach_count]
        outflow = outflow + spread_flows[reach_count:]
        if level_now + 1 < LEVELS:
            arrived = passed_along(routed, "basin", 1)
            prev_select, prev_valid, prev_target = level_select(
                prev_level, prev_down, level_now, slot_count
            )
            incoming = (prev_target[None, :] == reach_ids + reach_count) & prev_valid[None, :]
            inflow = inflow + jnp.dot(
                incoming.astype(jnp.bfloat16), arrived, preferred_element_type=jnp.float32
            )
    flows = outflow.astype(jnp.bfloat16)
    gauge_pick = (gauge_reach[:, None] == jnp.arange(reach_count, dtype=jnp.int32)[None, :]).astype(
        jnp.bfloat16
    )
    gauged = jnp.dot(gauge_pick, flows, preferred_element_type=jnp.float32)
    predicted = jnp.mean(gauged.reshape(-1, members_dev, WINDOWS, series_len // WINDOWS), axis=3)
    scaled = predicted / gauge_sigma[:, None, None]
    innovation = observed[:, None, :] / gauge_sigma[:, None, None] + obs_noise - scaled
    scaled = jnp.transpose(scaled, (0, 2, 1))
    innovation = jnp.transpose(innovation, (0, 2, 1))
    scaled, innovation = (
        lax.all_gather(scaled, "member", axis=2, tiled=True),
        lax.all_gather(innovation, "member", axis=2, tiled=True),
    )
    members = scaled.shape[2]
    scaled = scaled.reshape(-1, members)
    innovation = innovation.reshape(-1, members)
    spread = (scaled - jnp.mean(scaled, axis=1, keepdims=True)) / jnp.sqrt(members - 1.0)
    gram_part = jnp.dot(spread.T, spread, precision=lax.Precision.HIGHEST)
    cross_part = jnp.dot(spread.T, innovation, precision=lax.Precision.HIGHEST)
    gram_part, cross_part = lax.psum((gram_part, cross_part), "basin")
    gram = jnp.eye(members, dtype=jnp.float32) + gram_part
    factor = jnp.linalg.cholesky(gram)
    kalman_gain = jax.scipy.linalg.cho_solve((factor, True), cross_part)
    col_start = lax.axis_index("member") * members_dev
    all_params = lax.all_gather(route_params, "member", axis=2, tiled=True).reshape(-1, members)
    anomaly = all_params - jnp.mean(all_params, axis=1, keepdims=True)
    columns = lax.dynamic_slice_in_dim(kalman_gain, col_start, members_dev, 1)
    increment = jnp.dot(anomaly, columns, precision=lax.Precision.HIGHEST)
    updated = route_params.reshape(-1, members_dev) + increment / jnp.sqrt(members - 1.0)
    return (
        flows.reshape(reach_count, members_dev, series_len),
        updated.reshape(route_params.shape),
    )


def solution(mesh):
    return jax.shard_map(
        per_device,
        mesh=mesh,
        in_specs=(
            P(("groups", "basin"), "member", None),
            P(None, ("groups", "basin"), "member"),
            P(),
            P(("groups", "basin")),
            P(("groups", "basin")),
            P(("groups", "basin")),
            P(("groups", "basin")),
            P(("groups", "basin"), None),
            P(("groups", "basin"), "member", None),
        ),
        out_specs=(P(("groups", "basin"), "member", None), P(None, ("groups", "basin"), "member")),
        check_vma=False,
    )
```

```python
import functools

import jax
import jax.numpy as jnp
from jax import lax
from jax.experimental import pallas as pl
from jax.experimental.pallas import tpu as pltpu
from jax.sharding import PartitionSpec as P

LEVELS = 8
WINDOWS = 64
LANES = 128
EXTRA = 16
HIGHEST = lax.Precision.HIGHEST

def vmem():
    return pl.BlockSpec(memory_space=pltpu.VMEM)


def smem():
    return pl.BlockSpec(memory_space=pltpu.SMEM)


AHEAD = 8


ORDERS = {"basin": (3, 1, 2), "back": (3, 1, 2), "member": (1, 2, 3)}


def partners(length, axis):
    return [0] + list(ORDERS[axis])


def kept(x):
    return pltpu.with_memory_space_constraint(x, pltpu.VMEM)


def table_body(shapes_ref, table_ref):
    shape_count, block_len = shapes_ref.shape
    for s in range(shape_count):
        lags = shapes_ref[s : s + 1, :] * (1.0 / block_len)
        lags = jnp.concatenate([lags, jnp.zeros_like(lags)], axis=1)
        skewed = pltpu.roll(
            jnp.broadcast_to(lags, (block_len, 2 * block_len)), 0, 1, stride=1, stride_axis=0
        ).astype(jnp.bfloat16)
        cols = slice(s * block_len, (s + 1) * block_len)
        table_ref[:block_len, cols] = skewed[:, :block_len]
        table_ref[block_len:, cols] = skewed[:, block_len:]


def kernel_table(unit_shapes):
    shape_count, block_len = unit_shapes.shape
    return pl.pallas_call(
        table_body,
        out_shape=pltpu.VMEM((2 * block_len, shape_count * block_len), jnp.bfloat16),
        in_specs=[vmem()],
        out_specs=vmem(),
        name="table",
    )(unit_shapes)


def split_two(x):
    top = x.astype(jnp.bfloat16)
    rest = x - top.astype(jnp.float32)
    mid = rest.astype(jnp.bfloat16)
    return top, mid, rest - mid.astype(jnp.float32)


def pack_body(
    level_ref,
    down_ref,
    gauge_ref,
    sigma_ref,
    runoff_ref,
    params_ref,
    observed_ref,
    noise_ref,
    *rest,
):
    out_refs, (own_ref, tile_ref, stage_ref, extra_ref) = rest[:-4], rest[-4:]
    reach_count, members_dev, series_len = runoff_ref.shape
    shape_count = params_ref.shape[0]
    gauge_count, windows = observed_ref.shape
    block_len = out_refs[0].shape[1]
    block_count = series_len // block_len
    share = members_dev // len(out_refs)
    rows = share * block_count
    here = lax.axis_index("basin")
    for r in range(reach_count):
        series = runoff_ref[r].astype(jnp.float32)
        for i in range(block_count):
            at = (r * block_count + i) * members_dev
            for h in range(block_len // LANES):
                lane = i * block_len + h * LANES
                stage_ref[h, at : at + members_dev, :] = series[:, lane : lane + LANES]
    extra_ref[...] = jnp.zeros(extra_ref.shape, jnp.float32)
    for g in range(gauge_count):
        extra_ref[:members_dev, g * windows : (g + 1) * windows] = (
            observed_ref[g : g + 1, :] / sigma_ref[g] + noise_ref[g]
        )
    lower = slice(members_dev, members_dev + reach_count)
    for s in range(shape_count):
        extra_ref[lower, s * members_dev : (s + 1) * members_dev] = params_ref[s]
    at_row = lax.broadcasted_iota(jnp.int32, (reach_count, LANES), 0)
    at_lane = lax.broadcasted_iota(jnp.int32, (reach_count, LANES), 1)
    base = shape_count * members_dev
    facts = extra_ref[lower, :]
    cap = reach_count // 4
    facts = jnp.where(at_lane // cap == base // cap, jnp.float32(reach_count), facts)
    for r in range(reach_count):
        rank = jnp.int32(0)
        for q in range(r):
            rank = rank + (level_ref[q] == level_ref[r]).astype(jnp.int32)
        here_slot = (at_row == level_ref[r]) & (at_lane == base + rank)
        facts = jnp.where(here_slot, jnp.float32(r), facts)
        goal_slot = (at_row == level_ref[r]) & (at_lane == base + cap + rank)
        facts = jnp.where(goal_slot, down_ref[r].astype(jnp.float32), facts)
    for g in range(gauge_count):
        facts = jnp.where(
            (at_row == g) & (at_lane == base + 2 * cap), gauge_ref[g].astype(jnp.float32), facts
        )
        facts = jnp.where((at_row == g) & (at_lane == base + 2 * cap + 1), sigma_ref[g], facts)
    upper_top, upper_mid, _ = split_two(extra_ref[:members_dev, :])
    lower_top, lower_mid, lower_low = split_two(facts)
    half = LANES // 2
    lower_top = jnp.where(
        at_lane < half, lower_top.astype(jnp.float32), pltpu.roll(lower_low, half, 1)
    )
    tops = jnp.concatenate([upper_top.astype(jnp.float32), lower_top], axis=0)
    mids = jnp.concatenate(
        [upper_mid.astype(jnp.float32), lower_mid.astype(jnp.float32)], axis=0
    )
    extras = jnp.concatenate([tops, mids], axis=1).astype(jnp.bfloat16)
    for k, out_ref in zip(partners(len(out_refs), "basin"), out_refs):
        to = here ^ k
        for r in range(reach_count):
            for h in range(block_len // LANES):
                pieces = [
                    stage_ref[
                        h,
                        pl.ds(
                            r * block_count * members_dev + share * to + j,
                            block_count,
                            stride=members_dev,
                        ),
                        :,
                    ]
                    for j in range(share)
                ]
                out_ref[r * rows : (r + 1) * rows, h * LANES : (h + 1) * LANES] = jnp.concatenate(
                    pieces, axis=0
                ).astype(jnp.bfloat16)
        out_ref[reach_count * rows :, :] = extras
    own_ref[...] = params_ref[...]
    place_params(params_ref, tile_ref)


def route_body(table_ref, *rest, parts, reach_count, shape_count, gauge_count, members_dev):
    in_refs, rest = rest[:parts], rest[parts:]
    out_refs, rest = rest[:parts], rest[parts:]
    base_ref, state_ref, flows_ref, left_ref, facts_ref, facts_smem, sem = rest
    block_len = table_ref.shape[0] // 2
    rows = state_ref.shape[1]
    share = members_dev // parts
    block_count = rows // share
    total = parts * reach_count
    cap = reach_count // 4
    here = lax.axis_index("basin")
    half = LANES // 2
    base = shape_count * members_dev
    at_lane = lax.broadcasted_iota(jnp.int32, (reach_count, LANES), 1)
    facts_ref[total:, :] = jnp.zeros((facts_ref.shape[0] - total, LANES), jnp.float32)
    for k, in_ref in zip(partners(len(in_refs), "basin"), in_refs):
        source = here ^ k
        extras = in_ref[reach_count * rows :, :].astype(jnp.float32)
        tops, mids = extras[:, :LANES], extras[:, LANES:]
        base_ref[source] = tops[:members_dev] + mids[:members_dev]
        low = pltpu.roll(tops[members_dev:], half, 1)
        facts_ref[pl.ds(pl.multiple_of(source * reach_count, reach_count), reach_count), :] = jnp.where(
            at_lane < half, tops[members_dev:] + (mids[members_dev:] + low), 0.0
        )
    copy = pltpu.make_async_copy(facts_ref, facts_smem, sem)
    copy.start()
    for k, in_ref in zip(partners(len(in_refs), "basin"), in_refs):
        source = here ^ k
        for r in range(reach_count):
            state_ref[source * reach_count + r] = in_ref[r * rows : (r + 1) * rows, :].astype(
                jnp.float32
            )
    state_ref[total] = jnp.zeros(state_ref.shape[1:], jnp.float32)
    state_ref[total + 1] = jnp.zeros(state_ref.shape[1:], jnp.float32)
    copy.wait()

    first_row = lax.broadcasted_iota(jnp.int32, (block_count, block_len), 0) == 0
    slots = parts * cap

    def one_level(level_now, carry):
        picked, goals = [], []
        for c in range(slots):
            at = (c // cap) * reach_count + level_now
            lane = base + c % cap
            reach = facts_smem[at, lane].astype(jnp.int32)
            goal = (c // cap) * reach_count + facts_smem[at, lane + cap].astype(jnp.int32)
            real = reach < reach_count
            kept_goal = (goal < (c // cap + 2) * reach_count) & (goal < total) & real
            picked.append(jnp.where(real, (c // cap) * reach_count + reach, total))
            goals.append(jnp.where(kept_goal, goal, total + 1))
        for c in range(slots):
            rows_now = state_ref[picked[c]]
            left_ref[c * rows : (c + 1) * rows, :block_len] = rows_now.astype(jnp.bfloat16)
            earlier = [
                jnp.where(
                    first_row,
                    0.0,
                    pltpu.roll(rows_now[j * block_count : (j + 1) * block_count], 1, 0),
                )
                for j in range(share)
            ]
            left_ref[c * rows : (c + 1) * rows, block_len:] = jnp.concatenate(
                earlier, axis=0
            ).astype(jnp.bfloat16)
        left = left_ref[...]
        mixed = [
            jnp.dot(
                left,
                table_ref[:, s * block_len : (s + 1) * block_len],
                preferred_element_type=jnp.float32,
            )
            for s in range(shape_count)
        ]
        for c in range(slots):
            pieces = []
            for j in range(share):
                at = slice(c * rows + j * block_count, c * rows + (j + 1) * block_count)
                piece = None
                for s in range(shape_count):
                    weight = facts_smem[picked[c], s * members_dev + share * here + j]
                    term = mixed[s][at] * weight
                    piece = term if piece is None else piece + term
                pieces.append(piece)
            routed = jnp.concatenate(pieces, axis=0).astype(jnp.bfloat16)
            flows_ref[picked[c]] = routed
            state_ref[goals[c]] = state_ref[goals[c]] + routed.astype(jnp.float32)
        return carry

    lax.fori_loop(0, LEVELS, one_level, 0)

    gauges = parts * gauge_count
    span = block_count * block_len // WINDOWS
    wide = gauges * WINDOWS
    per_block = WINDOWS // block_count
    lag_at = lax.broadcasted_iota(jnp.int32, (block_len, wide), 0)
    col_at = lax.broadcasted_iota(jnp.int32, (block_len, wide), 1)
    windowing = jnp.where(lag_at // span == col_at % per_block, 1.0 / span, 0.0).astype(
        jnp.bfloat16
    )
    for g in range(gauges):
        reach = (g // gauge_count) * reach_count + facts_smem[
            (g // gauge_count) * reach_count + g % gauge_count, base + 2 * cap
        ].astype(jnp.int32)
        left_ref[g * rows : (g + 1) * rows, :block_len] = flows_ref[reach]
    means = jnp.dot(
        left_ref[: gauges * rows, :block_len], windowing, preferred_element_type=jnp.float32
    )
    row_at = lax.broadcasted_iota(jnp.int32, (block_count, wide), 0)
    col_at = lax.broadcasted_iota(jnp.int32, (block_count, wide), 1)
    sigma_row = jnp.zeros((1, wide), jnp.float32)
    for g in range(gauges):
        sigma = facts_smem[(g // gauge_count) * reach_count + g % gauge_count, base + 2 * cap + 1]
        sigma_row = jnp.where(col_at[:1] // WINDOWS == g, sigma, sigma_row)
    scaled = []
    for j in range(share):
        merged = jnp.zeros((block_count, wide), jnp.float32)
        for g in range(gauges):
            at = g * rows + j * block_count
            merged = jnp.where(
                (col_at // per_block) == g * block_count + row_at,
                means[at : at + block_count],
                merged,
            )
        scaled.append(jnp.sum(merged, axis=0, keepdims=True) / sigma_row)
    scaled = jnp.concatenate(scaled, axis=0)
    top, mid, low = split_two(scaled)
    chunks = []
    for part in (top.astype(jnp.float32), mid.astype(jnp.float32), low):
        chunks += [part[:, i * block_len : (i + 1) * block_len] for i in range(wide // block_len)]
    used = len(chunks) * share
    chunks.append(jnp.zeros((EXTRA - used, block_len), jnp.float32))
    extras = jnp.concatenate(chunks, axis=0).astype(jnp.bfloat16)
    for k, out_ref in zip(partners(len(out_refs), "back"), out_refs):
        to = here ^ k
        for r in range(reach_count):
            out_ref[r * rows : (r + 1) * rows, :] = flows_ref[to * reach_count + r]
        out_ref[reach_count * rows :, :] = extras


def gather_body(tile_ref, *rest, wide):
    in_refs, out_ref = rest[:-1], rest[-1]
    parts = len(in_refs)
    members_dev = out_ref.shape[0]
    share = members_dev // parts
    block_len = in_refs[0].shape[1]
    here = lax.axis_index("basin")
    pieces = wide // block_len
    at_row = lax.broadcasted_iota(jnp.int32, (members_dev, block_len), 0)
    placed = [jnp.zeros((members_dev, block_len), jnp.float32)] * pieces
    for k, in_ref in zip(partners(len(in_refs), "back"), in_refs):
        extras = in_ref[in_ref.shape[0] - EXTRA :, :].astype(jnp.float32)
        for i in range(pieces):
            for j in range(share):
                value = sum(
                    extras[(p * pieces + i) * share + j : (p * pieces + i) * share + j + 1]
                    for p in range(3)
                )
                placed[i] = jnp.where(at_row == share * (here ^ k) + j, value, placed[i])
    for i in range(pieces):
        out_ref[:, i * block_len : (i + 1) * block_len] = placed[i]
    out_ref[:, wide:] = tile_ref[...]


def place_params(params_ref, tile_ref):
    shape_count, _, members_dev = params_ref.shape
    members = members_dev * lax.axis_size("member")
    tile_ref[...] = jnp.zeros(tile_ref.shape, jnp.float32)
    for s in range(shape_count):
        tile_ref[:, s * members : s * members + members_dev] = params_ref[s]
    tile_ref[...] = pltpu.roll(tile_ref[...], lax.axis_index("member") * members_dev, 1)


def unpack_body(*refs, parts, reach_count):
    in_refs, (out_ref, stage_ref) = refs[:parts], refs[parts:]
    members_dev = out_ref.shape[1]
    block_len = in_refs[0].shape[1]
    share = members_dev // parts
    block_count = out_ref.shape[2] // block_len
    rows = share * block_count
    here = lax.axis_index("basin")
    for k, in_ref in zip(partners(len(in_refs), "back"), in_refs):
        source = here ^ k
        for r in range(reach_count):
            piece = in_ref[r * rows : (r + 1) * rows, :].astype(jnp.float32)
            for j in range(share):
                for h in range(block_len // LANES):
                    stage_ref[
                        h,
                        pl.ds(
                            r * block_count * members_dev + share * source + j,
                            block_count,
                            stride=members_dev,
                        ),
                        :,
                    ] = piece[j * block_count : (j + 1) * block_count, h * LANES : (h + 1) * LANES]
    for r in range(reach_count):
        for i in range(block_count):
            at = (r * block_count + i) * members_dev
            for h in range(block_len // LANES):
                lane = i * block_len + h * LANES
                out_ref[r, :, lane : lane + LANES] = stage_ref[
                    h, at : at + members_dev, :
                ].astype(jnp.bfloat16)


def solve_body(base_ref, params_ref, *rest):
    in_refs, (out_ref, all_ref, right_ref) = rest[:-3], rest[-3:]
    shape_count, reach_count, members_dev = params_ref.shape
    groups = len(in_refs)
    members = groups * members_dev
    wide = all_ref.shape[1]
    here = lax.axis_index("member")
    tiles = None
    for k, in_ref in zip(partners(len(in_refs), "member"), in_refs):
        at = pl.multiple_of((here ^ k) * members_dev, members_dev)
        all_ref[pl.ds(at, members_dev), :] = in_ref[:, :wide]
        tile = in_ref[:, wide:]
        tiles = tile if tiles is None else tiles + tile
    scaled = all_ref[...]
    root = jnp.sqrt(jnp.float32(members - 1))
    spread = (scaled - jnp.mean(scaled, axis=0, keepdims=True)) / root
    own = in_refs[0][:, :wide]
    right_ref[:members, :] = spread
    for n in range(base_ref.shape[0]):
        cols = slice(n * base_ref.shape[2], (n + 1) * base_ref.shape[2])
        right_ref[members : members + members_dev, cols] = base_ref[n] - own[:, cols]
    right_ref[members + members_dev :, :] = jnp.zeros(
        (right_ref.shape[0] - members - members_dev, wide), jnp.float32
    )
    system = lax.dot_general(
        spread,
        right_ref[...],
        (((1,), (1,)), ((), ())),
        precision=HIGHEST,
        preferred_element_type=jnp.float32,
    )
    row_at = lax.broadcasted_iota(jnp.int32, system.shape, 0)
    col_at = lax.broadcasted_iota(jnp.int32, system.shape, 1)
    system = system + jnp.where(row_at == col_at, 1.0, 0.0)
    for first in range(0, members, AHEAD):
        cols = [
            jnp.broadcast_to(system[:, i : i + 1], system.shape)
            for i in range(first, first + AHEAD)
        ]
        for t in range(AHEAD):
            i = first + t
            own_row = row_at == i
            inverse = 1.0 / cols[t][i : i + 1, :]
            pivot_row = system[i : i + 1, :] * inverse
            system = jnp.where(own_row, pivot_row, system - cols[t] * pivot_row)
            for u in range(t + 1, AHEAD):
                pivot_row = cols[u][i : i + 1, :] * inverse
                cols[u] = jnp.where(own_row, pivot_row, cols[u] - cols[t] * pivot_row)
    gain = system[:, members : members + members_dev]
    theta = jnp.concatenate(
        [tiles[:, s * members : (s + 1) * members] for s in range(shape_count)], axis=0
    )
    anomaly = theta - jnp.mean(theta, axis=1, keepdims=True)
    step = (
        jnp.dot(anomaly, gain, precision=HIGHEST, preferred_element_type=jnp.float32) / root
    )
    for s in range(shape_count):
        out_ref[s] = params_ref[s] + step[s * reach_count : (s + 1) * reach_count]


def exchanged(x, axis, by):
    length = lax.axis_size(axis)
    return lax.ppermute(x, axis, [(i, i ^ by) for i in range(length)])


def swapped(pieces, axis, order):
    return [pieces[0]] + [
        exchanged(piece, axis, by) for piece, by in zip(pieces[1:], partners(len(pieces), order)[1:])
    ]


def per_device_split(
    runoff,
    route_params,
    unit_shapes,
    level_map,
    down_map,
    gauge_reach,
    gauge_sigma,
    observed,
    obs_noise,
):
    f32, bf16 = jnp.float32, jnp.bfloat16
    parts, groups = lax.axis_size("basin"), lax.axis_size("member")
    reach_count, members_dev, series_len = runoff.shape
    shape_count, block_len = unit_shapes.shape
    gauge_count = observed.shape[0]
    block_count = series_len // block_len
    share = members_dev // parts
    rows = share * block_count
    total = parts * reach_count
    cap = reach_count // 4
    wide = parts * gauge_count * WINDOWS
    members = members_dev * groups
    sent = pltpu.VMEM((reach_count * rows + EXTRA, block_len), bf16)
    *packed, own_params, tile = pl.pallas_call(
        pack_body,
        out_shape=[sent] * parts
        + [pltpu.VMEM(route_params.shape, f32), pltpu.VMEM((reach_count, LANES), f32)],
        in_specs=[smem()] * 4 + [vmem()] * 4,
        out_specs=[vmem()] * (parts + 2),
        scratch_shapes=[
            pltpu.VMEM((block_len // LANES, reach_count * members_dev * block_count, LANES), f32),
            pltpu.VMEM((members_dev + reach_count, LANES), f32),
        ],
        name="pack",
    )(level_map, down_map, gauge_reach, gauge_sigma, runoff, route_params, observed, obs_noise)
    arrived = swapped(packed, "basin", "basin")
    conv_table = kernel_table(unit_shapes)
    *routed, noise_base = pl.pallas_call(
        functools.partial(
            route_body,
            parts=parts,
            reach_count=reach_count,
            shape_count=shape_count,
            gauge_count=gauge_count,
            members_dev=members_dev,
        ),
        out_shape=[sent] * parts
        + [pltpu.VMEM((parts, members_dev, gauge_count * WINDOWS), f32)],
        in_specs=[vmem()] * (1 + parts),
        out_specs=[vmem()] * (parts + 1),
        scratch_shapes=[
            pltpu.VMEM((total + 2, rows, block_len), f32),
            pltpu.VMEM((total + 1, rows, block_len), bf16),
            pltpu.VMEM((parts * max(cap, gauge_count) * rows, 2 * block_len), bf16),
            pltpu.VMEM((total + 8, LANES), f32),
            pltpu.SMEM((total + 8, LANES), f32),
            pltpu.SemaphoreType.DMA,
        ],
        name="route",
    )(kept(conv_table), *map(kept, arrived))
    returned = swapped(routed, "basin", "back")
    local = pl.pallas_call(
        functools.partial(gather_body, wide=wide),
        out_shape=pltpu.VMEM((members_dev, wide + LANES), f32),
        in_specs=[vmem()] * (1 + parts),
        out_specs=vmem(),
        name="gather",
    )(kept(tile), *map(kept, returned))
    everyone = swapped([local] * groups, "member", "member")
    flows = pl.pallas_call(
        functools.partial(unpack_body, parts=parts, reach_count=reach_count),
        out_shape=jax.ShapeDtypeStruct(runoff.shape, bf16),
        in_specs=[vmem()] * parts,
        out_specs=vmem(),
        scratch_shapes=[pltpu.VMEM((block_len // LANES, reach_count * members_dev * block_count, LANES), f32)],
        name="unpack",
    )(*map(kept, returned))
    updated = pl.pallas_call(
        solve_body,
        out_shape=jax.ShapeDtypeStruct(route_params.shape, f32),
        in_specs=[vmem()] * (2 + groups),
        out_specs=vmem(),
        scratch_shapes=[pltpu.VMEM((members, wide), f32), pltpu.VMEM((LANES, wide), f32)],
        name="solve",
    )(kept(noise_base), kept(own_params), *map(kept, everyone))
    return flows, updated


def power_of_two(x):
    return x & (x - 1) == 0


def per_device(*args):
    runoff, route_params, unit_shapes, _, _, _, _, observed, _ = args
    parts, groups = lax.axis_size("basin"), lax.axis_size("member")
    reach_count, members_dev, series_len = runoff.shape
    shape_count, block_len = unit_shapes.shape
    block_count = series_len // block_len
    gauge_count = observed.shape[0]
    wide = parts * gauge_count * WINDOWS
    share = max(members_dev // parts, 1)
    fits = (
        power_of_two(parts)
        and power_of_two(groups)
        and members_dev == share * parts
        and reach_count == 8
        and members_dev == 8
        and block_count == 8
        and series_len % block_len == 0
        and block_len == 2 * LANES
        and gauge_count * WINDOWS == LANES
        and wide % block_len == 0
        and 3 * share * (wide // block_len) <= EXTRA
        and (shape_count * members_dev + 8) * 2 <= LANES
        and reach_count == LEVELS
        and shape_count * groups * members_dev <= LANES
        and groups * members_dev + members_dev <= LANES
    )
    if fits:
        return per_device_split(*args)
    return per_device_chain(*args)


def passed_along(x, axis, by):
    length = lax.axis_size(axis)
    pairs = [(i, i + by) for i in range(length) if 0 <= i + by < length]
    return lax.ppermute(x, axis, pairs)


def route_rows(inflow_rows, slot_weights, conv_table):
    block_len = conv_table.shape[0] // 2
    row_count, series_len = inflow_rows.shape
    blocks = inflow_rows.reshape(row_count, series_len // block_len, block_len)
    earlier = jnp.concatenate([jnp.zeros_like(blocks[:, :1]), blocks[:, :-1]], axis=1)
    joined = jnp.concatenate([blocks, earlier], axis=2).reshape(-1, 2 * block_len)
    mixed_blocks = jnp.dot(joined, conv_table, preferred_element_type=jnp.float32)
    mixed_blocks = mixed_blocks.reshape(
        row_count, series_len // block_len, slot_weights.shape[1], block_len
    )
    return jnp.sum(mixed_blocks * slot_weights[:, None, :, None], axis=2).reshape(
        row_count, series_len
    )


def level_select(level_block, down_block, level_now, slot_count):
    entry_count = level_block.shape[0]
    entry_ids = jnp.arange(entry_count, dtype=jnp.int32)
    in_level = level_block == level_now
    before = (entry_ids[None, :] < entry_ids[:, None]) & in_level[None, :]
    rank = jnp.sum(before.astype(jnp.int32), axis=1)
    slot_ids = jnp.arange(slot_count, dtype=jnp.int32)
    select = (rank[None, :] == slot_ids[:, None]) & in_level[None, :]
    slot_valid = slot_ids < jnp.sum(in_level.astype(jnp.int32))
    slot_target = jnp.sum(jnp.where(select, down_block[None, :], 0), axis=1)
    return (select, slot_valid, slot_target)


def per_device_chain(
    runoff,
    route_params,
    unit_shapes,
    level_map,
    down_map,
    gauge_reach,
    gauge_sigma,
    observed,
    obs_noise,
):
    conv_table = kernel_table(unit_shapes)
    reach_count, members_dev, series_len = runoff.shape
    flat_len = members_dev * series_len
    slot_count = reach_count // 4
    shape_count = route_params.shape[0]
    inflow = runoff.astype(jnp.float32).reshape(reach_count, flat_len)
    outflow = jnp.zeros_like(inflow)
    reach_ids = jnp.arange(reach_count, dtype=jnp.int32)[:, None]
    params_rows = jnp.transpose(route_params, (1, 2, 0))
    prev_level, prev_down = passed_along((level_map, down_map), "basin", 1)
    for level_now in range(LEVELS):
        select, slot_valid, slot_target_row = level_select(
            level_map, down_map, level_now, slot_count
        )
        gathered = jnp.dot(
            select.astype(jnp.bfloat16),
            inflow.astype(jnp.bfloat16),
            preferred_element_type=jnp.float32,
        )
        gathered = gathered.astype(jnp.bfloat16).reshape(slot_count * members_dev, series_len)
        slot_weights = jnp.einsum(
            "cr,rms->cms", select.astype(jnp.float32), params_rows, precision=lax.Precision.HIGHEST
        ).reshape(-1, shape_count)
        routed = (
            route_rows(gathered, slot_weights, conv_table)
            .astype(jnp.bfloat16)
            .reshape(slot_count, flat_len)
        )
        slot_target = slot_target_row[None, :]
        slot_mask = slot_valid[None, :]
        local_edges = (slot_target == reach_ids) & slot_mask
        chosen = jnp.transpose(select) & slot_mask
        edge_matrix = jnp.concatenate([local_edges, chosen], axis=0).astype(jnp.bfloat16)
        spread_flows = jnp.dot(edge_matrix, routed, preferred_element_type=jnp.float32)
        inflow = inflow + spread_flows[:reach_count]
        outflow = outflow + spread_flows[reach_count:]
        if level_now + 1 < LEVELS:
            arrived = passed_along(routed, "basin", 1)
            prev_select, prev_valid, prev_target = level_select(
                prev_level, prev_down, level_now, slot_count
            )
            incoming = (prev_target[None, :] == reach_ids + reach_count) & prev_valid[None, :]
            inflow = inflow + jnp.dot(
                incoming.astype(jnp.bfloat16), arrived, preferred_element_type=jnp.float32
            )
    flows = outflow.astype(jnp.bfloat16)
    gauge_pick = (gauge_reach[:, None] == jnp.arange(reach_count, dtype=jnp.int32)[None, :]).astype(
        jnp.bfloat16
    )
    gauged = jnp.dot(gauge_pick, flows, preferred_element_type=jnp.float32)
    predicted = jnp.mean(gauged.reshape(-1, members_dev, WINDOWS, series_len // WINDOWS), axis=3)
    scaled = predicted / gauge_sigma[:, None, None]
    innovation = observed[:, None, :] / gauge_sigma[:, None, None] + obs_noise - scaled
    scaled = jnp.transpose(scaled, (0, 2, 1))
    innovation = jnp.transpose(innovation, (0, 2, 1))
    scaled, innovation = (
        lax.all_gather(scaled, "member", axis=2, tiled=True),
        lax.all_gather(innovation, "member", axis=2, tiled=True),
    )
    members = scaled.shape[2]
    scaled = scaled.reshape(-1, members)
    innovation = innovation.reshape(-1, members)
    spread = (scaled - jnp.mean(scaled, axis=1, keepdims=True)) / jnp.sqrt(members - 1.0)
    gram_part = jnp.dot(spread.T, spread, precision=lax.Precision.HIGHEST)
    cross_part = jnp.dot(spread.T, innovation, precision=lax.Precision.HIGHEST)
    gram_part, cross_part = lax.psum((gram_part, cross_part), "basin")
    gram = jnp.eye(members, dtype=jnp.float32) + gram_part
    factor = jnp.linalg.cholesky(gram)
    kalman_gain = jax.scipy.linalg.cho_solve((factor, True), cross_part)
    col_start = lax.axis_index("member") * members_dev
    all_params = lax.all_gather(route_params, "member", axis=2, tiled=True).reshape(-1, members)
    anomaly = all_params - jnp.mean(all_params, axis=1, keepdims=True)
    columns = lax.dynamic_slice_in_dim(kalman_gain, col_start, members_dev, 1)
    increment = jnp.dot(anomaly, columns, precision=lax.Precision.HIGHEST)
    updated = route_params.reshape(-1, members_dev) + increment / jnp.sqrt(members - 1.0)
    return (
        flows.reshape(reach_count, members_dev, series_len),
        updated.reshape(route_params.shape),
    )


def solution(mesh):
    return jax.shard_map(
        per_device,
        mesh=mesh,
        in_specs=(
            P(("groups", "basin"), "member", None),
            P(None, ("groups", "basin"), "member"),
            P(),
            P(("groups", "basin")),
            P(("groups", "basin")),
            P(("groups", "basin")),
            P(("groups", "basin")),
            P(("groups", "basin"), None),
            P(("groups", "basin"), "member", None),
        ),
        out_specs=(P(("groups", "basin"), "member", None), P(None, ("groups", "basin"), "member")),
        check_vma=False,
    )
```

```python
import functools

import jax
import jax.numpy as jnp
from jax import lax
from jax.experimental import pallas as pl
from jax.experimental.pallas import tpu as pltpu
from jax.sharding import PartitionSpec as P

LEVELS = 8
WINDOWS = 64
LANES = 128
EXTRA = 16
HIGHEST = lax.Precision.HIGHEST

def vmem():
    return pl.BlockSpec(memory_space=pltpu.VMEM)


def smem():
    return pl.BlockSpec(memory_space=pltpu.SMEM)


AHEAD = 16
CODE = 64


ORDERS = {"basin": (3, 1, 2), "back": (3, 1, 2), "member": (1, 2, 3)}


def partners(length, axis):
    return [0] + list(ORDERS[axis])


def kept(x):
    return pltpu.with_memory_space_constraint(x, pltpu.VMEM)


def table_body(shapes_ref, table_ref, window_ref, *, span):
    shape_count, block_len = shapes_ref.shape
    for s in range(shape_count):
        lags = shapes_ref[s : s + 1, :] * (1.0 / block_len)
        lags = jnp.concatenate([lags, jnp.zeros_like(lags)], axis=1)
        skewed = pltpu.roll(
            jnp.broadcast_to(lags, (block_len, 2 * block_len)), 0, 1, stride=1, stride_axis=0
        ).astype(jnp.bfloat16)
        cols = slice(s * block_len, (s + 1) * block_len)
        table_ref[:block_len, cols] = skewed[:, :block_len]
        table_ref[block_len:, cols] = skewed[:, block_len:]
    lag_at = lax.broadcasted_iota(jnp.int32, window_ref.shape, 0)
    col_at = lax.broadcasted_iota(jnp.int32, window_ref.shape, 1)
    window_ref[...] = jnp.where(
        lag_at // span == col_at % (block_len // span), 1.0 / span, 0.0
    ).astype(jnp.bfloat16)


def kernel_table(unit_shapes, span, wide):
    shape_count, block_len = unit_shapes.shape
    return pl.pallas_call(
        functools.partial(table_body, span=span),
        out_shape=[
            pltpu.VMEM((2 * block_len, shape_count * block_len), jnp.bfloat16),
            pltpu.VMEM((block_len, wide), jnp.bfloat16),
        ],
        in_specs=[vmem()],
        out_specs=[vmem()] * 2,
        name="table",
    )(unit_shapes)


def split_two(x):
    top = x.astype(jnp.bfloat16)
    rest = x - top.astype(jnp.float32)
    mid = rest.astype(jnp.bfloat16)
    return top, mid, rest - mid.astype(jnp.float32)


def pack_body(
    level_ref,
    down_ref,
    gauge_ref,
    sigma_ref,
    runoff_ref,
    params_ref,
    observed_ref,
    noise_ref,
    *rest,
):
    out_refs, (own_ref, tile_ref, stage_ref, extra_ref) = rest[:-4], rest[-4:]
    reach_count, members_dev, series_len = runoff_ref.shape
    shape_count = params_ref.shape[0]
    gauge_count, windows = observed_ref.shape
    block_len = out_refs[0].shape[1]
    block_count = series_len // block_len
    share = members_dev // len(out_refs)
    rows = share * block_count
    here = lax.axis_index("basin")
    for r in range(reach_count):
        series = runoff_ref[r].astype(jnp.float32)
        for i in range(block_count):
            at = (r * block_count + i) * members_dev
            for h in range(block_len // LANES):
                lane = i * block_len + h * LANES
                stage_ref[h, at : at + members_dev, :] = series[:, lane : lane + LANES]
    extra_ref[...] = jnp.zeros(extra_ref.shape, jnp.float32)
    for g in range(gauge_count):
        extra_ref[:members_dev, g * windows : (g + 1) * windows] = (
            observed_ref[g : g + 1, :] / sigma_ref[g] + noise_ref[g]
        )
    lower = slice(members_dev, members_dev + reach_count)
    for s in range(shape_count):
        extra_ref[lower, s * members_dev : (s + 1) * members_dev] = params_ref[s]
    at_row = lax.broadcasted_iota(jnp.int32, (reach_count, LANES), 0)
    at_lane = lax.broadcasted_iota(jnp.int32, (reach_count, LANES), 1)
    base = shape_count * members_dev
    facts = extra_ref[lower, :]
    cap = reach_count // 4
    facts = jnp.where(
        (at_lane >= base) & (at_lane < base + cap), jnp.float32(reach_count * CODE), facts
    )
    for r in range(reach_count):
        rank = jnp.int32(0)
        for q in range(r):
            rank = rank + (level_ref[q] == level_ref[r]).astype(jnp.int32)
        here_slot = (at_row == level_ref[r]) & (at_lane == base + rank)
        facts = jnp.where(here_slot, (down_ref[r] + r * CODE).astype(jnp.float32), facts)
    for g in range(gauge_count):
        facts = jnp.where(
            (at_row == g) & (at_lane == base + cap), gauge_ref[g].astype(jnp.float32), facts
        )
        facts = jnp.where((at_row == g) & (at_lane == base + cap + 1), sigma_ref[g], facts)
    upper_top, upper_mid, _ = split_two(extra_ref[:members_dev, :])
    lower_top, lower_mid, lower_low = split_two(facts)
    half = LANES // 2
    lower_top = jnp.where(
        at_lane < half, lower_top.astype(jnp.float32), pltpu.roll(lower_low, half, 1)
    )
    tops = jnp.concatenate([upper_top.astype(jnp.float32), lower_top], axis=0)
    mids = jnp.concatenate(
        [upper_mid.astype(jnp.float32), lower_mid.astype(jnp.float32)], axis=0
    )
    extras = jnp.concatenate([tops, mids], axis=1).astype(jnp.bfloat16)
    for k, out_ref in zip(partners(len(out_refs), "basin"), out_refs):
        to = here ^ k
        for r in range(reach_count):
            for h in range(block_len // LANES):
                pieces = [
                    stage_ref[
                        h,
                        pl.ds(
                            r * block_count * members_dev + share * to + j,
                            block_count,
                            stride=members_dev,
                        ),
                        :,
                    ]
                    for j in range(share)
                ]
                out_ref[r * rows : (r + 1) * rows, h * LANES : (h + 1) * LANES] = jnp.concatenate(
                    pieces, axis=0
                ).astype(jnp.bfloat16)
        out_ref[reach_count * rows :, :] = extras
    own_ref[...] = params_ref[...]
    place_params(params_ref, tile_ref)


def route_body(table_ref, window_ref, *rest, parts, reach_count, shape_count, gauge_count, members_dev):
    in_refs, rest = rest[:parts], rest[parts:]
    out_refs, rest = rest[:parts], rest[parts:]
    base_ref, state_ref, flows_ref, left_ref, weight_ref, code_ref = rest
    block_len = table_ref.shape[0] // 2
    rows = state_ref.shape[1]
    share = members_dev // parts
    block_count = rows // share
    total = parts * reach_count
    cap = reach_count // 4
    here = lax.axis_index("basin")
    half = LANES // 2
    base = shape_count * members_dev
    span = LANES // parts
    at_lane = lax.broadcasted_iota(jnp.int32, (reach_count, LANES), 1)
    facts = jnp.zeros((reach_count, LANES), jnp.float32)
    for k, in_ref in zip(partners(len(in_refs), "basin"), in_refs):
        source = here ^ k
        extras = in_ref[reach_count * rows :, :].astype(jnp.float32)
        tops, mids = extras[:, :LANES], extras[:, LANES:]
        base_ref[source] = tops[:members_dev] + mids[:members_dev]
        low = pltpu.roll(tops[members_dev:], half, 1)
        part = jnp.where(at_lane < span, tops[members_dev:] + (mids[members_dev:] + low), 0.0)
        facts = facts + pltpu.roll(part, source * span, 1)
    whole = facts.astype(jnp.int32)
    for level_now in range(LEVELS):
        for c in range(parts * cap):
            code_ref[level_now * parts * cap + c] = whole[
                level_now, (c // cap) * span + base + c % cap
            ]
    mine = pltpu.roll(facts, LANES - share * here, 1)
    for n in range(parts):
        for s in range(shape_count):
            for j in range(share):
                lane = n * span + s * members_dev + j
                weight_ref[s * share + j, n * reach_count : (n + 1) * reach_count, :] = (
                    jnp.broadcast_to(mine[:, lane : lane + 1], (reach_count, LANES))
                )
    for k, in_ref in zip(partners(len(in_refs), "basin"), in_refs):
        source = here ^ k
        for r in range(reach_count):
            state_ref[source * reach_count + r] = in_ref[r * rows : (r + 1) * rows, :].astype(
                jnp.float32
            )
    state_ref[total] = jnp.zeros(state_ref.shape[1:], jnp.float32)
    state_ref[total + 1] = jnp.zeros(state_ref.shape[1:], jnp.float32)

    first_row = lax.broadcasted_iota(jnp.int32, (block_count, block_len), 0) == 0
    slots = parts * cap

    def one_level(level_now, carry):
        picked, goals, sources = [], [], []
        for c in range(slots):
            code = code_ref[level_now * slots + c]
            reach = code // CODE
            goal = (c // cap) * reach_count + code % CODE
            real = reach < reach_count
            kept_goal = (goal < (c // cap + 2) * reach_count) & (goal < total) & real
            sources.append((c // cap) * reach_count + jnp.where(real, reach, 0))
            picked.append(jnp.where(real, (c // cap) * reach_count + reach, total))
            goals.append(jnp.where(kept_goal, goal, total + 1))
        for c in range(slots):
            rows_now = state_ref[picked[c]]
            left_ref[c * rows : (c + 1) * rows, :block_len] = rows_now.astype(jnp.bfloat16)
            earlier = [
                jnp.where(
                    first_row,
                    0.0,
                    pltpu.roll(rows_now[j * block_count : (j + 1) * block_count], 1, 0),
                )
                for j in range(share)
            ]
            left_ref[c * rows : (c + 1) * rows, block_len:] = jnp.concatenate(
                earlier, axis=0
            ).astype(jnp.bfloat16)
        left = left_ref[...]
        mixed = [
            jnp.dot(
                left,
                table_ref[:, s * block_len : (s + 1) * block_len],
                preferred_element_type=jnp.float32,
            )
            for s in range(shape_count)
        ]
        for c in range(slots):
            pieces = []
            for j in range(share):
                at = slice(c * rows + j * block_count, c * rows + (j + 1) * block_count)
                piece = None
                for s in range(shape_count):
                    weight = weight_ref[s * share + j, pl.ds(sources[c], 1), :]
                    weight = jnp.concatenate([weight] * (block_len // LANES), axis=1)
                    term = mixed[s][at] * weight
                    piece = term if piece is None else piece + term
                pieces.append(piece)
            routed = jnp.concatenate(pieces, axis=0).astype(jnp.bfloat16)
            flows_ref[picked[c]] = routed
            state_ref[goals[c]] = state_ref[goals[c]] + routed.astype(jnp.float32)
        return carry

    lax.fori_loop(0, LEVELS, one_level, 0)

    gauges = parts * gauge_count
    wide = gauges * WINDOWS
    per_block = WINDOWS // block_count
    for g in range(gauges):
        reach = (g // gauge_count) * reach_count + whole[
            g % gauge_count, (g // gauge_count) * span + base + cap
        ]
        left_ref[g * rows : (g + 1) * rows, :block_len] = flows_ref[reach]
    means = jnp.dot(
        left_ref[: gauges * rows, :block_len], window_ref[...], preferred_element_type=jnp.float32
    )
    row_at = lax.broadcasted_iota(jnp.int32, (block_count, wide), 0)
    col_at = lax.broadcasted_iota(jnp.int32, (block_count, wide), 1)
    sigma_row = jnp.zeros((1, wide), jnp.float32)
    for g in range(gauges):
        sigma = facts[g % gauge_count, (g // gauge_count) * span + base + cap + 1]
        sigma_row = jnp.where(col_at[:1] // WINDOWS == g, sigma, sigma_row)
    scaled = []
    for j in range(share):
        merged = jnp.zeros((block_count, wide), jnp.float32)
        for g in range(gauges):
            at = g * rows + j * block_count
            merged = jnp.where(
                (col_at // per_block) == g * block_count + row_at,
                means[at : at + block_count],
                merged,
            )
        scaled.append(jnp.sum(merged, axis=0, keepdims=True) / sigma_row)
    scaled = jnp.concatenate(scaled, axis=0)
    top, mid, low = split_two(scaled)
    chunks = []
    for part in (top.astype(jnp.float32), mid.astype(jnp.float32), low):
        chunks += [part[:, i * block_len : (i + 1) * block_len] for i in range(wide // block_len)]
    used = len(chunks) * share
    chunks.append(jnp.zeros((EXTRA - used, block_len), jnp.float32))
    extras = jnp.concatenate(chunks, axis=0).astype(jnp.bfloat16)
    for k, out_ref in zip(partners(len(out_refs), "back"), out_refs):
        to = here ^ k
        for r in range(reach_count):
            out_ref[r * rows : (r + 1) * rows, :] = flows_ref[to * reach_count + r]
        out_ref[reach_count * rows :, :] = extras


def gather_body(tile_ref, *rest, wide):
    in_refs, out_ref = rest[:-1], rest[-1]
    parts = len(in_refs)
    members_dev = out_ref.shape[0]
    share = members_dev // parts
    block_len = in_refs[0].shape[1]
    here = lax.axis_index("basin")
    pieces = wide // block_len
    at_row = lax.broadcasted_iota(jnp.int32, (members_dev, block_len), 0)
    placed = [jnp.zeros((members_dev, block_len), jnp.float32)] * pieces
    for k, in_ref in zip(partners(len(in_refs), "back"), in_refs):
        extras = in_ref[in_ref.shape[0] - EXTRA :, :].astype(jnp.float32)
        for i in range(pieces):
            for j in range(share):
                value = sum(
                    extras[(p * pieces + i) * share + j : (p * pieces + i) * share + j + 1]
                    for p in range(3)
                )
                placed[i] = jnp.where(at_row == share * (here ^ k) + j, value, placed[i])
    for i in range(pieces):
        out_ref[:, i * block_len : (i + 1) * block_len] = placed[i]
    out_ref[:, wide:] = tile_ref[...]


def place_params(params_ref, tile_ref):
    shape_count, _, members_dev = params_ref.shape
    members = members_dev * lax.axis_size("member")
    tile_ref[...] = jnp.zeros(tile_ref.shape, jnp.float32)
    for s in range(shape_count):
        tile_ref[:, s * members : s * members + members_dev] = params_ref[s]
    tile_ref[...] = pltpu.roll(tile_ref[...], lax.axis_index("member") * members_dev, 1)


def unpack_body(*refs, parts, reach_count):
    in_refs, (out_ref, stage_ref) = refs[:parts], refs[parts:]
    members_dev = out_ref.shape[1]
    block_len = in_refs[0].shape[1]
    share = members_dev // parts
    block_count = out_ref.shape[2] // block_len
    rows = share * block_count
    here = lax.axis_index("basin")
    for k, in_ref in zip(partners(len(in_refs), "back"), in_refs):
        source = here ^ k
        for r in range(reach_count):
            piece = in_ref[r * rows : (r + 1) * rows, :].astype(jnp.float32)
            for j in range(share):
                for h in range(block_len // LANES):
                    stage_ref[
                        h,
                        pl.ds(
                            r * block_count * members_dev + share * source + j,
                            block_count,
                            stride=members_dev,
                        ),
                        :,
                    ] = piece[j * block_count : (j + 1) * block_count, h * LANES : (h + 1) * LANES]
    for r in range(reach_count):
        for i in range(block_count):
            at = (r * block_count + i) * members_dev
            for h in range(block_len // LANES):
                lane = i * block_len + h * LANES
                out_ref[r, :, lane : lane + LANES] = stage_ref[
                    h, at : at + members_dev, :
                ].astype(jnp.bfloat16)


def solve_body(base_ref, params_ref, *rest):
    in_refs, (out_ref, all_ref, right_ref) = rest[:-3], rest[-3:]
    shape_count, reach_count, members_dev = params_ref.shape
    groups = len(in_refs)
    members = groups * members_dev
    wide = all_ref.shape[1]
    here = lax.axis_index("member")
    tiles = None
    for k, in_ref in zip(partners(len(in_refs), "member"), in_refs):
        at = pl.multiple_of((here ^ k) * members_dev, members_dev)
        all_ref[pl.ds(at, members_dev), :] = in_ref[:, :wide]
        tile = in_ref[:, wide:]
        tiles = tile if tiles is None else tiles + tile
    scaled = all_ref[...]
    root = jnp.sqrt(jnp.float32(members - 1))
    spread = (scaled - jnp.mean(scaled, axis=0, keepdims=True)) / root
    own = in_refs[0][:, :wide]
    right_ref[:members, :] = spread
    for n in range(base_ref.shape[0]):
        cols = slice(n * base_ref.shape[2], (n + 1) * base_ref.shape[2])
        right_ref[members : members + members_dev, cols] = base_ref[n] - own[:, cols]
    right_ref[members + members_dev :, :] = jnp.zeros(
        (right_ref.shape[0] - members - members_dev, wide), jnp.float32
    )
    system = lax.dot_general(
        spread,
        right_ref[...],
        (((1,), (1,)), ((), ())),
        precision=HIGHEST,
        preferred_element_type=jnp.float32,
    )
    row_at = lax.broadcasted_iota(jnp.int32, system.shape, 0)
    col_at = lax.broadcasted_iota(jnp.int32, system.shape, 1)
    system = system + jnp.where(row_at == col_at, 1.0, 0.0)
    for first in range(0, members, AHEAD):
        cols = [
            jnp.broadcast_to(system[:, i : i + 1], system.shape)
            for i in range(first, first + AHEAD)
        ]
        for t in range(AHEAD):
            i = first + t
            own_row = row_at == i
            inverse = 1.0 / cols[t][i : i + 1, :]
            pivot_row = system[i : i + 1, :] * inverse
            system = jnp.where(own_row, pivot_row, system - cols[t] * pivot_row)
            for u in range(t + 1, AHEAD):
                pivot_row = cols[u][i : i + 1, :] * inverse
                cols[u] = jnp.where(own_row, pivot_row, cols[u] - cols[t] * pivot_row)
    gain = system[:, members : members + members_dev]
    theta = jnp.concatenate(
        [tiles[:, s * members : (s + 1) * members] for s in range(shape_count)], axis=0
    )
    anomaly = theta - jnp.mean(theta, axis=1, keepdims=True)
    step = (
        jnp.dot(anomaly, gain, precision=HIGHEST, preferred_element_type=jnp.float32) / root
    )
    for s in range(shape_count):
        out_ref[s] = params_ref[s] + step[s * reach_count : (s + 1) * reach_count]


def exchanged(x, axis, by):
    length = lax.axis_size(axis)
    return lax.ppermute(x, axis, [(i, i ^ by) for i in range(length)])


def swapped(pieces, axis, order):
    return [pieces[0]] + [
        exchanged(piece, axis, by) for piece, by in zip(pieces[1:], partners(len(pieces), order)[1:])
    ]


def per_device_split(
    runoff,
    route_params,
    unit_shapes,
    level_map,
    down_map,
    gauge_reach,
    gauge_sigma,
    observed,
    obs_noise,
):
    f32, bf16 = jnp.float32, jnp.bfloat16
    parts, groups = lax.axis_size("basin"), lax.axis_size("member")
    reach_count, members_dev, series_len = runoff.shape
    shape_count, block_len = unit_shapes.shape
    gauge_count = observed.shape[0]
    block_count = series_len // block_len
    share = members_dev // parts
    rows = share * block_count
    total = parts * reach_count
    cap = reach_count // 4
    wide = parts * gauge_count * WINDOWS
    members = members_dev * groups
    sent = pltpu.VMEM((reach_count * rows + EXTRA, block_len), bf16)
    *packed, own_params, tile = pl.pallas_call(
        pack_body,
        out_shape=[sent] * parts
        + [pltpu.VMEM(route_params.shape, f32), pltpu.VMEM((reach_count, LANES), f32)],
        in_specs=[smem()] * 4 + [vmem()] * 4,
        out_specs=[vmem()] * (parts + 2),
        scratch_shapes=[
            pltpu.VMEM((block_len // LANES, reach_count * members_dev * block_count, LANES), f32),
            pltpu.VMEM((members_dev + reach_count, LANES), f32),
        ],
        name="pack",
    )(level_map, down_map, gauge_reach, gauge_sigma, runoff, route_params, observed, obs_noise)
    arrived = swapped(packed, "basin", "basin")
    conv_table, window_table = kernel_table(unit_shapes, series_len // WINDOWS, wide)
    *routed, noise_base = pl.pallas_call(
        functools.partial(
            route_body,
            parts=parts,
            reach_count=reach_count,
            shape_count=shape_count,
            gauge_count=gauge_count,
            members_dev=members_dev,
        ),
        out_shape=[sent] * parts
        + [pltpu.VMEM((parts, members_dev, gauge_count * WINDOWS), f32)],
        in_specs=[vmem()] * (2 + parts),
        out_specs=[vmem()] * (parts + 1),
        scratch_shapes=[
            pltpu.VMEM((total + 2, rows, block_len), f32),
            pltpu.VMEM((total + 1, rows, block_len), bf16),
            pltpu.VMEM((parts * max(cap, gauge_count) * rows, 2 * block_len), bf16),
            pltpu.VMEM((shape_count * share, total, LANES), f32),
            pltpu.SMEM((LEVELS * parts * cap,), jnp.int32),
        ],
        name="route",
    )(kept(conv_table), kept(window_table), *map(kept, arrived))
    returned = swapped(routed, "basin", "back")
    local = pl.pallas_call(
        functools.partial(gather_body, wide=wide),
        out_shape=pltpu.VMEM((members_dev, wide + LANES), f32),
        in_specs=[vmem()] * (1 + parts),
        out_specs=vmem(),
        name="gather",
    )(kept(tile), *map(kept, returned))
    everyone = swapped([local] * groups, "member", "member")
    flows = pl.pallas_call(
        functools.partial(unpack_body, parts=parts, reach_count=reach_count),
        out_shape=jax.ShapeDtypeStruct(runoff.shape, bf16),
        in_specs=[vmem()] * parts,
        out_specs=vmem(),
        scratch_shapes=[pltpu.VMEM((block_len // LANES, reach_count * members_dev * block_count, LANES), f32)],
        name="unpack",
    )(*map(kept, returned))
    updated = pl.pallas_call(
        solve_body,
        out_shape=jax.ShapeDtypeStruct(route_params.shape, f32),
        in_specs=[vmem()] * (2 + groups),
        out_specs=vmem(),
        scratch_shapes=[pltpu.VMEM((members, wide), f32), pltpu.VMEM((LANES, wide), f32)],
        name="solve",
    )(kept(noise_base), kept(own_params), *map(kept, everyone))
    return flows, updated


def power_of_two(x):
    return x & (x - 1) == 0


def per_device(*args):
    runoff, route_params, unit_shapes, _, _, _, _, observed, _ = args
    parts, groups = lax.axis_size("basin"), lax.axis_size("member")
    reach_count, members_dev, series_len = runoff.shape
    shape_count, block_len = unit_shapes.shape
    block_count = series_len // block_len
    gauge_count = observed.shape[0]
    wide = parts * gauge_count * WINDOWS
    share = max(members_dev // parts, 1)
    fits = (
        power_of_two(parts)
        and power_of_two(groups)
        and members_dev == share * parts
        and reach_count == 8
        and members_dev == 8
        and block_count == 8
        and series_len % block_len == 0
        and block_len == 2 * LANES
        and gauge_count * WINDOWS == LANES
        and wide % block_len == 0
        and 3 * share * (wide // block_len) <= EXTRA
        and shape_count * members_dev + reach_count // 4 + 2 <= LANES // parts
        and 2 * reach_count < CODE
        and parts >= 2
        and reach_count == LEVELS
        and shape_count * groups * members_dev <= LANES
        and groups * members_dev + members_dev <= LANES
    )
    if fits:
        return per_device_split(*args)
    return per_device_chain(*args)


def passed_along(x, axis, by):
    length = lax.axis_size(axis)
    pairs = [(i, i + by) for i in range(length) if 0 <= i + by < length]
    return lax.ppermute(x, axis, pairs)


def route_rows(inflow_rows, slot_weights, conv_table):
    block_len = conv_table.shape[0] // 2
    row_count, series_len = inflow_rows.shape
    blocks = inflow_rows.reshape(row_count, series_len // block_len, block_len)
    earlier = jnp.concatenate([jnp.zeros_like(blocks[:, :1]), blocks[:, :-1]], axis=1)
    joined = jnp.concatenate([blocks, earlier], axis=2).reshape(-1, 2 * block_len)
    mixed_blocks = jnp.dot(joined, conv_table, preferred_element_type=jnp.float32)
    mixed_blocks = mixed_blocks.reshape(
        row_count, series_len // block_len, slot_weights.shape[1], block_len
    )
    return jnp.sum(mixed_blocks * slot_weights[:, None, :, None], axis=2).reshape(
        row_count, series_len
    )


def level_select(level_block, down_block, level_now, slot_count):
    entry_count = level_block.shape[0]
    entry_ids = jnp.arange(entry_count, dtype=jnp.int32)
    in_level = level_block == level_now
    before = (entry_ids[None, :] < entry_ids[:, None]) & in_level[None, :]
    rank = jnp.sum(before.astype(jnp.int32), axis=1)
    slot_ids = jnp.arange(slot_count, dtype=jnp.int32)
    select = (rank[None, :] == slot_ids[:, None]) & in_level[None, :]
    slot_valid = slot_ids < jnp.sum(in_level.astype(jnp.int32))
    slot_target = jnp.sum(jnp.where(select, down_block[None, :], 0), axis=1)
    return (select, slot_valid, slot_target)


def per_device_chain(
    runoff,
    route_params,
    unit_shapes,
    level_map,
    down_map,
    gauge_reach,
    gauge_sigma,
    observed,
    obs_noise,
):
    conv_table, _ = kernel_table(unit_shapes, runoff.shape[2] // WINDOWS, LANES)
    reach_count, members_dev, series_len = runoff.shape
    flat_len = members_dev * series_len
    slot_count = reach_count // 4
    shape_count = route_params.shape[0]
    inflow = runoff.astype(jnp.float32).reshape(reach_count, flat_len)
    outflow = jnp.zeros_like(inflow)
    reach_ids = jnp.arange(reach_count, dtype=jnp.int32)[:, None]
    params_rows = jnp.transpose(route_params, (1, 2, 0))
    prev_level, prev_down = passed_along((level_map, down_map), "basin", 1)
    for level_now in range(LEVELS):
        select, slot_valid, slot_target_row = level_select(
            level_map, down_map, level_now, slot_count
        )
        gathered = jnp.dot(
            select.astype(jnp.bfloat16),
            inflow.astype(jnp.bfloat16),
            preferred_element_type=jnp.float32,
        )
        gathered = gathered.astype(jnp.bfloat16).reshape(slot_count * members_dev, series_len)
        slot_weights = jnp.einsum(
            "cr,rms->cms", select.astype(jnp.float32), params_rows, precision=lax.Precision.HIGHEST
        ).reshape(-1, shape_count)
        routed = (
            route_rows(gathered, slot_weights, conv_table)
            .astype(jnp.bfloat16)
            .reshape(slot_count, flat_len)
        )
        slot_target = slot_target_row[None, :]
        slot_mask = slot_valid[None, :]
        local_edges = (slot_target == reach_ids) & slot_mask
        chosen = jnp.transpose(select) & slot_mask
        edge_matrix = jnp.concatenate([local_edges, chosen], axis=0).astype(jnp.bfloat16)
        spread_flows = jnp.dot(edge_matrix, routed, preferred_element_type=jnp.float32)
        inflow = inflow + spread_flows[:reach_count]
        outflow = outflow + spread_flows[reach_count:]
        if level_now + 1 < LEVELS:
            arrived = passed_along(routed, "basin", 1)
            prev_select, prev_valid, prev_target = level_select(
                prev_level, prev_down, level_now, slot_count
            )
            incoming = (prev_target[None, :] == reach_ids + reach_count) & prev_valid[None, :]
            inflow = inflow + jnp.dot(
                incoming.astype(jnp.bfloat16), arrived, preferred_element_type=jnp.float32
            )
    flows = outflow.astype(jnp.bfloat16)
    gauge_pick = (gauge_reach[:, None] == jnp.arange(reach_count, dtype=jnp.int32)[None, :]).astype(
        jnp.bfloat16
    )
    gauged = jnp.dot(gauge_pick, flows, preferred_element_type=jnp.float32)
    predicted = jnp.mean(gauged.reshape(-1, members_dev, WINDOWS, series_len // WINDOWS), axis=3)
    scaled = predicted / gauge_sigma[:, None, None]
    innovation = observed[:, None, :] / gauge_sigma[:, None, None] + obs_noise - scaled
    scaled = jnp.transpose(scaled, (0, 2, 1))
    innovation = jnp.transpose(innovation, (0, 2, 1))
    scaled, innovation = (
        lax.all_gather(scaled, "member", axis=2, tiled=True),
        lax.all_gather(innovation, "member", axis=2, tiled=True),
    )
    members = scaled.shape[2]
    scaled = scaled.reshape(-1, members)
    innovation = innovation.reshape(-1, members)
    spread = (scaled - jnp.mean(scaled, axis=1, keepdims=True)) / jnp.sqrt(members - 1.0)
    gram_part = jnp.dot(spread.T, spread, precision=lax.Precision.HIGHEST)
    cross_part = jnp.dot(spread.T, innovation, precision=lax.Precision.HIGHEST)
    gram_part, cross_part = lax.psum((gram_part, cross_part), "basin")
    gram = jnp.eye(members, dtype=jnp.float32) + gram_part
    factor = jnp.linalg.cholesky(gram)
    kalman_gain = jax.scipy.linalg.cho_solve((factor, True), cross_part)
    col_start = lax.axis_index("member") * members_dev
    all_params = lax.all_gather(route_params, "member", axis=2, tiled=True).reshape(-1, members)
    anomaly = all_params - jnp.mean(all_params, axis=1, keepdims=True)
    columns = lax.dynamic_slice_in_dim(kalman_gain, col_start, members_dev, 1)
    increment = jnp.dot(anomaly, columns, precision=lax.Precision.HIGHEST)
    updated = route_params.reshape(-1, members_dev) + increment / jnp.sqrt(members - 1.0)
    return (
        flows.reshape(reach_count, members_dev, series_len),
        updated.reshape(route_params.shape),
    )


def solution(mesh):
    return jax.shard_map(
        per_device,
        mesh=mesh,
        in_specs=(
            P(("groups", "basin"), "member", None),
            P(None, ("groups", "basin"), "member"),
            P(),
            P(("groups", "basin")),
            P(("groups", "basin")),
            P(("groups", "basin")),
            P(("groups", "basin")),
            P(("groups", "basin"), None),
            P(("groups", "basin"), "member", None),
        ),
        out_specs=(P(("groups", "basin"), "member", None), P(None, ("groups", "basin"), "member")),
        check_vma=False,
    )
```

```python
import functools

import jax
import jax.numpy as jnp
from jax import lax
from jax.experimental import pallas as pl
from jax.experimental.pallas import tpu as pltpu
from jax.sharding import PartitionSpec as P

LEVELS = 8
WINDOWS = 64
LANES = 128
EXTRA = 16
HIGHEST = lax.Precision.HIGHEST

def vmem():
    return pl.BlockSpec(memory_space=pltpu.VMEM)


def smem():
    return pl.BlockSpec(memory_space=pltpu.SMEM)


AHEAD = 16
CODE = 64


ORDERS = {
    "basin": ((3, 1, 2), (3, 1, 2)),
    "back": ((3, 1, 2), (2, 3, 1)),
    "member": ((1, 2, 3), (1, 2, 3)),
}


def partners(length, step):
    even, odd = ORDERS[step]
    if even == odd:
        return [0] + list(even)
    side = lax.axis_index("member") % 2
    return [0] + [jnp.where(side == 0, a, b) for a, b in zip(even, odd)]


def kept(x):
    return pltpu.with_memory_space_constraint(x, pltpu.VMEM)


def table_body(shapes_ref, table_ref, window_ref, *, span):
    shape_count, block_len = shapes_ref.shape
    for s in range(shape_count):
        lags = shapes_ref[s : s + 1, :] * (1.0 / block_len)
        lags = jnp.concatenate([lags, jnp.zeros_like(lags)], axis=1)
        skewed = pltpu.roll(
            jnp.broadcast_to(lags, (block_len, 2 * block_len)), 0, 1, stride=1, stride_axis=0
        ).astype(jnp.bfloat16)
        cols = slice(s * block_len, (s + 1) * block_len)
        table_ref[:block_len, cols] = skewed[:, :block_len]
        table_ref[block_len:, cols] = skewed[:, block_len:]
    lag_at = lax.broadcasted_iota(jnp.int32, window_ref.shape, 0)
    col_at = lax.broadcasted_iota(jnp.int32, window_ref.shape, 1)
    window_ref[...] = jnp.where(
        lag_at // span == col_at % (block_len // span), 1.0 / span, 0.0
    ).astype(jnp.bfloat16)


def kernel_table(unit_shapes, span, wide):
    shape_count, block_len = unit_shapes.shape
    return pl.pallas_call(
        functools.partial(table_body, span=span),
        out_shape=[
            pltpu.VMEM((2 * block_len, shape_count * block_len), jnp.bfloat16),
            pltpu.VMEM((block_len, wide), jnp.bfloat16),
        ],
        in_specs=[vmem()],
        out_specs=[vmem()] * 2,
        name="table",
    )(unit_shapes)


def split_two(x):
    top = x.astype(jnp.bfloat16)
    rest = x - top.astype(jnp.float32)
    mid = rest.astype(jnp.bfloat16)
    return top, mid, rest - mid.astype(jnp.float32)


def pack_body(
    level_ref,
    down_ref,
    gauge_ref,
    sigma_ref,
    runoff_ref,
    params_ref,
    observed_ref,
    noise_ref,
    *rest,
):
    out_refs, (own_ref, tile_ref, stage_ref, extra_ref) = rest[:-4], rest[-4:]
    reach_count, members_dev, series_len = runoff_ref.shape
    shape_count = params_ref.shape[0]
    gauge_count, windows = observed_ref.shape
    block_len = out_refs[0].shape[1]
    block_count = series_len // block_len
    share = members_dev // len(out_refs)
    rows = share * block_count
    here = lax.axis_index("basin")
    for r in range(reach_count):
        series = runoff_ref[r].astype(jnp.float32)
        for i in range(block_count):
            at = (r * block_count + i) * members_dev
            for h in range(block_len // LANES):
                lane = i * block_len + h * LANES
                stage_ref[h, at : at + members_dev, :] = series[:, lane : lane + LANES]
    extra_ref[...] = jnp.zeros(extra_ref.shape, jnp.float32)
    for g in range(gauge_count):
        extra_ref[:members_dev, g * windows : (g + 1) * windows] = (
            observed_ref[g : g + 1, :] / sigma_ref[g] + noise_ref[g]
        )
    lower = slice(members_dev, members_dev + reach_count)
    for s in range(shape_count):
        extra_ref[lower, s * members_dev : (s + 1) * members_dev] = params_ref[s]
    at_row = lax.broadcasted_iota(jnp.int32, (reach_count, LANES), 0)
    at_lane = lax.broadcasted_iota(jnp.int32, (reach_count, LANES), 1)
    base = shape_count * members_dev
    facts = extra_ref[lower, :]
    cap = reach_count // 4
    facts = jnp.where(
        (at_lane >= base) & (at_lane < base + cap), jnp.float32(reach_count * CODE), facts
    )
    for r in range(reach_count):
        rank = jnp.int32(0)
        for q in range(r):
            rank = rank + (level_ref[q] == level_ref[r]).astype(jnp.int32)
        here_slot = (at_row == level_ref[r]) & (at_lane == base + rank)
        facts = jnp.where(here_slot, (down_ref[r] + r * CODE).astype(jnp.float32), facts)
    for g in range(gauge_count):
        facts = jnp.where(
            (at_row == g) & (at_lane == base + cap), gauge_ref[g].astype(jnp.float32), facts
        )
        facts = jnp.where((at_row == g) & (at_lane == base + cap + 1), sigma_ref[g], facts)
    upper_top, upper_mid, _ = split_two(extra_ref[:members_dev, :])
    lower_top, lower_mid, lower_low = split_two(facts)
    half = LANES // 2
    lower_top = jnp.where(
        at_lane < half, lower_top.astype(jnp.float32), pltpu.roll(lower_low, half, 1)
    )
    tops = jnp.concatenate([upper_top.astype(jnp.float32), lower_top], axis=0)
    mids = jnp.concatenate(
        [upper_mid.astype(jnp.float32), lower_mid.astype(jnp.float32)], axis=0
    )
    extras = jnp.concatenate([tops, mids], axis=1).astype(jnp.bfloat16)
    for k, out_ref in zip(partners(len(out_refs), "basin"), out_refs):
        to = here ^ k
        for r in range(reach_count):
            for h in range(block_len // LANES):
                pieces = [
                    stage_ref[
                        h,
                        pl.ds(
                            r * block_count * members_dev + share * to + j,
                            block_count,
                            stride=members_dev,
                        ),
                        :,
                    ]
                    for j in range(share)
                ]
                out_ref[r * rows : (r + 1) * rows, h * LANES : (h + 1) * LANES] = jnp.concatenate(
                    pieces, axis=0
                ).astype(jnp.bfloat16)
        out_ref[reach_count * rows :, :] = extras
    own_ref[...] = params_ref[...]
    place_params(params_ref, tile_ref)


def route_body(table_ref, window_ref, *rest, parts, reach_count, shape_count, gauge_count, members_dev):
    in_refs, rest = rest[:parts], rest[parts:]
    out_refs, rest = rest[:parts], rest[parts:]
    base_ref, state_ref, flows_ref, left_ref, weight_ref, code_ref = rest
    block_len = table_ref.shape[0] // 2
    rows = state_ref.shape[1]
    share = members_dev // parts
    block_count = rows // share
    total = parts * reach_count
    cap = reach_count // 4
    here = lax.axis_index("basin")
    half = LANES // 2
    base = shape_count * members_dev
    span = LANES // parts
    at_lane = lax.broadcasted_iota(jnp.int32, (reach_count, LANES), 1)
    facts = jnp.zeros((reach_count, LANES), jnp.float32)
    for k, in_ref in zip(partners(len(in_refs), "basin"), in_refs):
        source = here ^ k
        extras = in_ref[reach_count * rows :, :].astype(jnp.float32)
        tops, mids = extras[:, :LANES], extras[:, LANES:]
        base_ref[source] = tops[:members_dev] + mids[:members_dev]
        low = pltpu.roll(tops[members_dev:], half, 1)
        part = jnp.where(at_lane < span, tops[members_dev:] + (mids[members_dev:] + low), 0.0)
        facts = facts + pltpu.roll(part, source * span, 1)
    whole = facts.astype(jnp.int32)
    for level_now in range(LEVELS):
        for c in range(parts * cap):
            code_ref[level_now * parts * cap + c] = whole[
                level_now, (c // cap) * span + base + c % cap
            ]
    mine = pltpu.roll(facts, LANES - share * here, 1)
    for n in range(parts):
        for s in range(shape_count):
            for j in range(share):
                lane = n * span + s * members_dev + j
                weight_ref[s * share + j, n * reach_count : (n + 1) * reach_count, :] = (
                    jnp.broadcast_to(mine[:, lane : lane + 1], (reach_count, LANES))
                )
    for k, in_ref in zip(partners(len(in_refs), "basin"), in_refs):
        source = here ^ k
        for r in range(reach_count):
            state_ref[source * reach_count + r] = in_ref[r * rows : (r + 1) * rows, :].astype(
                jnp.float32
            )
    state_ref[total] = jnp.zeros(state_ref.shape[1:], jnp.float32)
    state_ref[total + 1] = jnp.zeros(state_ref.shape[1:], jnp.float32)

    first_row = lax.broadcasted_iota(jnp.int32, (block_count, block_len), 0) == 0
    slots = parts * cap

    def one_level(level_now, carry):
        picked, goals, sources = [], [], []
        for c in range(slots):
            code = code_ref[level_now * slots + c]
            reach = code // CODE
            goal = (c // cap) * reach_count + code % CODE
            real = reach < reach_count
            kept_goal = (goal < (c // cap + 2) * reach_count) & (goal < total) & real
            sources.append((c // cap) * reach_count + jnp.where(real, reach, 0))
            picked.append(jnp.where(real, (c // cap) * reach_count + reach, total))
            goals.append(jnp.where(kept_goal, goal, total + 1))
        for c in range(slots):
            rows_now = state_ref[picked[c]]
            left_ref[c * rows : (c + 1) * rows, :block_len] = rows_now.astype(jnp.bfloat16)
            earlier = [
                jnp.where(
                    first_row,
                    0.0,
                    pltpu.roll(rows_now[j * block_count : (j + 1) * block_count], 1, 0),
                )
                for j in range(share)
            ]
            left_ref[c * rows : (c + 1) * rows, block_len:] = jnp.concatenate(
                earlier, axis=0
            ).astype(jnp.bfloat16)
        left = left_ref[...]
        mixed = [
            jnp.dot(
                left,
                table_ref[:, s * block_len : (s + 1) * block_len],
                preferred_element_type=jnp.float32,
            )
            for s in range(shape_count)
        ]
        for c in range(slots):
            pieces = []
            for j in range(share):
                at = slice(c * rows + j * block_count, c * rows + (j + 1) * block_count)
                piece = None
                for s in range(shape_count):
                    weight = weight_ref[s * share + j, pl.ds(sources[c], 1), :]
                    weight = jnp.concatenate([weight] * (block_len // LANES), axis=1)
                    term = mixed[s][at] * weight
                    piece = term if piece is None else piece + term
                pieces.append(piece)
            routed = jnp.concatenate(pieces, axis=0).astype(jnp.bfloat16)
            flows_ref[picked[c]] = routed
            state_ref[goals[c]] = state_ref[goals[c]] + routed.astype(jnp.float32)
        return carry

    lax.fori_loop(0, LEVELS, one_level, 0)

    gauges = parts * gauge_count
    wide = gauges * WINDOWS
    per_block = WINDOWS // block_count
    for g in range(gauges):
        reach = (g // gauge_count) * reach_count + whole[
            g % gauge_count, (g // gauge_count) * span + base + cap
        ]
        left_ref[g * rows : (g + 1) * rows, :block_len] = flows_ref[reach]
    means = jnp.dot(
        left_ref[: gauges * rows, :block_len], window_ref[...], preferred_element_type=jnp.float32
    )
    row_at = lax.broadcasted_iota(jnp.int32, (block_count, wide), 0)
    col_at = lax.broadcasted_iota(jnp.int32, (block_count, wide), 1)
    sigma_row = jnp.zeros((1, wide), jnp.float32)
    for g in range(gauges):
        sigma = facts[g % gauge_count, (g // gauge_count) * span + base + cap + 1]
        sigma_row = jnp.where(col_at[:1] // WINDOWS == g, sigma, sigma_row)
    scaled = []
    for j in range(share):
        merged = jnp.zeros((block_count, wide), jnp.float32)
        for g in range(gauges):
            at = g * rows + j * block_count
            merged = jnp.where(
                (col_at // per_block) == g * block_count + row_at,
                means[at : at + block_count],
                merged,
            )
        scaled.append(jnp.sum(merged, axis=0, keepdims=True) / sigma_row)
    scaled = jnp.concatenate(scaled, axis=0)
    top, mid, low = split_two(scaled)
    chunks = []
    for part in (top.astype(jnp.float32), mid.astype(jnp.float32), low):
        chunks += [part[:, i * block_len : (i + 1) * block_len] for i in range(wide // block_len)]
    used = len(chunks) * share
    chunks.append(jnp.zeros((EXTRA - used, block_len), jnp.float32))
    extras = jnp.concatenate(chunks, axis=0).astype(jnp.bfloat16)
    for k, out_ref in zip(partners(len(out_refs), "back"), out_refs):
        to = here ^ k
        for r in range(reach_count):
            out_ref[r * rows : (r + 1) * rows, :] = flows_ref[to * reach_count + r]
        out_ref[reach_count * rows :, :] = extras


def gather_body(tile_ref, *rest, wide):
    in_refs, out_ref = rest[:-1], rest[-1]
    parts = len(in_refs)
    members_dev = out_ref.shape[0]
    share = members_dev // parts
    block_len = in_refs[0].shape[1]
    here = lax.axis_index("basin")
    pieces = wide // block_len
    at_row = lax.broadcasted_iota(jnp.int32, (members_dev, block_len), 0)
    placed = [jnp.zeros((members_dev, block_len), jnp.float32)] * pieces
    for k, in_ref in zip(partners(len(in_refs), "back"), in_refs):
        extras = in_ref[in_ref.shape[0] - EXTRA :, :].astype(jnp.float32)
        for i in range(pieces):
            for j in range(share):
                value = sum(
                    extras[(p * pieces + i) * share + j : (p * pieces + i) * share + j + 1]
                    for p in range(3)
                )
                placed[i] = jnp.where(at_row == share * (here ^ k) + j, value, placed[i])
    for i in range(pieces):
        out_ref[:, i * block_len : (i + 1) * block_len] = placed[i]
    out_ref[:, wide:] = tile_ref[...]


def place_params(params_ref, tile_ref):
    shape_count, _, members_dev = params_ref.shape
    members = members_dev * lax.axis_size("member")
    tile_ref[...] = jnp.zeros(tile_ref.shape, jnp.float32)
    for s in range(shape_count):
        tile_ref[:, s * members : s * members + members_dev] = params_ref[s]
    tile_ref[...] = pltpu.roll(tile_ref[...], lax.axis_index("member") * members_dev, 1)


def unpack_body(*refs, parts, reach_count):
    in_refs, (out_ref, stage_ref) = refs[:parts], refs[parts:]
    members_dev = out_ref.shape[1]
    block_len = in_refs[0].shape[1]
    share = members_dev // parts
    block_count = out_ref.shape[2] // block_len
    rows = share * block_count
    here = lax.axis_index("basin")
    for k, in_ref in zip(partners(len(in_refs), "back"), in_refs):
        source = here ^ k
        for r in range(reach_count):
            piece = in_ref[r * rows : (r + 1) * rows, :].astype(jnp.float32)
            for j in range(share):
                for h in range(block_len // LANES):
                    stage_ref[
                        h,
                        pl.ds(
                            r * block_count * members_dev + share * source + j,
                            block_count,
                            stride=members_dev,
                        ),
                        :,
                    ] = piece[j * block_count : (j + 1) * block_count, h * LANES : (h + 1) * LANES]
    for r in range(reach_count):
        for i in range(block_count):
            at = (r * block_count + i) * members_dev
            for h in range(block_len // LANES):
                lane = i * block_len + h * LANES
                out_ref[r, :, lane : lane + LANES] = stage_ref[
                    h, at : at + members_dev, :
                ].astype(jnp.bfloat16)


def solve_body(base_ref, params_ref, *rest):
    in_refs, (out_ref, all_ref, right_ref) = rest[:-3], rest[-3:]
    shape_count, reach_count, members_dev = params_ref.shape
    groups = len(in_refs)
    members = groups * members_dev
    wide = all_ref.shape[1]
    here = lax.axis_index("member")
    tiles = None
    for k, in_ref in zip(partners(len(in_refs), "member"), in_refs):
        at = pl.multiple_of((here ^ k) * members_dev, members_dev)
        all_ref[pl.ds(at, members_dev), :] = in_ref[:, :wide]
        tile = in_ref[:, wide:]
        tiles = tile if tiles is None else tiles + tile
    scaled = all_ref[...]
    root = jnp.sqrt(jnp.float32(members - 1))
    spread = (scaled - jnp.mean(scaled, axis=0, keepdims=True)) / root
    own = in_refs[0][:, :wide]
    right_ref[:members, :] = spread
    for n in range(base_ref.shape[0]):
        cols = slice(n * base_ref.shape[2], (n + 1) * base_ref.shape[2])
        right_ref[members : members + members_dev, cols] = base_ref[n] - own[:, cols]
    right_ref[members + members_dev :, :] = jnp.zeros(
        (right_ref.shape[0] - members - members_dev, wide), jnp.float32
    )
    system = lax.dot_general(
        spread,
        right_ref[...],
        (((1,), (1,)), ((), ())),
        precision=HIGHEST,
        preferred_element_type=jnp.float32,
    )
    row_at = lax.broadcasted_iota(jnp.int32, system.shape, 0)
    col_at = lax.broadcasted_iota(jnp.int32, system.shape, 1)
    system = system + jnp.where(row_at == col_at, 1.0, 0.0)
    for first in range(0, members, AHEAD):
        cols = [
            jnp.broadcast_to(system[:, i : i + 1], system.shape)
            for i in range(first, first + AHEAD)
        ]
        for t in range(AHEAD):
            i = first + t
            own_row = row_at == i
            inverse = 1.0 / cols[t][i : i + 1, :]
            pivot_row = system[i : i + 1, :] * inverse
            system = jnp.where(own_row, pivot_row, system - cols[t] * pivot_row)
            for u in range(t + 1, AHEAD):
                pivot_row = cols[u][i : i + 1, :] * inverse
                cols[u] = jnp.where(own_row, pivot_row, cols[u] - cols[t] * pivot_row)
    gain = system[:, members : members + members_dev]
    theta = jnp.concatenate(
        [tiles[:, s * members : (s + 1) * members] for s in range(shape_count)], axis=0
    )
    anomaly = theta - jnp.mean(theta, axis=1, keepdims=True)
    step = (
        jnp.dot(anomaly, gain, precision=HIGHEST, preferred_element_type=jnp.float32) / root
    )
    for s in range(shape_count):
        out_ref[s] = params_ref[s] + step[s * reach_count : (s + 1) * reach_count]


def swapped(pieces, axis, step):
    results = [pieces[0]]
    groups = lax.axis_size("member")
    for piece, *by in zip(pieces[1:], *ORDERS[step]):
        if axis == "member":
            pairs = [(m, m ^ by[m % 2]) for m in range(groups)]
            results.append(lax.ppermute(piece, axis, pairs))
        else:
            pairs = [
                (b * groups + m, (b ^ by[m % 2]) * groups + m)
                for b in range(lax.axis_size(axis))
                for m in range(groups)
            ]
            results.append(lax.ppermute(piece, (axis, "member"), pairs))
    return results


def per_device_split(
    runoff,
    route_params,
    unit_shapes,
    level_map,
    down_map,
    gauge_reach,
    gauge_sigma,
    observed,
    obs_noise,
):
    f32, bf16 = jnp.float32, jnp.bfloat16
    parts, groups = lax.axis_size("basin"), lax.axis_size("member")
    reach_count, members_dev, series_len = runoff.shape
    shape_count, block_len = unit_shapes.shape
    gauge_count = observed.shape[0]
    block_count = series_len // block_len
    share = members_dev // parts
    rows = share * block_count
    total = parts * reach_count
    cap = reach_count // 4
    wide = parts * gauge_count * WINDOWS
    members = members_dev * groups
    sent = pltpu.VMEM((reach_count * rows + EXTRA, block_len), bf16)
    *packed, own_params, tile = pl.pallas_call(
        pack_body,
        out_shape=[sent] * parts
        + [pltpu.VMEM(route_params.shape, f32), pltpu.VMEM((reach_count, LANES), f32)],
        in_specs=[smem()] * 4 + [vmem()] * 4,
        out_specs=[vmem()] * (parts + 2),
        scratch_shapes=[
            pltpu.VMEM((block_len // LANES, reach_count * members_dev * block_count, LANES), f32),
            pltpu.VMEM((members_dev + reach_count, LANES), f32),
        ],
        name="pack",
    )(level_map, down_map, gauge_reach, gauge_sigma, runoff, route_params, observed, obs_noise)
    arrived = swapped(packed, "basin", "basin")
    conv_table, window_table = kernel_table(unit_shapes, series_len // WINDOWS, wide)
    *routed, noise_base = pl.pallas_call(
        functools.partial(
            route_body,
            parts=parts,
            reach_count=reach_count,
            shape_count=shape_count,
            gauge_count=gauge_count,
            members_dev=members_dev,
        ),
        out_shape=[sent] * parts
        + [pltpu.VMEM((parts, members_dev, gauge_count * WINDOWS), f32)],
        in_specs=[vmem()] * (2 + parts),
        out_specs=[vmem()] * (parts + 1),
        scratch_shapes=[
            pltpu.VMEM((total + 2, rows, block_len), f32),
            pltpu.VMEM((total + 1, rows, block_len), bf16),
            pltpu.VMEM((parts * max(cap, gauge_count) * rows, 2 * block_len), bf16),
            pltpu.VMEM((shape_count * share, total, LANES), f32),
            pltpu.SMEM((LEVELS * parts * cap,), jnp.int32),
        ],
        name="route",
    )(kept(conv_table), kept(window_table), *map(kept, arrived))
    returned = swapped(routed, "basin", "back")
    local = pl.pallas_call(
        functools.partial(gather_body, wide=wide),
        out_shape=pltpu.VMEM((members_dev, wide + LANES), f32),
        in_specs=[vmem()] * (1 + parts),
        out_specs=vmem(),
        name="gather",
    )(kept(tile), *map(kept, returned))
    everyone = swapped([local] * groups, "member", "member")
    flows = pl.pallas_call(
        functools.partial(unpack_body, parts=parts, reach_count=reach_count),
        out_shape=jax.ShapeDtypeStruct(runoff.shape, bf16),
        in_specs=[vmem()] * parts,
        out_specs=vmem(),
        scratch_shapes=[pltpu.VMEM((block_len // LANES, reach_count * members_dev * block_count, LANES), f32)],
        name="unpack",
    )(*map(kept, returned))
    updated = pl.pallas_call(
        solve_body,
        out_shape=jax.ShapeDtypeStruct(route_params.shape, f32),
        in_specs=[vmem()] * (2 + groups),
        out_specs=vmem(),
        scratch_shapes=[pltpu.VMEM((members, wide), f32), pltpu.VMEM((LANES, wide), f32)],
        name="solve",
    )(kept(noise_base), kept(own_params), *map(kept, everyone))
    return flows, updated


def per_device(*args):
    runoff, route_params, unit_shapes, _, _, _, _, observed, _ = args
    parts, groups = lax.axis_size("basin"), lax.axis_size("member")
    reach_count, members_dev, series_len = runoff.shape
    shape_count, block_len = unit_shapes.shape
    block_count = series_len // block_len
    gauge_count = observed.shape[0]
    wide = parts * gauge_count * WINDOWS
    share = max(members_dev // parts, 1)
    fits = (
        parts == 4
        and groups == 4
        and members_dev == share * parts
        and reach_count == 8
        and members_dev == 8
        and block_count == 8
        and series_len % block_len == 0
        and block_len == 2 * LANES
        and gauge_count * WINDOWS == LANES
        and wide % block_len == 0
        and 3 * share * (wide // block_len) <= EXTRA
        and shape_count * members_dev + reach_count // 4 + 2 <= LANES // parts
        and 2 * reach_count < CODE
        and parts >= 2
        and reach_count == LEVELS
        and shape_count * groups * members_dev <= LANES
        and groups * members_dev + members_dev <= LANES
    )
    if fits:
        return per_device_split(*args)
    return per_device_chain(*args)


def passed_along(x, axis, by):
    length = lax.axis_size(axis)
    pairs = [(i, i + by) for i in range(length) if 0 <= i + by < length]
    return lax.ppermute(x, axis, pairs)


def route_rows(inflow_rows, slot_weights, conv_table):
    block_len = conv_table.shape[0] // 2
    row_count, series_len = inflow_rows.shape
    blocks = inflow_rows.reshape(row_count, series_len // block_len, block_len)
    earlier = jnp.concatenate([jnp.zeros_like(blocks[:, :1]), blocks[:, :-1]], axis=1)
    joined = jnp.concatenate([blocks, earlier], axis=2).reshape(-1, 2 * block_len)
    mixed_blocks = jnp.dot(joined, conv_table, preferred_element_type=jnp.float32)
    mixed_blocks = mixed_blocks.reshape(
        row_count, series_len // block_len, slot_weights.shape[1], block_len
    )
    return jnp.sum(mixed_blocks * slot_weights[:, None, :, None], axis=2).reshape(
        row_count, series_len
    )


def level_select(level_block, down_block, level_now, slot_count):
    entry_count = level_block.shape[0]
    entry_ids = jnp.arange(entry_count, dtype=jnp.int32)
    in_level = level_block == level_now
    before = (entry_ids[None, :] < entry_ids[:, None]) & in_level[None, :]
    rank = jnp.sum(before.astype(jnp.int32), axis=1)
    slot_ids = jnp.arange(slot_count, dtype=jnp.int32)
    select = (rank[None, :] == slot_ids[:, None]) & in_level[None, :]
    slot_valid = slot_ids < jnp.sum(in_level.astype(jnp.int32))
    slot_target = jnp.sum(jnp.where(select, down_block[None, :], 0), axis=1)
    return (select, slot_valid, slot_target)


def per_device_chain(
    runoff,
    route_params,
    unit_shapes,
    level_map,
    down_map,
    gauge_reach,
    gauge_sigma,
    observed,
    obs_noise,
):
    conv_table, _ = kernel_table(unit_shapes, runoff.shape[2] // WINDOWS, LANES)
    reach_count, members_dev, series_len = runoff.shape
    flat_len = members_dev * series_len
    slot_count = reach_count // 4
    shape_count = route_params.shape[0]
    inflow = runoff.astype(jnp.float32).reshape(reach_count, flat_len)
    outflow = jnp.zeros_like(inflow)
    reach_ids = jnp.arange(reach_count, dtype=jnp.int32)[:, None]
    params_rows = jnp.transpose(route_params, (1, 2, 0))
    prev_level, prev_down = passed_along((level_map, down_map), "basin", 1)
    for level_now in range(LEVELS):
        select, slot_valid, slot_target_row = level_select(
            level_map, down_map, level_now, slot_count
        )
        gathered = jnp.dot(
            select.astype(jnp.bfloat16),
            inflow.astype(jnp.bfloat16),
            preferred_element_type=jnp.float32,
        )
        gathered = gathered.astype(jnp.bfloat16).reshape(slot_count * members_dev, series_len)
        slot_weights = jnp.einsum(
            "cr,rms->cms", select.astype(jnp.float32), params_rows, precision=lax.Precision.HIGHEST
        ).reshape(-1, shape_count)
        routed = (
            route_rows(gathered, slot_weights, conv_table)
            .astype(jnp.bfloat16)
            .reshape(slot_count, flat_len)
        )
        slot_target = slot_target_row[None, :]
        slot_mask = slot_valid[None, :]
        local_edges = (slot_target == reach_ids) & slot_mask
        chosen = jnp.transpose(select) & slot_mask
        edge_matrix = jnp.concatenate([local_edges, chosen], axis=0).astype(jnp.bfloat16)
        spread_flows = jnp.dot(edge_matrix, routed, preferred_element_type=jnp.float32)
        inflow = inflow + spread_flows[:reach_count]
        outflow = outflow + spread_flows[reach_count:]
        if level_now + 1 < LEVELS:
            arrived = passed_along(routed, "basin", 1)
            prev_select, prev_valid, prev_target = level_select(
                prev_level, prev_down, level_now, slot_count
            )
            incoming = (prev_target[None, :] == reach_ids + reach_count) & prev_valid[None, :]
            inflow = inflow + jnp.dot(
                incoming.astype(jnp.bfloat16), arrived, preferred_element_type=jnp.float32
            )
    flows = outflow.astype(jnp.bfloat16)
    gauge_pick = (gauge_reach[:, None] == jnp.arange(reach_count, dtype=jnp.int32)[None, :]).astype(
        jnp.bfloat16
    )
    gauged = jnp.dot(gauge_pick, flows, preferred_element_type=jnp.float32)
    predicted = jnp.mean(gauged.reshape(-1, members_dev, WINDOWS, series_len // WINDOWS), axis=3)
    scaled = predicted / gauge_sigma[:, None, None]
    innovation = observed[:, None, :] / gauge_sigma[:, None, None] + obs_noise - scaled
    scaled = jnp.transpose(scaled, (0, 2, 1))
    innovation = jnp.transpose(innovation, (0, 2, 1))
    scaled, innovation = (
        lax.all_gather(scaled, "member", axis=2, tiled=True),
        lax.all_gather(innovation, "member", axis=2, tiled=True),
    )
    members = scaled.shape[2]
    scaled = scaled.reshape(-1, members)
    innovation = innovation.reshape(-1, members)
    spread = (scaled - jnp.mean(scaled, axis=1, keepdims=True)) / jnp.sqrt(members - 1.0)
    gram_part = jnp.dot(spread.T, spread, precision=lax.Precision.HIGHEST)
    cross_part = jnp.dot(spread.T, innovation, precision=lax.Precision.HIGHEST)
    gram_part, cross_part = lax.psum((gram_part, cross_part), "basin")
    gram = jnp.eye(members, dtype=jnp.float32) + gram_part
    factor = jnp.linalg.cholesky(gram)
    kalman_gain = jax.scipy.linalg.cho_solve((factor, True), cross_part)
    col_start = lax.axis_index("member") * members_dev
    all_params = lax.all_gather(route_params, "member", axis=2, tiled=True).reshape(-1, members)
    anomaly = all_params - jnp.mean(all_params, axis=1, keepdims=True)
    columns = lax.dynamic_slice_in_dim(kalman_gain, col_start, members_dev, 1)
    increment = jnp.dot(anomaly, columns, precision=lax.Precision.HIGHEST)
    updated = route_params.reshape(-1, members_dev) + increment / jnp.sqrt(members - 1.0)
    return (
        flows.reshape(reach_count, members_dev, series_len),
        updated.reshape(route_params.shape),
    )


def solution(mesh):
    return jax.shard_map(
        per_device,
        mesh=mesh,
        in_specs=(
            P(("groups", "basin"), "member", None),
            P(None, ("groups", "basin"), "member"),
            P(),
            P(("groups", "basin")),
            P(("groups", "basin")),
            P(("groups", "basin")),
            P(("groups", "basin")),
            P(("groups", "basin"), None),
            P(("groups", "basin"), "member", None),
        ),
        out_specs=(P(("groups", "basin"), "member", None), P(None, ("groups", "basin"), "member")),
        check_vma=False,
    )
```

```python
import functools

import jax
import jax.numpy as jnp
from jax import lax
from jax.experimental import pallas as pl
from jax.experimental.pallas import tpu as pltpu
from jax.sharding import PartitionSpec as P

LEVELS = 8
WINDOWS = 64
LANES = 128
EXTRA = 16
HIGHEST = lax.Precision.HIGHEST

def vmem():
    return pl.BlockSpec(memory_space=pltpu.VMEM)


def smem():
    return pl.BlockSpec(memory_space=pltpu.SMEM)


AHEAD = 16
CODE = 64


ORDERS = {
    "basin": ((3, 1, 2), (3, 1, 2)),
    "back": ((3, 1, 2), (2, 3, 1)),
    "member": ((1, 2, 3), (1, 2, 3)),
}


def partners(length, step):
    even, odd = ORDERS[step]
    if even == odd:
        return [0] + list(even)
    side = lax.axis_index("member") % 2
    return [0] + [jnp.where(side == 0, a, b) for a, b in zip(even, odd)]


def kept(x):
    return pltpu.with_memory_space_constraint(x, pltpu.VMEM)


def table_body(shapes_ref, table_ref, window_ref, *, span):
    shape_count, block_len = shapes_ref.shape
    for s in range(shape_count):
        lags = shapes_ref[s : s + 1, :] * (1.0 / block_len)
        lags = jnp.concatenate([lags, jnp.zeros_like(lags)], axis=1)
        skewed = pltpu.roll(
            jnp.broadcast_to(lags, (block_len, 2 * block_len)), 0, 1, stride=1, stride_axis=0
        ).astype(jnp.bfloat16)
        cols = slice(s * block_len, (s + 1) * block_len)
        table_ref[:block_len, cols] = skewed[:, :block_len]
        table_ref[block_len:, cols] = skewed[:, block_len:]
    lag_at = lax.broadcasted_iota(jnp.int32, window_ref.shape, 0)
    col_at = lax.broadcasted_iota(jnp.int32, window_ref.shape, 1)
    window_ref[...] = jnp.where(
        lag_at // span == col_at % (block_len // span), 1.0 / span, 0.0
    ).astype(jnp.bfloat16)


def kernel_table(unit_shapes, span, wide):
    shape_count, block_len = unit_shapes.shape
    return pl.pallas_call(
        functools.partial(table_body, span=span),
        out_shape=[
            pltpu.VMEM((2 * block_len, shape_count * block_len), jnp.bfloat16),
            pltpu.VMEM((block_len, wide), jnp.bfloat16),
        ],
        in_specs=[vmem()],
        out_specs=[vmem()] * 2,
        name="table",
    )(unit_shapes)


def split_two(x):
    top = x.astype(jnp.bfloat16)
    rest = x - top.astype(jnp.float32)
    mid = rest.astype(jnp.bfloat16)
    return top, mid, rest - mid.astype(jnp.float32)


def pack_body(
    level_ref,
    down_ref,
    gauge_ref,
    sigma_ref,
    runoff_ref,
    params_ref,
    observed_ref,
    noise_ref,
    *rest,
):
    out_refs, (own_ref, tile_ref, base_ref, stage_ref, extra_ref) = rest[:-5], rest[-5:]
    reach_count, members_dev, series_len = runoff_ref.shape
    shape_count = params_ref.shape[0]
    gauge_count, windows = observed_ref.shape
    block_len = out_refs[0].shape[1]
    block_count = series_len // block_len
    share = members_dev // len(out_refs)
    rows = share * block_count
    here = lax.axis_index("basin")
    for r in range(reach_count):
        series = runoff_ref[r].astype(jnp.float32)
        for i in range(block_count):
            at = (r * block_count + i) * members_dev
            for h in range(block_len // LANES):
                lane = i * block_len + h * LANES
                stage_ref[h, at : at + members_dev, :] = series[:, lane : lane + LANES]
    extra_ref[...] = jnp.zeros(extra_ref.shape, jnp.float32)
    for g in range(gauge_count):
        base_ref[:, g * windows : (g + 1) * windows] = (
            observed_ref[g : g + 1, :] / sigma_ref[g] + noise_ref[g]
        )
    for s in range(shape_count):
        extra_ref[:, s * members_dev : (s + 1) * members_dev] = params_ref[s]
    at_row = lax.broadcasted_iota(jnp.int32, (reach_count, LANES), 0)
    at_lane = lax.broadcasted_iota(jnp.int32, (reach_count, LANES), 1)
    base = shape_count * members_dev
    facts = extra_ref[...]
    cap = reach_count // 4
    facts = jnp.where(
        (at_lane >= base) & (at_lane < base + cap), jnp.float32(reach_count * CODE), facts
    )
    for r in range(reach_count):
        rank = jnp.int32(0)
        for q in range(r):
            rank = rank + (level_ref[q] == level_ref[r]).astype(jnp.int32)
        here_slot = (at_row == level_ref[r]) & (at_lane == base + rank)
        facts = jnp.where(here_slot, (down_ref[r] + r * CODE).astype(jnp.float32), facts)
    for g in range(gauge_count):
        facts = jnp.where(
            (at_row == g) & (at_lane == base + cap), gauge_ref[g].astype(jnp.float32), facts
        )
        facts = jnp.where((at_row == g) & (at_lane == base + cap + 1), sigma_ref[g], facts)
    span = LANES // len(out_refs)
    top, mid, low = split_two(facts)
    terms = (
        top.astype(jnp.float32)
        + pltpu.roll(mid.astype(jnp.float32), span, 1)
        + pltpu.roll(low, 2 * span, 1)
    )
    extras = jnp.concatenate([terms, base_ref[...]], axis=1).astype(jnp.bfloat16)
    for k, out_ref in zip(partners(len(out_refs), "basin"), out_refs):
        to = here ^ k
        for r in range(reach_count):
            for h in range(block_len // LANES):
                pieces = [
                    stage_ref[
                        h,
                        pl.ds(
                            r * block_count * members_dev + share * to + j,
                            block_count,
                            stride=members_dev,
                        ),
                        :,
                    ]
                    for j in range(share)
                ]
                out_ref[r * rows : (r + 1) * rows, h * LANES : (h + 1) * LANES] = jnp.concatenate(
                    pieces, axis=0
                ).astype(jnp.bfloat16)
        out_ref[reach_count * rows :, :] = extras
    own_ref[...] = params_ref[...]
    place_params(params_ref, tile_ref)


def route_body(
    table_ref, window_ref, own_base_ref, *rest, parts, reach_count, shape_count, gauge_count, members_dev
):
    in_refs, rest = rest[:parts], rest[parts:]
    out_refs, rest = rest[:parts], rest[parts:]
    base_ref, state_ref, flows_ref, left_ref, weight_ref, code_ref = rest
    block_len = table_ref.shape[0] // 2
    rows = state_ref.shape[1]
    share = members_dev // parts
    block_count = rows // share
    total = parts * reach_count
    cap = reach_count // 4
    here = lax.axis_index("basin")
    base = shape_count * members_dev
    span = LANES // parts
    at_lane = lax.broadcasted_iota(jnp.int32, (reach_count, LANES), 1)
    facts = jnp.zeros((reach_count, LANES), jnp.float32)
    for k, in_ref in zip(partners(len(in_refs), "basin"), in_refs):
        source = here ^ k
        extras = in_ref[reach_count * rows :, :].astype(jnp.float32)
        terms = extras[:, :LANES]
        base_ref[source] = extras[:, LANES:]
        rest_terms = pltpu.roll(terms, LANES - span, 1) + pltpu.roll(terms, LANES - 2 * span, 1)
        part = jnp.where(at_lane < span, terms + rest_terms, 0.0)
        facts = facts + pltpu.roll(part, source * span, 1)
    whole = facts.astype(jnp.int32)
    for level_now in range(LEVELS):
        for c in range(parts * cap):
            code_ref[level_now * parts * cap + c] = whole[
                level_now, (c // cap) * span + base + c % cap
            ]
    mine = pltpu.roll(facts, LANES - share * here, 1)
    for n in range(parts):
        for s in range(shape_count):
            for j in range(share):
                lane = n * span + s * members_dev + j
                weight_ref[s * share + j, n * reach_count : (n + 1) * reach_count, :] = (
                    jnp.broadcast_to(mine[:, lane : lane + 1], (reach_count, LANES))
                )
    for k, in_ref in zip(partners(len(in_refs), "basin"), in_refs):
        source = here ^ k
        for r in range(reach_count):
            state_ref[source * reach_count + r] = in_ref[r * rows : (r + 1) * rows, :].astype(
                jnp.float32
            )
    state_ref[total] = jnp.zeros(state_ref.shape[1:], jnp.float32)
    state_ref[total + 1] = jnp.zeros(state_ref.shape[1:], jnp.float32)

    first_row = lax.broadcasted_iota(jnp.int32, (block_count, block_len), 0) == 0
    slots = parts * cap

    def one_level(level_now, carry):
        picked, goals, sources = [], [], []
        for c in range(slots):
            code = code_ref[level_now * slots + c]
            reach = code // CODE
            goal = (c // cap) * reach_count + code % CODE
            real = reach < reach_count
            kept_goal = (goal < (c // cap + 2) * reach_count) & (goal < total) & real
            sources.append((c // cap) * reach_count + jnp.where(real, reach, 0))
            picked.append(jnp.where(real, (c // cap) * reach_count + reach, total))
            goals.append(jnp.where(kept_goal, goal, total + 1))
        for c in range(slots):
            rows_now = state_ref[picked[c]]
            left_ref[c * rows : (c + 1) * rows, :block_len] = rows_now.astype(jnp.bfloat16)
            earlier = [
                jnp.where(
                    first_row,
                    0.0,
                    pltpu.roll(rows_now[j * block_count : (j + 1) * block_count], 1, 0),
                )
                for j in range(share)
            ]
            left_ref[c * rows : (c + 1) * rows, block_len:] = jnp.concatenate(
                earlier, axis=0
            ).astype(jnp.bfloat16)
        left = left_ref[...]
        mixed = [
            jnp.dot(
                left,
                table_ref[:, s * block_len : (s + 1) * block_len],
                preferred_element_type=jnp.float32,
            )
            for s in range(shape_count)
        ]
        for c in range(slots):
            pieces = []
            for j in range(share):
                at = slice(c * rows + j * block_count, c * rows + (j + 1) * block_count)
                piece = None
                for s in range(shape_count):
                    weight = weight_ref[s * share + j, pl.ds(sources[c], 1), :]
                    weight = jnp.concatenate([weight] * (block_len // LANES), axis=1)
                    term = mixed[s][at] * weight
                    piece = term if piece is None else piece + term
                pieces.append(piece)
            routed = jnp.concatenate(pieces, axis=0).astype(jnp.bfloat16)
            flows_ref[picked[c]] = routed
            state_ref[goals[c]] = state_ref[goals[c]] + routed.astype(jnp.float32)
        return carry

    lax.fori_loop(0, LEVELS, one_level, 0)

    gauges = parts * gauge_count
    wide = gauges * WINDOWS
    per_block = WINDOWS // block_count
    for g in range(gauges):
        reach = (g // gauge_count) * reach_count + whole[
            g % gauge_count, (g // gauge_count) * span + base + cap
        ]
        left_ref[g * rows : (g + 1) * rows, :block_len] = flows_ref[reach]
    means = jnp.dot(
        left_ref[: gauges * rows, :block_len], window_ref[...], preferred_element_type=jnp.float32
    )
    row_at = lax.broadcasted_iota(jnp.int32, (block_count, wide), 0)
    col_at = lax.broadcasted_iota(jnp.int32, (block_count, wide), 1)
    sigma_row = jnp.zeros((1, wide), jnp.float32)
    for g in range(gauges):
        sigma = facts[g % gauge_count, (g // gauge_count) * span + base + cap + 1]
        sigma_row = jnp.where(col_at[:1] // WINDOWS == g, sigma, sigma_row)
    scaled = []
    for j in range(share):
        merged = jnp.zeros((block_count, wide), jnp.float32)
        for g in range(gauges):
            at = g * rows + j * block_count
            merged = jnp.where(
                (col_at // per_block) == g * block_count + row_at,
                means[at : at + block_count],
                merged,
            )
        scaled.append(jnp.sum(merged, axis=0, keepdims=True) / sigma_row)
    scaled = jnp.concatenate(scaled, axis=0)
    top, mid, low = split_two(scaled)
    _, base_mid, _ = split_two(own_base_ref[...])
    base_mid = base_mid.astype(jnp.float32)
    middle = members_dev // 2
    chunks = [jnp.concatenate([base_mid[:middle], base_mid[middle:]], axis=1)]
    for part in (top.astype(jnp.float32), mid.astype(jnp.float32), low):
        chunks += [part[:, i * block_len : (i + 1) * block_len] for i in range(wide // block_len)]
    used = middle + (len(chunks) - 1) * share
    if used < EXTRA:
        chunks.append(jnp.zeros((EXTRA - used, block_len), jnp.float32))
    extras = jnp.concatenate(chunks, axis=0).astype(jnp.bfloat16)
    for k, out_ref in zip(partners(len(out_refs), "back"), out_refs):
        to = here ^ k
        for r in range(reach_count):
            out_ref[r * rows : (r + 1) * rows, :] = flows_ref[to * reach_count + r]
        out_ref[reach_count * rows :, :] = extras


def gather_body(tile_ref, top_ref, *rest, wide):
    in_refs, (out_ref, base_ref) = rest[:-2], rest[-2:]
    parts = len(in_refs)
    members_dev = out_ref.shape[0]
    share = members_dev // parts
    block_len = in_refs[0].shape[1]
    here = lax.axis_index("basin")
    pieces = wide // block_len
    at_row = lax.broadcasted_iota(jnp.int32, (members_dev, block_len), 0)
    placed = [jnp.zeros((members_dev, block_len), jnp.float32)] * pieces
    for k, in_ref in zip(partners(len(in_refs), "back"), in_refs):
        extras = in_ref[in_ref.shape[0] - EXTRA :, :].astype(jnp.float32)
        middle = members_dev // 2
        base_ref[here ^ k] = top_ref[here ^ k] + jnp.concatenate(
            [extras[:middle, :LANES], extras[:middle, LANES:]], axis=0
        )
        extras = extras[middle:]
        for i in range(pieces):
            for j in range(share):
                value = sum(
                    extras[(p * pieces + i) * share + j : (p * pieces + i) * share + j + 1]
                    for p in range(3)
                )
                placed[i] = jnp.where(at_row == share * (here ^ k) + j, value, placed[i])
    for i in range(pieces):
        out_ref[:, i * block_len : (i + 1) * block_len] = placed[i]
    out_ref[:, wide:] = tile_ref[...]


def place_params(params_ref, tile_ref):
    shape_count, _, members_dev = params_ref.shape
    members = members_dev * lax.axis_size("member")
    tile_ref[...] = jnp.zeros(tile_ref.shape, jnp.float32)
    for s in range(shape_count):
        tile_ref[:, s * members : s * members + members_dev] = params_ref[s]
    tile_ref[...] = pltpu.roll(tile_ref[...], lax.axis_index("member") * members_dev, 1)


def unpack_body(*refs, parts, reach_count):
    in_refs, (out_ref, stage_ref) = refs[:parts], refs[parts:]
    members_dev = out_ref.shape[1]
    block_len = in_refs[0].shape[1]
    share = members_dev // parts
    block_count = out_ref.shape[2] // block_len
    rows = share * block_count
    here = lax.axis_index("basin")
    for k, in_ref in zip(partners(len(in_refs), "back"), in_refs):
        source = here ^ k
        for r in range(reach_count):
            piece = in_ref[r * rows : (r + 1) * rows, :].astype(jnp.float32)
            for j in range(share):
                for h in range(block_len // LANES):
                    stage_ref[
                        h,
                        pl.ds(
                            r * block_count * members_dev + share * source + j,
                            block_count,
                            stride=members_dev,
                        ),
                        :,
                    ] = piece[j * block_count : (j + 1) * block_count, h * LANES : (h + 1) * LANES]
    for r in range(reach_count):
        for i in range(block_count):
            at = (r * block_count + i) * members_dev
            for h in range(block_len // LANES):
                lane = i * block_len + h * LANES
                out_ref[r, :, lane : lane + LANES] = stage_ref[
                    h, at : at + members_dev, :
                ].astype(jnp.bfloat16)


def solve_body(base_ref, params_ref, *rest):
    in_refs, (out_ref, all_ref, right_ref) = rest[:-3], rest[-3:]
    shape_count, reach_count, members_dev = params_ref.shape
    groups = len(in_refs)
    members = groups * members_dev
    wide = all_ref.shape[1]
    here = lax.axis_index("member")
    tiles = None
    for k, in_ref in zip(partners(len(in_refs), "member"), in_refs):
        at = pl.multiple_of((here ^ k) * members_dev, members_dev)
        all_ref[pl.ds(at, members_dev), :] = in_ref[:, :wide]
        tile = in_ref[:, wide:]
        tiles = tile if tiles is None else tiles + tile
    scaled = all_ref[...]
    root = jnp.sqrt(jnp.float32(members - 1))
    spread = (scaled - jnp.mean(scaled, axis=0, keepdims=True)) / root
    own = in_refs[0][:, :wide]
    right_ref[:members, :] = spread
    for n in range(base_ref.shape[0]):
        cols = slice(n * base_ref.shape[2], (n + 1) * base_ref.shape[2])
        right_ref[members : members + members_dev, cols] = base_ref[n] - own[:, cols]
    right_ref[members + members_dev :, :] = jnp.zeros(
        (right_ref.shape[0] - members - members_dev, wide), jnp.float32
    )
    system = lax.dot_general(
        spread,
        right_ref[...],
        (((1,), (1,)), ((), ())),
        precision=HIGHEST,
        preferred_element_type=jnp.float32,
    )
    row_at = lax.broadcasted_iota(jnp.int32, system.shape, 0)
    col_at = lax.broadcasted_iota(jnp.int32, system.shape, 1)
    system = system + jnp.where(row_at == col_at, 1.0, 0.0)
    tiles_down = range(0, members, members_dev)
    system = [system[g : g + members_dev] for g in tiles_down]
    tile_row = row_at[:members_dev]
    for first in range(0, members, AHEAD):
        cols = [
            [jnp.broadcast_to(tile[:, i : i + 1], tile.shape) for tile in system]
            for i in range(first, first + AHEAD)
        ]
        for t in range(AHEAD):
            here_tile, here_row = divmod(first + t, members_dev)
            factors = cols[t]
            inverse = 1.0 / factors[here_tile][here_row : here_row + 1, :]
            own_row = tile_row == here_row

            def cleared(tiles):
                pivot_row = tiles[here_tile][here_row : here_row + 1, :] * inverse
                done = [tile - factor * pivot_row for tile, factor in zip(tiles, factors)]
                done[here_tile] = jnp.where(own_row, pivot_row, done[here_tile])
                return done

            system = cleared(system)
            for u in range(t + 1, AHEAD):
                cols[u] = cleared(cols[u])
    system = jnp.concatenate(system, axis=0)
    gain = system[:, members : members + members_dev]
    theta = jnp.concatenate(
        [tiles[:, s * members : (s + 1) * members] for s in range(shape_count)], axis=0
    )
    anomaly = theta - jnp.mean(theta, axis=1, keepdims=True)
    step = (
        jnp.dot(anomaly, gain, precision=HIGHEST, preferred_element_type=jnp.float32) / root
    )
    for s in range(shape_count):
        out_ref[s] = params_ref[s] + step[s * reach_count : (s + 1) * reach_count]


def swapped(pieces, axis, step):
    results = [pieces[0]]
    groups = lax.axis_size("member")
    for piece, *by in zip(pieces[1:], *ORDERS[step]):
        if axis == "member":
            pairs = [(m, m ^ by[m % 2]) for m in range(groups)]
            results.append(lax.ppermute(piece, axis, pairs))
        else:
            pairs = [
                (b * groups + m, (b ^ by[m % 2]) * groups + m)
                for b in range(lax.axis_size(axis))
                for m in range(groups)
            ]
            results.append(lax.ppermute(piece, (axis, "member"), pairs))
    return results


def per_device_split(
    runoff,
    route_params,
    unit_shapes,
    level_map,
    down_map,
    gauge_reach,
    gauge_sigma,
    observed,
    obs_noise,
):
    f32, bf16 = jnp.float32, jnp.bfloat16
    parts, groups = lax.axis_size("basin"), lax.axis_size("member")
    reach_count, members_dev, series_len = runoff.shape
    shape_count, block_len = unit_shapes.shape
    gauge_count = observed.shape[0]
    block_count = series_len // block_len
    share = members_dev // parts
    rows = share * block_count
    total = parts * reach_count
    cap = reach_count // 4
    wide = parts * gauge_count * WINDOWS
    members = members_dev * groups
    sent = pltpu.VMEM((reach_count * rows + reach_count, block_len), bf16)
    sent_back = pltpu.VMEM((reach_count * rows + EXTRA, block_len), bf16)
    base = pltpu.VMEM((members_dev, gauge_count * WINDOWS), f32)
    *packed, own_params, tile, own_base = pl.pallas_call(
        pack_body,
        out_shape=[sent] * parts
        + [pltpu.VMEM(route_params.shape, f32), pltpu.VMEM((reach_count, LANES), f32), base],
        in_specs=[smem()] * 4 + [vmem()] * 4,
        out_specs=[vmem()] * (parts + 3),
        scratch_shapes=[
            pltpu.VMEM((block_len // LANES, reach_count * members_dev * block_count, LANES), f32),
            pltpu.VMEM((reach_count, LANES), f32),
        ],
        name="pack",
    )(level_map, down_map, gauge_reach, gauge_sigma, runoff, route_params, observed, obs_noise)
    arrived = swapped(packed, "basin", "basin")
    conv_table, window_table = kernel_table(unit_shapes, series_len // WINDOWS, wide)
    *routed, base_top = pl.pallas_call(
        functools.partial(
            route_body,
            parts=parts,
            reach_count=reach_count,
            shape_count=shape_count,
            gauge_count=gauge_count,
            members_dev=members_dev,
        ),
        out_shape=[sent_back] * parts + [pltpu.VMEM((parts,) + base.shape, f32)],
        in_specs=[vmem()] * (3 + parts),
        out_specs=[vmem()] * (parts + 1),
        scratch_shapes=[
            pltpu.VMEM((total + 2, rows, block_len), f32),
            pltpu.VMEM((total + 1, rows, block_len), bf16),
            pltpu.VMEM((parts * max(cap, gauge_count) * rows, 2 * block_len), bf16),
            pltpu.VMEM((shape_count * share, total, LANES), f32),
            pltpu.SMEM((LEVELS * parts * cap,), jnp.int32),
        ],
        name="route",
    )(kept(conv_table), kept(window_table), kept(own_base), *map(kept, arrived))
    returned = swapped(routed, "basin", "back")
    local, noise_base = pl.pallas_call(
        functools.partial(gather_body, wide=wide),
        out_shape=[
            pltpu.VMEM((members_dev, wide + LANES), f32),
            pltpu.VMEM((parts,) + base.shape, f32),
        ],
        in_specs=[vmem()] * (2 + parts),
        out_specs=[vmem()] * 2,
        name="gather",
    )(kept(tile), kept(base_top), *map(kept, returned))
    everyone = swapped([local] * groups, "member", "member")
    flows = pl.pallas_call(
        functools.partial(unpack_body, parts=parts, reach_count=reach_count),
        out_shape=jax.ShapeDtypeStruct(runoff.shape, bf16),
        in_specs=[vmem()] * parts,
        out_specs=vmem(),
        scratch_shapes=[pltpu.VMEM((block_len // LANES, reach_count * members_dev * block_count, LANES), f32)],
        name="unpack",
    )(*map(kept, returned))
    updated = pl.pallas_call(
        solve_body,
        out_shape=jax.ShapeDtypeStruct(route_params.shape, f32),
        in_specs=[vmem()] * (2 + groups),
        out_specs=vmem(),
        scratch_shapes=[pltpu.VMEM((members, wide), f32), pltpu.VMEM((LANES, wide), f32)],
        name="solve",
    )(kept(noise_base), kept(own_params), *map(kept, everyone))
    return flows, updated


def per_device(*args):
    runoff, route_params, unit_shapes, _, _, _, _, observed, _ = args
    parts, groups = lax.axis_size("basin"), lax.axis_size("member")
    reach_count, members_dev, series_len = runoff.shape
    shape_count, block_len = unit_shapes.shape
    block_count = series_len // block_len
    gauge_count = observed.shape[0]
    wide = parts * gauge_count * WINDOWS
    share = max(members_dev // parts, 1)
    fits = (
        parts == 4
        and groups == 4
        and members_dev == share * parts
        and reach_count == 8
        and members_dev == 8
        and block_count == 8
        and series_len % block_len == 0
        and block_len == 2 * LANES
        and gauge_count * WINDOWS == LANES
        and wide % block_len == 0
        and members_dev // 2 + 3 * share * (wide // block_len) <= EXTRA
        and shape_count * members_dev + reach_count // 4 + 2 <= LANES // parts
        and 2 * reach_count < CODE
        and parts >= 2
        and reach_count == LEVELS
        and shape_count * groups * members_dev <= LANES
        and groups * members_dev + members_dev <= LANES
    )
    if fits:
        return per_device_split(*args)
    return per_device_chain(*args)


def passed_along(x, axis, by):
    length = lax.axis_size(axis)
    pairs = [(i, i + by) for i in range(length) if 0 <= i + by < length]
    return lax.ppermute(x, axis, pairs)


def route_rows(inflow_rows, slot_weights, conv_table):
    block_len = conv_table.shape[0] // 2
    row_count, series_len = inflow_rows.shape
    blocks = inflow_rows.reshape(row_count, series_len // block_len, block_len)
    earlier = jnp.concatenate([jnp.zeros_like(blocks[:, :1]), blocks[:, :-1]], axis=1)
    joined = jnp.concatenate([blocks, earlier], axis=2).reshape(-1, 2 * block_len)
    mixed_blocks = jnp.dot(joined, conv_table, preferred_element_type=jnp.float32)
    mixed_blocks = mixed_blocks.reshape(
        row_count, series_len // block_len, slot_weights.shape[1], block_len
    )
    return jnp.sum(mixed_blocks * slot_weights[:, None, :, None], axis=2).reshape(
        row_count, series_len
    )


def level_select(level_block, down_block, level_now, slot_count):
    entry_count = level_block.shape[0]
    entry_ids = jnp.arange(entry_count, dtype=jnp.int32)
    in_level = level_block == level_now
    before = (entry_ids[None, :] < entry_ids[:, None]) & in_level[None, :]
    rank = jnp.sum(before.astype(jnp.int32), axis=1)
    slot_ids = jnp.arange(slot_count, dtype=jnp.int32)
    select = (rank[None, :] == slot_ids[:, None]) & in_level[None, :]
    slot_valid = slot_ids < jnp.sum(in_level.astype(jnp.int32))
    slot_target = jnp.sum(jnp.where(select, down_block[None, :], 0), axis=1)
    return (select, slot_valid, slot_target)


def per_device_chain(
    runoff,
    route_params,
    unit_shapes,
    level_map,
    down_map,
    gauge_reach,
    gauge_sigma,
    observed,
    obs_noise,
):
    conv_table, _ = kernel_table(unit_shapes, runoff.shape[2] // WINDOWS, LANES)
    reach_count, members_dev, series_len = runoff.shape
    flat_len = members_dev * series_len
    slot_count = reach_count // 4
    shape_count = route_params.shape[0]
    inflow = runoff.astype(jnp.float32).reshape(reach_count, flat_len)
    outflow = jnp.zeros_like(inflow)
    reach_ids = jnp.arange(reach_count, dtype=jnp.int32)[:, None]
    params_rows = jnp.transpose(route_params, (1, 2, 0))
    prev_level, prev_down = passed_along((level_map, down_map), "basin", 1)
    for level_now in range(LEVELS):
        select, slot_valid, slot_target_row = level_select(
            level_map, down_map, level_now, slot_count
        )
        gathered = jnp.dot(
            select.astype(jnp.bfloat16),
            inflow.astype(jnp.bfloat16),
            preferred_element_type=jnp.float32,
        )
        gathered = gathered.astype(jnp.bfloat16).reshape(slot_count * members_dev, series_len)
        slot_weights = jnp.einsum(
            "cr,rms->cms", select.astype(jnp.float32), params_rows, precision=lax.Precision.HIGHEST
        ).reshape(-1, shape_count)
        routed = (
            route_rows(gathered, slot_weights, conv_table)
            .astype(jnp.bfloat16)
            .reshape(slot_count, flat_len)
        )
        slot_target = slot_target_row[None, :]
        slot_mask = slot_valid[None, :]
        local_edges = (slot_target == reach_ids) & slot_mask
        chosen = jnp.transpose(select) & slot_mask
        edge_matrix = jnp.concatenate([local_edges, chosen], axis=0).astype(jnp.bfloat16)
        spread_flows = jnp.dot(edge_matrix, routed, preferred_element_type=jnp.float32)
        inflow = inflow + spread_flows[:reach_count]
        outflow = outflow + spread_flows[reach_count:]
        if level_now + 1 < LEVELS:
            arrived = passed_along(routed, "basin", 1)
            prev_select, prev_valid, prev_target = level_select(
                prev_level, prev_down, level_now, slot_count
            )
            incoming = (prev_target[None, :] == reach_ids + reach_count) & prev_valid[None, :]
            inflow = inflow + jnp.dot(
                incoming.astype(jnp.bfloat16), arrived, preferred_element_type=jnp.float32
            )
    flows = outflow.astype(jnp.bfloat16)
    gauge_pick = (gauge_reach[:, None] == jnp.arange(reach_count, dtype=jnp.int32)[None, :]).astype(
        jnp.bfloat16
    )
    gauged = jnp.dot(gauge_pick, flows, preferred_element_type=jnp.float32)
    predicted = jnp.mean(gauged.reshape(-1, members_dev, WINDOWS, series_len // WINDOWS), axis=3)
    scaled = predicted / gauge_sigma[:, None, None]
    innovation = observed[:, None, :] / gauge_sigma[:, None, None] + obs_noise - scaled
    scaled = jnp.transpose(scaled, (0, 2, 1))
    innovation = jnp.transpose(innovation, (0, 2, 1))
    scaled, innovation = (
        lax.all_gather(scaled, "member", axis=2, tiled=True),
        lax.all_gather(innovation, "member", axis=2, tiled=True),
    )
    members = scaled.shape[2]
    scaled = scaled.reshape(-1, members)
    innovation = innovation.reshape(-1, members)
    spread = (scaled - jnp.mean(scaled, axis=1, keepdims=True)) / jnp.sqrt(members - 1.0)
    gram_part = jnp.dot(spread.T, spread, precision=lax.Precision.HIGHEST)
    cross_part = jnp.dot(spread.T, innovation, precision=lax.Precision.HIGHEST)
    gram_part, cross_part = lax.psum((gram_part, cross_part), "basin")
    gram = jnp.eye(members, dtype=jnp.float32) + gram_part
    factor = jnp.linalg.cholesky(gram)
    kalman_gain = jax.scipy.linalg.cho_solve((factor, True), cross_part)
    col_start = lax.axis_index("member") * members_dev
    all_params = lax.all_gather(route_params, "member", axis=2, tiled=True).reshape(-1, members)
    anomaly = all_params - jnp.mean(all_params, axis=1, keepdims=True)
    columns = lax.dynamic_slice_in_dim(kalman_gain, col_start, members_dev, 1)
    increment = jnp.dot(anomaly, columns, precision=lax.Precision.HIGHEST)
    updated = route_params.reshape(-1, members_dev) + increment / jnp.sqrt(members - 1.0)
    return (
        flows.reshape(reach_count, members_dev, series_len),
        updated.reshape(route_params.shape),
    )


def solution(mesh):
    return jax.shard_map(
        per_device,
        mesh=mesh,
        in_specs=(
            P(("groups", "basin"), "member", None),
            P(None, ("groups", "basin"), "member"),
            P(),
            P(("groups", "basin")),
            P(("groups", "basin")),
            P(("groups", "basin")),
            P(("groups", "basin")),
            P(("groups", "basin"), None),
            P(("groups", "basin"), "member", None),
        ),
        out_specs=(P(("groups", "basin"), "member", None), P(None, ("groups", "basin"), "member")),
        check_vma=False,
    )
```

```python
import functools

import jax
import jax.numpy as jnp
from jax import lax
from jax.experimental import pallas as pl
from jax.experimental.pallas import tpu as pltpu
from jax.sharding import PartitionSpec as P

LEVELS = 8
WINDOWS = 64
LANES = 128
EXTRA = 16
HIGHEST = lax.Precision.HIGHEST

def vmem():
    return pl.BlockSpec(memory_space=pltpu.VMEM)


def smem():
    return pl.BlockSpec(memory_space=pltpu.SMEM)


AHEAD = 16
CODE = 64


ORDERS = {
    "basin": ((3, 1, 2), (3, 2, 1)),
    "back": ((3, 1, 2), (2, 3, 1)),
    "member": ((1, 2, 3), (1, 2, 3)),
}


def partners(length, step):
    even, odd = ORDERS[step]
    if even == odd:
        return [0] + list(even)
    side = lax.axis_index("member") % 2
    return [0] + [jnp.where(side == 0, a, b) for a, b in zip(even, odd)]


def kept(x):
    return pltpu.with_memory_space_constraint(x, pltpu.VMEM)


def table_body(shapes_ref, table_ref, window_ref, *, span):
    shape_count, block_len = shapes_ref.shape
    for s in range(shape_count):
        lags = shapes_ref[s : s + 1, :] * (1.0 / block_len)
        lags = jnp.concatenate([lags, jnp.zeros_like(lags)], axis=1)
        skewed = pltpu.roll(
            jnp.broadcast_to(lags, (block_len, 2 * block_len)), 0, 1, stride=1, stride_axis=0
        ).astype(jnp.bfloat16)
        cols = slice(s * block_len, (s + 1) * block_len)
        table_ref[:block_len, cols] = skewed[:, :block_len]
        table_ref[block_len:, cols] = skewed[:, block_len:]
    lag_at = lax.broadcasted_iota(jnp.int32, window_ref.shape, 0)
    col_at = lax.broadcasted_iota(jnp.int32, window_ref.shape, 1)
    window_ref[...] = jnp.where(
        lag_at // span == col_at % (block_len // span), 1.0 / span, 0.0
    ).astype(jnp.bfloat16)


def kernel_table(unit_shapes, span, wide):
    shape_count, block_len = unit_shapes.shape
    return pl.pallas_call(
        functools.partial(table_body, span=span),
        out_shape=[
            pltpu.VMEM((2 * block_len, shape_count * block_len), jnp.bfloat16),
            pltpu.VMEM((block_len, wide), jnp.bfloat16),
        ],
        in_specs=[vmem()],
        out_specs=[vmem()] * 2,
        name="table",
    )(unit_shapes)


def split_two(x):
    top = x.astype(jnp.bfloat16)
    rest = x - top.astype(jnp.float32)
    mid = rest.astype(jnp.bfloat16)
    return top, mid, rest - mid.astype(jnp.float32)


def pack_body(
    level_ref,
    down_ref,
    gauge_ref,
    sigma_ref,
    runoff_ref,
    params_ref,
    observed_ref,
    noise_ref,
    *rest,
):
    out_refs, (own_ref, tile_ref, base_ref, stage_ref, extra_ref) = rest[:-5], rest[-5:]
    reach_count, members_dev, series_len = runoff_ref.shape
    shape_count = params_ref.shape[0]
    gauge_count, windows = observed_ref.shape
    block_len = out_refs[0].shape[1]
    block_count = series_len // block_len
    share = members_dev // len(out_refs)
    rows = share * block_count
    here = lax.axis_index("basin")
    for r in range(reach_count):
        series = runoff_ref[r].astype(jnp.float32)
        for i in range(block_count):
            at = (r * block_count + i) * members_dev
            for h in range(block_len // LANES):
                lane = i * block_len + h * LANES
                stage_ref[h, at : at + members_dev, :] = series[:, lane : lane + LANES]
    extra_ref[...] = jnp.zeros(extra_ref.shape, jnp.float32)
    for g in range(gauge_count):
        base_ref[:, g * windows : (g + 1) * windows] = (
            observed_ref[g : g + 1, :] / sigma_ref[g] + noise_ref[g]
        )
    for s in range(shape_count):
        extra_ref[:, s * members_dev : (s + 1) * members_dev] = params_ref[s]
    at_row = lax.broadcasted_iota(jnp.int32, (reach_count, LANES), 0)
    at_lane = lax.broadcasted_iota(jnp.int32, (reach_count, LANES), 1)
    base = shape_count * members_dev
    facts = extra_ref[...]
    cap = reach_count // 4
    facts = jnp.where(
        (at_lane >= base) & (at_lane < base + cap), jnp.float32(reach_count * CODE), facts
    )
    for r in range(reach_count):
        rank = jnp.int32(0)
        for q in range(r):
            rank = rank + (level_ref[q] == level_ref[r]).astype(jnp.int32)
        here_slot = (at_row == level_ref[r]) & (at_lane == base + rank)
        facts = jnp.where(here_slot, (down_ref[r] + r * CODE).astype(jnp.float32), facts)
    for g in range(gauge_count):
        facts = jnp.where(
            (at_row == g) & (at_lane == base + cap), gauge_ref[g].astype(jnp.float32), facts
        )
        facts = jnp.where((at_row == g) & (at_lane == base + cap + 1), sigma_ref[g], facts)
    span = LANES // len(out_refs)
    top, mid, low = split_two(facts)
    terms = (
        top.astype(jnp.float32)
        + pltpu.roll(mid.astype(jnp.float32), span, 1)
        + pltpu.roll(low, 2 * span, 1)
    )
    extras = jnp.concatenate([terms, base_ref[...]], axis=1).astype(jnp.bfloat16)
    for k, out_ref in zip(partners(len(out_refs), "basin"), out_refs):
        to = here ^ k
        for r in range(reach_count):
            for h in range(block_len // LANES):
                pieces = [
                    stage_ref[
                        h,
                        pl.ds(
                            r * block_count * members_dev + share * to + j,
                            block_count,
                            stride=members_dev,
                        ),
                        :,
                    ]
                    for j in range(share)
                ]
                out_ref[r * rows : (r + 1) * rows, h * LANES : (h + 1) * LANES] = jnp.concatenate(
                    pieces, axis=0
                ).astype(jnp.bfloat16)
        out_ref[reach_count * rows :, :] = extras
    own_ref[...] = params_ref[...]
    place_params(params_ref, tile_ref)


def route_body(
    table_ref, window_ref, own_base_ref, *rest, parts, reach_count, shape_count, gauge_count, members_dev
):
    in_refs, rest = rest[:parts], rest[parts:]
    out_refs, rest = rest[:parts], rest[parts:]
    base_ref, state_ref, flows_ref, left_ref, weight_ref, code_ref = rest
    block_len = table_ref.shape[0] // 2
    rows = state_ref.shape[1]
    share = members_dev // parts
    block_count = rows // share
    total = parts * reach_count
    cap = reach_count // 4
    here = lax.axis_index("basin")
    base = shape_count * members_dev
    span = LANES // parts
    at_lane = lax.broadcasted_iota(jnp.int32, (reach_count, LANES), 1)
    facts = jnp.zeros((reach_count, LANES), jnp.float32)
    for k, in_ref in zip(partners(len(in_refs), "basin"), in_refs):
        source = here ^ k
        extras = in_ref[reach_count * rows :, :].astype(jnp.float32)
        terms = extras[:, :LANES]
        base_ref[source] = extras[:, LANES:]
        rest_terms = pltpu.roll(terms, LANES - span, 1) + pltpu.roll(terms, LANES - 2 * span, 1)
        part = jnp.where(at_lane < span, terms + rest_terms, 0.0)
        facts = facts + pltpu.roll(part, source * span, 1)
    whole = facts.astype(jnp.int32)
    for level_now in range(LEVELS):
        for c in range(parts * cap):
            code_ref[level_now * parts * cap + c] = whole[
                level_now, (c // cap) * span + base + c % cap
            ]
    mine = pltpu.roll(facts, LANES - share * here, 1)
    for n in range(parts):
        for s in range(shape_count):
            for j in range(share):
                lane = n * span + s * members_dev + j
                weight_ref[s * share + j, n * reach_count : (n + 1) * reach_count, :] = (
                    jnp.broadcast_to(mine[:, lane : lane + 1], (reach_count, LANES))
                )
    for k, in_ref in zip(partners(len(in_refs), "basin"), in_refs):
        source = here ^ k
        for r in range(reach_count):
            state_ref[source * reach_count + r] = in_ref[r * rows : (r + 1) * rows, :].astype(
                jnp.float32
            )
    state_ref[total] = jnp.zeros(state_ref.shape[1:], jnp.float32)
    state_ref[total + 1] = jnp.zeros(state_ref.shape[1:], jnp.float32)

    first_row = lax.broadcasted_iota(jnp.int32, (block_count, block_len), 0) == 0
    slots = parts * cap

    def one_level(level_now, carry):
        picked, goals, sources = [], [], []
        for c in range(slots):
            code = code_ref[level_now * slots + c]
            reach = code // CODE
            goal = (c // cap) * reach_count + code % CODE
            real = reach < reach_count
            kept_goal = (goal < (c // cap + 2) * reach_count) & (goal < total) & real
            sources.append((c // cap) * reach_count + jnp.where(real, reach, 0))
            picked.append(jnp.where(real, (c // cap) * reach_count + reach, total))
            goals.append(jnp.where(kept_goal, goal, total + 1))
        for c in range(slots):
            rows_now = state_ref[picked[c]]
            left_ref[c * rows : (c + 1) * rows, :block_len] = rows_now.astype(jnp.bfloat16)
            earlier = [
                jnp.where(
                    first_row,
                    0.0,
                    pltpu.roll(rows_now[j * block_count : (j + 1) * block_count], 1, 0),
                )
                for j in range(share)
            ]
            left_ref[c * rows : (c + 1) * rows, block_len:] = jnp.concatenate(
                earlier, axis=0
            ).astype(jnp.bfloat16)
        left = left_ref[...]
        mixed = [
            jnp.dot(
                left,
                table_ref[:, s * block_len : (s + 1) * block_len],
                preferred_element_type=jnp.float32,
            )
            for s in range(shape_count)
        ]
        for c in range(slots):
            pieces = []
            for j in range(share):
                at = slice(c * rows + j * block_count, c * rows + (j + 1) * block_count)
                piece = None
                for s in range(shape_count):
                    weight = weight_ref[s * share + j, pl.ds(sources[c], 1), :]
                    weight = jnp.concatenate([weight] * (block_len // LANES), axis=1)
                    term = mixed[s][at] * weight
                    piece = term if piece is None else piece + term
                pieces.append(piece)
            routed = jnp.concatenate(pieces, axis=0).astype(jnp.bfloat16)
            flows_ref[picked[c]] = routed
            state_ref[goals[c]] = state_ref[goals[c]] + routed.astype(jnp.float32)
        return carry

    lax.fori_loop(0, LEVELS, one_level, 0)

    gauges = parts * gauge_count
    wide = gauges * WINDOWS
    per_block = WINDOWS // block_count
    for g in range(gauges):
        reach = (g // gauge_count) * reach_count + whole[
            g % gauge_count, (g // gauge_count) * span + base + cap
        ]
        left_ref[g * rows : (g + 1) * rows, :block_len] = flows_ref[reach]
    means = jnp.dot(
        left_ref[: gauges * rows, :block_len], window_ref[...], preferred_element_type=jnp.float32
    )
    row_at = lax.broadcasted_iota(jnp.int32, (block_count, wide), 0)
    col_at = lax.broadcasted_iota(jnp.int32, (block_count, wide), 1)
    sigma_row = jnp.zeros((1, wide), jnp.float32)
    for g in range(gauges):
        sigma = facts[g % gauge_count, (g // gauge_count) * span + base + cap + 1]
        sigma_row = jnp.where(col_at[:1] // WINDOWS == g, sigma, sigma_row)
    scaled = []
    for j in range(share):
        merged = jnp.zeros((block_count, wide), jnp.float32)
        for g in range(gauges):
            at = g * rows + j * block_count
            merged = jnp.where(
                (col_at // per_block) == g * block_count + row_at,
                means[at : at + block_count],
                merged,
            )
        scaled.append(jnp.sum(merged, axis=0, keepdims=True) / sigma_row)
    scaled = jnp.concatenate(scaled, axis=0)
    top, mid, low = split_two(scaled)
    _, base_mid, _ = split_two(own_base_ref[...])
    base_mid = base_mid.astype(jnp.float32)
    middle = members_dev // 2
    chunks = [jnp.concatenate([base_mid[:middle], base_mid[middle:]], axis=1)]
    for part in (top.astype(jnp.float32), mid.astype(jnp.float32), low):
        chunks += [part[:, i * block_len : (i + 1) * block_len] for i in range(wide // block_len)]
    used = middle + (len(chunks) - 1) * share
    if used < EXTRA:
        chunks.append(jnp.zeros((EXTRA - used, block_len), jnp.float32))
    extras = jnp.concatenate(chunks, axis=0).astype(jnp.bfloat16)
    for k, out_ref in zip(partners(len(out_refs), "back"), out_refs):
        to = here ^ k
        for r in range(reach_count):
            out_ref[r * rows : (r + 1) * rows, :] = flows_ref[to * reach_count + r]
        out_ref[reach_count * rows :, :] = extras


def gather_body(tile_ref, top_ref, *rest, wide):
    in_refs, (out_ref, base_ref) = rest[:-2], rest[-2:]
    parts = len(in_refs)
    members_dev = out_ref.shape[0]
    share = members_dev // parts
    block_len = in_refs[0].shape[1]
    here = lax.axis_index("basin")
    pieces = wide // block_len
    at_row = lax.broadcasted_iota(jnp.int32, (members_dev, block_len), 0)
    placed = [jnp.zeros((members_dev, block_len), jnp.float32)] * pieces
    for k, in_ref in zip(partners(len(in_refs), "back"), in_refs):
        extras = in_ref[in_ref.shape[0] - EXTRA :, :].astype(jnp.float32)
        middle = members_dev // 2
        base_ref[here ^ k] = top_ref[here ^ k] + jnp.concatenate(
            [extras[:middle, :LANES], extras[:middle, LANES:]], axis=0
        )
        extras = extras[middle:]
        for i in range(pieces):
            for j in range(share):
                value = sum(
                    extras[(p * pieces + i) * share + j : (p * pieces + i) * share + j + 1]
                    for p in range(3)
                )
                placed[i] = jnp.where(at_row == share * (here ^ k) + j, value, placed[i])
    for i in range(pieces):
        out_ref[:, i * block_len : (i + 1) * block_len] = placed[i]
    out_ref[:, wide:] = tile_ref[...]


def place_params(params_ref, tile_ref):
    shape_count, _, members_dev = params_ref.shape
    members = members_dev * lax.axis_size("member")
    tile_ref[...] = jnp.zeros(tile_ref.shape, jnp.float32)
    for s in range(shape_count):
        tile_ref[:, s * members : s * members + members_dev] = params_ref[s]
    tile_ref[...] = pltpu.roll(tile_ref[...], lax.axis_index("member") * members_dev, 1)


def unpack_body(*refs, parts, reach_count):
    in_refs, (out_ref, stage_ref) = refs[:parts], refs[parts:]
    members_dev = out_ref.shape[1]
    block_len = in_refs[0].shape[1]
    share = members_dev // parts
    block_count = out_ref.shape[2] // block_len
    rows = share * block_count
    here = lax.axis_index("basin")
    for k, in_ref in zip(partners(len(in_refs), "back"), in_refs):
        source = here ^ k
        for r in range(reach_count):
            piece = in_ref[r * rows : (r + 1) * rows, :].astype(jnp.float32)
            for j in range(share):
                for h in range(block_len // LANES):
                    stage_ref[
                        h,
                        pl.ds(
                            r * block_count * members_dev + share * source + j,
                            block_count,
                            stride=members_dev,
                        ),
                        :,
                    ] = piece[j * block_count : (j + 1) * block_count, h * LANES : (h + 1) * LANES]
    for r in range(reach_count):
        for i in range(block_count):
            at = (r * block_count + i) * members_dev
            for h in range(block_len // LANES):
                lane = i * block_len + h * LANES
                out_ref[r, :, lane : lane + LANES] = stage_ref[
                    h, at : at + members_dev, :
                ].astype(jnp.bfloat16)


def solve_body(base_ref, params_ref, *rest):
    in_refs, (out_ref, all_ref, right_ref) = rest[:-3], rest[-3:]
    shape_count, reach_count, members_dev = params_ref.shape
    groups = len(in_refs)
    members = groups * members_dev
    wide = all_ref.shape[1]
    here = lax.axis_index("member")
    tiles = None
    for k, in_ref in zip(partners(len(in_refs), "member"), in_refs):
        at = pl.multiple_of((here ^ k) * members_dev, members_dev)
        all_ref[pl.ds(at, members_dev), :] = in_ref[:, :wide]
        tile = in_ref[:, wide:]
        tiles = tile if tiles is None else tiles + tile
    scaled = all_ref[...]
    root = jnp.sqrt(jnp.float32(members - 1))
    spread = (scaled - jnp.mean(scaled, axis=0, keepdims=True)) / root
    own = in_refs[0][:, :wide]
    right_ref[:members, :] = spread
    for n in range(base_ref.shape[0]):
        cols = slice(n * base_ref.shape[2], (n + 1) * base_ref.shape[2])
        right_ref[members : members + members_dev, cols] = base_ref[n] - own[:, cols]
    right_ref[members + members_dev :, :] = jnp.zeros(
        (right_ref.shape[0] - members - members_dev, wide), jnp.float32
    )
    system = lax.dot_general(
        spread,
        right_ref[...],
        (((1,), (1,)), ((), ())),
        precision=HIGHEST,
        preferred_element_type=jnp.float32,
    )
    row_at = lax.broadcasted_iota(jnp.int32, system.shape, 0)
    col_at = lax.broadcasted_iota(jnp.int32, system.shape, 1)
    system = system + jnp.where(row_at == col_at, 1.0, 0.0)
    tiles_down = range(0, members, members_dev)
    system = [system[g : g + members_dev] for g in tiles_down]
    tile_row = row_at[:members_dev]
    for first in range(0, members, AHEAD):
        cols = [
            [jnp.broadcast_to(tile[:, i : i + 1], tile.shape) for tile in system]
            for i in range(first, first + AHEAD)
        ]
        for t in range(AHEAD):
            here_tile, here_row = divmod(first + t, members_dev)
            factors = cols[t]
            inverse = 1.0 / factors[here_tile][here_row : here_row + 1, :]
            own_row = tile_row == here_row

            def cleared(tiles):
                pivot_row = tiles[here_tile][here_row : here_row + 1, :] * inverse
                done = [tile - factor * pivot_row for tile, factor in zip(tiles, factors)]
                done[here_tile] = jnp.where(own_row, pivot_row, done[here_tile])
                return done

            system = cleared(system)
            for u in range(t + 1, AHEAD):
                cols[u] = cleared(cols[u])
    system = jnp.concatenate(system, axis=0)
    gain = system[:, members : members + members_dev]
    theta = jnp.concatenate(
        [tiles[:, s * members : (s + 1) * members] for s in range(shape_count)], axis=0
    )
    anomaly = theta - jnp.mean(theta, axis=1, keepdims=True)
    step = (
        jnp.dot(anomaly, gain, precision=HIGHEST, preferred_element_type=jnp.float32) / root
    )
    for s in range(shape_count):
        out_ref[s] = params_ref[s] + step[s * reach_count : (s + 1) * reach_count]


def swapped(pieces, axis, step):
    results = [pieces[0]]
    groups = lax.axis_size("member")
    for piece, *by in zip(pieces[1:], *ORDERS[step]):
        if axis == "member":
            pairs = [(m, m ^ by[m % 2]) for m in range(groups)]
            results.append(lax.ppermute(piece, axis, pairs))
        else:
            pairs = [
                (b * groups + m, (b ^ by[m % 2]) * groups + m)
                for b in range(lax.axis_size(axis))
                for m in range(groups)
            ]
            results.append(lax.ppermute(piece, (axis, "member"), pairs))
    return results


def per_device_split(
    runoff,
    route_params,
    unit_shapes,
    level_map,
    down_map,
    gauge_reach,
    gauge_sigma,
    observed,
    obs_noise,
):
    f32, bf16 = jnp.float32, jnp.bfloat16
    parts, groups = lax.axis_size("basin"), lax.axis_size("member")
    reach_count, members_dev, series_len = runoff.shape
    shape_count, block_len = unit_shapes.shape
    gauge_count = observed.shape[0]
    block_count = series_len // block_len
    share = members_dev // parts
    rows = share * block_count
    total = parts * reach_count
    cap = reach_count // 4
    wide = parts * gauge_count * WINDOWS
    members = members_dev * groups
    sent = pltpu.VMEM((reach_count * rows + reach_count, block_len), bf16)
    sent_back = pltpu.VMEM((reach_count * rows + EXTRA, block_len), bf16)
    base = pltpu.VMEM((members_dev, gauge_count * WINDOWS), f32)
    *packed, own_params, tile, own_base = pl.pallas_call(
        pack_body,
        out_shape=[sent] * parts
        + [pltpu.VMEM(route_params.shape, f32), pltpu.VMEM((reach_count, LANES), f32), base],
        in_specs=[smem()] * 4 + [vmem()] * 4,
        out_specs=[vmem()] * (parts + 3),
        scratch_shapes=[
            pltpu.VMEM((block_len // LANES, reach_count * members_dev * block_count, LANES), f32),
            pltpu.VMEM((reach_count, LANES), f32),
        ],
        name="pack",
    )(level_map, down_map, gauge_reach, gauge_sigma, runoff, route_params, observed, obs_noise)
    arrived = swapped(packed, "basin", "basin")
    conv_table, window_table = kernel_table(unit_shapes, series_len // WINDOWS, wide)
    *routed, base_top = pl.pallas_call(
        functools.partial(
            route_body,
            parts=parts,
            reach_count=reach_count,
            shape_count=shape_count,
            gauge_count=gauge_count,
            members_dev=members_dev,
        ),
        out_shape=[sent_back] * parts + [pltpu.VMEM((parts,) + base.shape, f32)],
        in_specs=[vmem()] * (3 + parts),
        out_specs=[vmem()] * (parts + 1),
        scratch_shapes=[
            pltpu.VMEM((total + 2, rows, block_len), f32),
            pltpu.VMEM((total + 1, rows, block_len), bf16),
            pltpu.VMEM((parts * max(cap, gauge_count) * rows, 2 * block_len), bf16),
            pltpu.VMEM((shape_count * share, total, LANES), f32),
            pltpu.SMEM((LEVELS * parts * cap,), jnp.int32),
        ],
        name="route",
    )(kept(conv_table), kept(window_table), kept(own_base), *map(kept, arrived))
    returned = swapped(routed, "basin", "back")
    local, noise_base = pl.pallas_call(
        functools.partial(gather_body, wide=wide),
        out_shape=[
            pltpu.VMEM((members_dev, wide + LANES), f32),
            pltpu.VMEM((parts,) + base.shape, f32),
        ],
        in_specs=[vmem()] * (2 + parts),
        out_specs=[vmem()] * 2,
        name="gather",
    )(kept(tile), kept(base_top), *map(kept, returned))
    everyone = swapped([local] * groups, "member", "member")
    flows = pl.pallas_call(
        functools.partial(unpack_body, parts=parts, reach_count=reach_count),
        out_shape=jax.ShapeDtypeStruct(runoff.shape, bf16),
        in_specs=[vmem()] * parts,
        out_specs=vmem(),
        scratch_shapes=[pltpu.VMEM((block_len // LANES, reach_count * members_dev * block_count, LANES), f32)],
        name="unpack",
    )(*map(kept, returned))
    updated = pl.pallas_call(
        solve_body,
        out_shape=jax.ShapeDtypeStruct(route_params.shape, f32),
        in_specs=[vmem()] * (2 + groups),
        out_specs=vmem(),
        scratch_shapes=[pltpu.VMEM((members, wide), f32), pltpu.VMEM((LANES, wide), f32)],
        name="solve",
    )(kept(noise_base), kept(own_params), *map(kept, everyone))
    return flows, updated


def per_device(*args):
    runoff, route_params, unit_shapes, _, _, _, _, observed, _ = args
    parts, groups = lax.axis_size("basin"), lax.axis_size("member")
    reach_count, members_dev, series_len = runoff.shape
    shape_count, block_len = unit_shapes.shape
    block_count = series_len // block_len
    gauge_count = observed.shape[0]
    wide = parts * gauge_count * WINDOWS
    share = max(members_dev // parts, 1)
    fits = (
        parts == 4
        and groups == 4
        and members_dev == share * parts
        and reach_count == 8
        and members_dev == 8
        and block_count == 8
        and series_len % block_len == 0
        and block_len == 2 * LANES
        and gauge_count * WINDOWS == LANES
        and wide % block_len == 0
        and members_dev // 2 + 3 * share * (wide // block_len) <= EXTRA
        and shape_count * members_dev + reach_count // 4 + 2 <= LANES // parts
        and 2 * reach_count < CODE
        and parts >= 2
        and reach_count == LEVELS
        and shape_count * groups * members_dev <= LANES
        and groups * members_dev + members_dev <= LANES
    )
    if fits:
        return per_device_split(*args)
    return per_device_chain(*args)


def passed_along(x, axis, by):
    length = lax.axis_size(axis)
    pairs = [(i, i + by) for i in range(length) if 0 <= i + by < length]
    return lax.ppermute(x, axis, pairs)


def route_rows(inflow_rows, slot_weights, conv_table):
    block_len = conv_table.shape[0] // 2
    row_count, series_len = inflow_rows.shape
    blocks = inflow_rows.reshape(row_count, series_len // block_len, block_len)
    earlier = jnp.concatenate([jnp.zeros_like(blocks[:, :1]), blocks[:, :-1]], axis=1)
    joined = jnp.concatenate([blocks, earlier], axis=2).reshape(-1, 2 * block_len)
    mixed_blocks = jnp.dot(joined, conv_table, preferred_element_type=jnp.float32)
    mixed_blocks = mixed_blocks.reshape(
        row_count, series_len // block_len, slot_weights.shape[1], block_len
    )
    return jnp.sum(mixed_blocks * slot_weights[:, None, :, None], axis=2).reshape(
        row_count, series_len
    )


def level_select(level_block, down_block, level_now, slot_count):
    entry_count = level_block.shape[0]
    entry_ids = jnp.arange(entry_count, dtype=jnp.int32)
    in_level = level_block == level_now
    before = (entry_ids[None, :] < entry_ids[:, None]) & in_level[None, :]
    rank = jnp.sum(before.astype(jnp.int32), axis=1)
    slot_ids = jnp.arange(slot_count, dtype=jnp.int32)
    select = (rank[None, :] == slot_ids[:, None]) & in_level[None, :]
    slot_valid = slot_ids < jnp.sum(in_level.astype(jnp.int32))
    slot_target = jnp.sum(jnp.where(select, down_block[None, :], 0), axis=1)
    return (select, slot_valid, slot_target)


def per_device_chain(
    runoff,
    route_params,
    unit_shapes,
    level_map,
    down_map,
    gauge_reach,
    gauge_sigma,
    observed,
    obs_noise,
):
    conv_table, _ = kernel_table(unit_shapes, runoff.shape[2] // WINDOWS, LANES)
    reach_count, members_dev, series_len = runoff.shape
    flat_len = members_dev * series_len
    slot_count = reach_count // 4
    shape_count = route_params.shape[0]
    inflow = runoff.astype(jnp.float32).reshape(reach_count, flat_len)
    outflow = jnp.zeros_like(inflow)
    reach_ids = jnp.arange(reach_count, dtype=jnp.int32)[:, None]
    params_rows = jnp.transpose(route_params, (1, 2, 0))
    prev_level, prev_down = passed_along((level_map, down_map), "basin", 1)
    for level_now in range(LEVELS):
        select, slot_valid, slot_target_row = level_select(
            level_map, down_map, level_now, slot_count
        )
        gathered = jnp.dot(
            select.astype(jnp.bfloat16),
            inflow.astype(jnp.bfloat16),
            preferred_element_type=jnp.float32,
        )
        gathered = gathered.astype(jnp.bfloat16).reshape(slot_count * members_dev, series_len)
        slot_weights = jnp.einsum(
            "cr,rms->cms", select.astype(jnp.float32), params_rows, precision=lax.Precision.HIGHEST
        ).reshape(-1, shape_count)
        routed = (
            route_rows(gathered, slot_weights, conv_table)
            .astype(jnp.bfloat16)
            .reshape(slot_count, flat_len)
        )
        slot_target = slot_target_row[None, :]
        slot_mask = slot_valid[None, :]
        local_edges = (slot_target == reach_ids) & slot_mask
        chosen = jnp.transpose(select) & slot_mask
        edge_matrix = jnp.concatenate([local_edges, chosen], axis=0).astype(jnp.bfloat16)
        spread_flows = jnp.dot(edge_matrix, routed, preferred_element_type=jnp.float32)
        inflow = inflow + spread_flows[:reach_count]
        outflow = outflow + spread_flows[reach_count:]
        if level_now + 1 < LEVELS:
            arrived = passed_along(routed, "basin", 1)
            prev_select, prev_valid, prev_target = level_select(
                prev_level, prev_down, level_now, slot_count
            )
            incoming = (prev_target[None, :] == reach_ids + reach_count) & prev_valid[None, :]
            inflow = inflow + jnp.dot(
                incoming.astype(jnp.bfloat16), arrived, preferred_element_type=jnp.float32
            )
    flows = outflow.astype(jnp.bfloat16)
    gauge_pick = (gauge_reach[:, None] == jnp.arange(reach_count, dtype=jnp.int32)[None, :]).astype(
        jnp.bfloat16
    )
    gauged = jnp.dot(gauge_pick, flows, preferred_element_type=jnp.float32)
    predicted = jnp.mean(gauged.reshape(-1, members_dev, WINDOWS, series_len // WINDOWS), axis=3)
    scaled = predicted / gauge_sigma[:, None, None]
    innovation = observed[:, None, :] / gauge_sigma[:, None, None] + obs_noise - scaled
    scaled = jnp.transpose(scaled, (0, 2, 1))
    innovation = jnp.transpose(innovation, (0, 2, 1))
    scaled, innovation = (
        lax.all_gather(scaled, "member", axis=2, tiled=True),
        lax.all_gather(innovation, "member", axis=2, tiled=True),
    )
    members = scaled.shape[2]
    scaled = scaled.reshape(-1, members)
    innovation = innovation.reshape(-1, members)
    spread = (scaled - jnp.mean(scaled, axis=1, keepdims=True)) / jnp.sqrt(members - 1.0)
    gram_part = jnp.dot(spread.T, spread, precision=lax.Precision.HIGHEST)
    cross_part = jnp.dot(spread.T, innovation, precision=lax.Precision.HIGHEST)
    gram_part, cross_part = lax.psum((gram_part, cross_part), "basin")
    gram = jnp.eye(members, dtype=jnp.float32) + gram_part
    factor = jnp.linalg.cholesky(gram)
    kalman_gain = jax.scipy.linalg.cho_solve((factor, True), cross_part)
    col_start = lax.axis_index("member") * members_dev
    all_params = lax.all_gather(route_params, "member", axis=2, tiled=True).reshape(-1, members)
    anomaly = all_params - jnp.mean(all_params, axis=1, keepdims=True)
    columns = lax.dynamic_slice_in_dim(kalman_gain, col_start, members_dev, 1)
    increment = jnp.dot(anomaly, columns, precision=lax.Precision.HIGHEST)
    updated = route_params.reshape(-1, members_dev) + increment / jnp.sqrt(members - 1.0)
    return (
        flows.reshape(reach_count, members_dev, series_len),
        updated.reshape(route_params.shape),
    )


def solution(mesh):
    return jax.shard_map(
        per_device,
        mesh=mesh,
        in_specs=(
            P(("groups", "basin"), "member", None),
            P(None, ("groups", "basin"), "member"),
            P(),
            P(("groups", "basin")),
            P(("groups", "basin")),
            P(("groups", "basin")),
            P(("groups", "basin")),
            P(("groups", "basin"), None),
            P(("groups", "basin"), "member", None),
        ),
        out_specs=(P(("groups", "basin"), "member", None), P(None, ("groups", "basin"), "member")),
        check_vma=False,
    )
```

```python
import functools

import jax
import jax.numpy as jnp
from jax import lax
from jax.experimental import pallas as pl
from jax.experimental.pallas import tpu as pltpu
from jax.sharding import PartitionSpec as P

LEVELS = 8
WINDOWS = 64
LANES = 128
EXTRA = 16
HIGHEST = lax.Precision.HIGHEST

def vmem():
    return pl.BlockSpec(memory_space=pltpu.VMEM)


def smem():
    return pl.BlockSpec(memory_space=pltpu.SMEM)


AHEAD = 16
CODE = 64


ORDERS = {
    "basin": ((3, 1, 2), (3, 2, 1)),
    "back": ((3, 1, 2), (2, 3, 1)),
    "member": ((1, 2, 3), (1, 2, 3)),
}


def partners(length, step):
    even, odd = ORDERS[step]
    if even == odd:
        return [0] + list(even)
    side = lax.axis_index("member") % 2
    return [0] + [jnp.where(side == 0, a, b) for a, b in zip(even, odd)]


def kept(x):
    return pltpu.with_memory_space_constraint(x, pltpu.VMEM)


def table_body(shapes_ref, table_ref, window_ref, *, span):
    shape_count, block_len = shapes_ref.shape
    for s in range(shape_count):
        lags = shapes_ref[s : s + 1, :] * (1.0 / block_len)
        lags = jnp.concatenate([lags, jnp.zeros_like(lags)], axis=1)
        skewed = pltpu.roll(
            jnp.broadcast_to(lags, (block_len, 2 * block_len)), 0, 1, stride=1, stride_axis=0
        ).astype(jnp.bfloat16)
        cols = slice(s * block_len, (s + 1) * block_len)
        table_ref[:block_len, cols] = skewed[:, :block_len]
        table_ref[block_len:, cols] = skewed[:, block_len:]
    lag_at = lax.broadcasted_iota(jnp.int32, window_ref.shape, 0)
    col_at = lax.broadcasted_iota(jnp.int32, window_ref.shape, 1)
    window_ref[...] = jnp.where(
        lag_at // span == col_at % (block_len // span), 1.0 / span, 0.0
    ).astype(jnp.bfloat16)


def kernel_table(unit_shapes, span, wide):
    shape_count, block_len = unit_shapes.shape
    return pl.pallas_call(
        functools.partial(table_body, span=span),
        out_shape=[
            pltpu.VMEM((2 * block_len, shape_count * block_len), jnp.bfloat16),
            pltpu.VMEM((block_len, wide), jnp.bfloat16),
        ],
        in_specs=[vmem()],
        out_specs=[vmem()] * 2,
        name="table",
    )(unit_shapes)


def split_two(x):
    top = x.astype(jnp.bfloat16)
    rest = x - top.astype(jnp.float32)
    mid = rest.astype(jnp.bfloat16)
    return top, mid, rest - mid.astype(jnp.float32)


def pack_body(
    level_ref,
    down_ref,
    gauge_ref,
    sigma_ref,
    runoff_ref,
    params_ref,
    observed_ref,
    noise_ref,
    *rest,
):
    out_refs, (own_ref, tile_ref, base_ref, stage_ref, extra_ref) = rest[:-5], rest[-5:]
    reach_count, members_dev, series_len = runoff_ref.shape
    shape_count = params_ref.shape[0]
    gauge_count, windows = observed_ref.shape
    block_len = out_refs[0].shape[1]
    block_count = series_len // block_len
    share = members_dev // len(out_refs)
    rows = share * block_count
    here = lax.axis_index("basin")
    for r in range(reach_count):
        series = runoff_ref[r].astype(jnp.float32)
        for i in range(block_count):
            at = (r * block_count + i) * members_dev
            for h in range(block_len // LANES):
                lane = i * block_len + h * LANES
                stage_ref[h, at : at + members_dev, :] = series[:, lane : lane + LANES]
    extra_ref[...] = jnp.zeros(extra_ref.shape, jnp.float32)
    for g in range(gauge_count):
        base_ref[:, g * windows : (g + 1) * windows] = (
            observed_ref[g : g + 1, :] / sigma_ref[g] + noise_ref[g]
        )
    for s in range(shape_count):
        extra_ref[:, s * members_dev : (s + 1) * members_dev] = params_ref[s]
    at_row = lax.broadcasted_iota(jnp.int32, (reach_count, LANES), 0)
    at_lane = lax.broadcasted_iota(jnp.int32, (reach_count, LANES), 1)
    base = shape_count * members_dev
    facts = extra_ref[...]
    cap = reach_count // 4
    facts = jnp.where(
        (at_lane >= base) & (at_lane < base + cap), jnp.float32(reach_count * CODE), facts
    )
    for r in range(reach_count):
        rank = jnp.int32(0)
        for q in range(r):
            rank = rank + (level_ref[q] == level_ref[r]).astype(jnp.int32)
        here_slot = (at_row == level_ref[r]) & (at_lane == base + rank)
        facts = jnp.where(here_slot, (down_ref[r] + r * CODE).astype(jnp.float32), facts)
    for g in range(gauge_count):
        facts = jnp.where(
            (at_row == g) & (at_lane == base + cap), gauge_ref[g].astype(jnp.float32), facts
        )
        facts = jnp.where((at_row == g) & (at_lane == base + cap + 1), sigma_ref[g], facts)
    span = LANES // len(out_refs)
    top, mid, low = split_two(facts)
    terms = (
        top.astype(jnp.float32)
        + pltpu.roll(mid.astype(jnp.float32), span, 1)
        + pltpu.roll(low, 2 * span, 1)
    )
    extras = jnp.concatenate([terms, base_ref[...]], axis=1).astype(jnp.bfloat16)
    for k, out_ref in zip(partners(len(out_refs), "basin"), out_refs):
        to = here ^ k
        for r in range(reach_count):
            for h in range(block_len // LANES):
                pieces = [
                    stage_ref[
                        h,
                        pl.ds(
                            r * block_count * members_dev + share * to + j,
                            block_count,
                            stride=members_dev,
                        ),
                        :,
                    ]
                    for j in range(share)
                ]
                out_ref[r * rows : (r + 1) * rows, h * LANES : (h + 1) * LANES] = jnp.concatenate(
                    pieces, axis=0
                ).astype(jnp.bfloat16)
        out_ref[reach_count * rows :, :] = extras
    own_ref[...] = params_ref[...]
    place_params(params_ref, tile_ref)


def route_body(
    table_ref, window_ref, own_base_ref, *rest, parts, reach_count, shape_count, gauge_count, members_dev
):
    in_refs, rest = rest[:parts], rest[parts:]
    out_refs, rest = rest[:parts], rest[parts:]
    base_ref, state_ref, flows_ref, left_ref, weight_ref, code_ref = rest
    block_len = table_ref.shape[0] // 2
    rows = state_ref.shape[1]
    share = members_dev // parts
    block_count = rows // share
    total = parts * reach_count
    cap = reach_count // 4
    here = lax.axis_index("basin")
    base = shape_count * members_dev
    span = LANES // parts
    at_lane = lax.broadcasted_iota(jnp.int32, (reach_count, LANES), 1)
    facts = jnp.zeros((reach_count, LANES), jnp.float32)
    for k, in_ref in zip(partners(len(in_refs), "basin"), in_refs):
        source = here ^ k
        extras = in_ref[reach_count * rows :, :].astype(jnp.float32)
        terms = extras[:, :LANES]
        base_ref[source] = extras[:, LANES:]
        rest_terms = pltpu.roll(terms, LANES - span, 1) + pltpu.roll(terms, LANES - 2 * span, 1)
        part = jnp.where(at_lane < span, terms + rest_terms, 0.0)
        facts = facts + pltpu.roll(part, source * span, 1)
    whole = facts.astype(jnp.int32)
    for level_now in range(LEVELS):
        for c in range(parts * cap):
            code_ref[level_now * parts * cap + c] = whole[
                level_now, (c // cap) * span + base + c % cap
            ]
    mine = pltpu.roll(facts, LANES - share * here, 1)
    for n in range(parts):
        for s in range(shape_count):
            for j in range(share):
                lane = n * span + s * members_dev + j
                weight_ref[s * share + j, n * reach_count : (n + 1) * reach_count, :] = (
                    jnp.broadcast_to(mine[:, lane : lane + 1], (reach_count, LANES))
                )
    for k, in_ref in zip(partners(len(in_refs), "basin"), in_refs):
        source = here ^ k
        for r in range(reach_count):
            state_ref[source * reach_count + r] = in_ref[r * rows : (r + 1) * rows, :].astype(
                jnp.float32
            )
    state_ref[total] = jnp.zeros(state_ref.shape[1:], jnp.float32)
    state_ref[total + 1] = jnp.zeros(state_ref.shape[1:], jnp.float32)

    first_row = lax.broadcasted_iota(jnp.int32, (block_count, block_len), 0) == 0
    slots = parts * cap

    def one_level(level_now, carry):
        picked, goals, sources = [], [], []
        for c in range(slots):
            code = code_ref[level_now * slots + c]
            reach = code // CODE
            goal = (c // cap) * reach_count + code % CODE
            real = reach < reach_count
            kept_goal = (goal < (c // cap + 2) * reach_count) & (goal < total) & real
            sources.append((c // cap) * reach_count + jnp.where(real, reach, 0))
            picked.append(jnp.where(real, (c // cap) * reach_count + reach, total))
            goals.append(jnp.where(kept_goal, goal, total + 1))
        for c in range(slots):
            rows_now = state_ref[picked[c]]
            left_ref[c * rows : (c + 1) * rows, :block_len] = rows_now.astype(jnp.bfloat16)
            earlier = [
                jnp.where(
                    first_row,
                    0.0,
                    pltpu.roll(rows_now[j * block_count : (j + 1) * block_count], 1, 0),
                )
                for j in range(share)
            ]
            left_ref[c * rows : (c + 1) * rows, block_len:] = jnp.concatenate(
                earlier, axis=0
            ).astype(jnp.bfloat16)
        left = left_ref[...]
        mixed = [
            jnp.dot(
                left,
                table_ref[:, s * block_len : (s + 1) * block_len],
                preferred_element_type=jnp.float32,
            )
            for s in range(shape_count)
        ]
        for c in range(slots):
            pieces = []
            for j in range(share):
                at = slice(c * rows + j * block_count, c * rows + (j + 1) * block_count)
                piece = None
                for s in range(shape_count):
                    weight = weight_ref[s * share + j, pl.ds(sources[c], 1), :]
                    weight = jnp.concatenate([weight] * (block_len // LANES), axis=1)
                    term = mixed[s][at] * weight
                    piece = term if piece is None else piece + term
                pieces.append(piece)
            routed = jnp.concatenate(pieces, axis=0).astype(jnp.bfloat16)
            flows_ref[picked[c]] = routed
            state_ref[goals[c]] = state_ref[goals[c]] + routed.astype(jnp.float32)
        return carry

    lax.fori_loop(0, LEVELS, one_level, 0, unroll=True)

    gauges = parts * gauge_count
    wide = gauges * WINDOWS
    per_block = WINDOWS // block_count
    for g in range(gauges):
        reach = (g // gauge_count) * reach_count + whole[
            g % gauge_count, (g // gauge_count) * span + base + cap
        ]
        left_ref[g * rows : (g + 1) * rows, :block_len] = flows_ref[reach]
    means = jnp.dot(
        left_ref[: gauges * rows, :block_len], window_ref[...], preferred_element_type=jnp.float32
    )
    row_at = lax.broadcasted_iota(jnp.int32, (block_count, wide), 0)
    col_at = lax.broadcasted_iota(jnp.int32, (block_count, wide), 1)
    sigma_row = jnp.zeros((1, wide), jnp.float32)
    for g in range(gauges):
        sigma = facts[g % gauge_count, (g // gauge_count) * span + base + cap + 1]
        sigma_row = jnp.where(col_at[:1] // WINDOWS == g, sigma, sigma_row)
    scaled = []
    for j in range(share):
        merged = jnp.zeros((block_count, wide), jnp.float32)
        for g in range(gauges):
            at = g * rows + j * block_count
            merged = jnp.where(
                (col_at // per_block) == g * block_count + row_at,
                means[at : at + block_count],
                merged,
            )
        scaled.append(jnp.sum(merged, axis=0, keepdims=True) / sigma_row)
    scaled = jnp.concatenate(scaled, axis=0)
    top, mid, low = split_two(scaled)
    _, base_mid, _ = split_two(own_base_ref[...])
    base_mid = base_mid.astype(jnp.float32)
    middle = members_dev // 2
    chunks = [jnp.concatenate([base_mid[:middle], base_mid[middle:]], axis=1)]
    for part in (top.astype(jnp.float32), mid.astype(jnp.float32), low):
        chunks += [part[:, i * block_len : (i + 1) * block_len] for i in range(wide // block_len)]
    used = middle + (len(chunks) - 1) * share
    if used < EXTRA:
        chunks.append(jnp.zeros((EXTRA - used, block_len), jnp.float32))
    extras = jnp.concatenate(chunks, axis=0).astype(jnp.bfloat16)
    for k, out_ref in zip(partners(len(out_refs), "back"), out_refs):
        to = here ^ k
        for r in range(reach_count):
            out_ref[r * rows : (r + 1) * rows, :] = flows_ref[to * reach_count + r]
        out_ref[reach_count * rows :, :] = extras


def gather_body(tile_ref, top_ref, *rest, wide):
    in_refs, (out_ref, base_ref) = rest[:-2], rest[-2:]
    parts = len(in_refs)
    members_dev = out_ref.shape[0]
    share = members_dev // parts
    block_len = in_refs[0].shape[1]
    here = lax.axis_index("basin")
    pieces = wide // block_len
    at_row = lax.broadcasted_iota(jnp.int32, (members_dev, block_len), 0)
    placed = [jnp.zeros((members_dev, block_len), jnp.float32)] * pieces
    for k, in_ref in zip(partners(len(in_refs), "back"), in_refs):
        extras = in_ref[in_ref.shape[0] - EXTRA :, :].astype(jnp.float32)
        middle = members_dev // 2
        base_ref[here ^ k] = top_ref[here ^ k] + jnp.concatenate(
            [extras[:middle, :LANES], extras[:middle, LANES:]], axis=0
        )
        extras = extras[middle:]
        for i in range(pieces):
            for j in range(share):
                value = sum(
                    extras[(p * pieces + i) * share + j : (p * pieces + i) * share + j + 1]
                    for p in range(3)
                )
                placed[i] = jnp.where(at_row == share * (here ^ k) + j, value, placed[i])
    for i in range(pieces):
        out_ref[:, i * block_len : (i + 1) * block_len] = placed[i]
    out_ref[:, wide:] = tile_ref[...]


def place_params(params_ref, tile_ref):
    shape_count, _, members_dev = params_ref.shape
    members = members_dev * lax.axis_size("member")
    tile_ref[...] = jnp.zeros(tile_ref.shape, jnp.float32)
    for s in range(shape_count):
        tile_ref[:, s * members : s * members + members_dev] = params_ref[s]
    tile_ref[...] = pltpu.roll(tile_ref[...], lax.axis_index("member") * members_dev, 1)


def unpack_body(*refs, parts, reach_count):
    in_refs, (out_ref, stage_ref) = refs[:parts], refs[parts:]
    members_dev = out_ref.shape[1]
    block_len = in_refs[0].shape[1]
    share = members_dev // parts
    block_count = out_ref.shape[2] // block_len
    rows = share * block_count
    here = lax.axis_index("basin")
    for k, in_ref in zip(partners(len(in_refs), "back"), in_refs):
        source = here ^ k
        for r in range(reach_count):
            piece = in_ref[r * rows : (r + 1) * rows, :].astype(jnp.float32)
            for j in range(share):
                for h in range(block_len // LANES):
                    stage_ref[
                        h,
                        pl.ds(
                            r * block_count * members_dev + share * source + j,
                            block_count,
                            stride=members_dev,
                        ),
                        :,
                    ] = piece[j * block_count : (j + 1) * block_count, h * LANES : (h + 1) * LANES]
    for r in range(reach_count):
        for i in range(block_count):
            at = (r * block_count + i) * members_dev
            for h in range(block_len // LANES):
                lane = i * block_len + h * LANES
                out_ref[r, :, lane : lane + LANES] = stage_ref[
                    h, at : at + members_dev, :
                ].astype(jnp.bfloat16)


def solve_body(base_ref, params_ref, *rest):
    in_refs, (out_ref, all_ref, right_ref) = rest[:-3], rest[-3:]
    shape_count, reach_count, members_dev = params_ref.shape
    groups = len(in_refs)
    members = groups * members_dev
    wide = all_ref.shape[1]
    here = lax.axis_index("member")
    tiles = None
    for k, in_ref in zip(partners(len(in_refs), "member"), in_refs):
        at = pl.multiple_of((here ^ k) * members_dev, members_dev)
        all_ref[pl.ds(at, members_dev), :] = in_ref[:, :wide]
        tile = in_ref[:, wide:]
        tiles = tile if tiles is None else tiles + tile
    scaled = all_ref[...]
    root = jnp.sqrt(jnp.float32(members - 1))
    spread = (scaled - jnp.mean(scaled, axis=0, keepdims=True)) / root
    own = in_refs[0][:, :wide]
    right_ref[:members, :] = spread
    for n in range(base_ref.shape[0]):
        cols = slice(n * base_ref.shape[2], (n + 1) * base_ref.shape[2])
        right_ref[members : members + members_dev, cols] = base_ref[n] - own[:, cols]
    right_ref[members + members_dev :, :] = jnp.zeros(
        (right_ref.shape[0] - members - members_dev, wide), jnp.float32
    )
    system = lax.dot_general(
        spread,
        right_ref[...],
        (((1,), (1,)), ((), ())),
        precision=HIGHEST,
        preferred_element_type=jnp.float32,
    )
    row_at = lax.broadcasted_iota(jnp.int32, system.shape, 0)
    col_at = lax.broadcasted_iota(jnp.int32, system.shape, 1)
    system = system + jnp.where(row_at == col_at, 1.0, 0.0)
    tiles_down = range(0, members, members_dev)
    system = [system[g : g + members_dev] for g in tiles_down]
    tile_row = row_at[:members_dev]
    for first in range(0, members, AHEAD):
        cols = [
            [jnp.broadcast_to(tile[:, i : i + 1], tile.shape) for tile in system]
            for i in range(first, first + AHEAD)
        ]
        for t in range(AHEAD):
            here_tile, here_row = divmod(first + t, members_dev)
            factors = cols[t]
            inverse = 1.0 / factors[here_tile][here_row : here_row + 1, :]
            own_row = tile_row == here_row

            def cleared(tiles):
                pivot_row = tiles[here_tile][here_row : here_row + 1, :] * inverse
                done = [tile - factor * pivot_row for tile, factor in zip(tiles, factors)]
                done[here_tile] = jnp.where(own_row, pivot_row, done[here_tile])
                return done

            system = cleared(system)
            for u in range(t + 1, AHEAD):
                cols[u] = cleared(cols[u])
    system = jnp.concatenate(system, axis=0)
    gain = system[:, members : members + members_dev]
    theta = jnp.concatenate(
        [tiles[:, s * members : (s + 1) * members] for s in range(shape_count)], axis=0
    )
    anomaly = theta - jnp.mean(theta, axis=1, keepdims=True)
    step = (
        jnp.dot(anomaly, gain, precision=HIGHEST, preferred_element_type=jnp.float32) / root
    )
    for s in range(shape_count):
        out_ref[s] = params_ref[s] + step[s * reach_count : (s + 1) * reach_count]


def swapped(pieces, axis, step):
    results = [pieces[0]]
    groups = lax.axis_size("member")
    for piece, *by in zip(pieces[1:], *ORDERS[step]):
        if axis == "member":
            pairs = [(m, m ^ by[m % 2]) for m in range(groups)]
            results.append(lax.ppermute(piece, axis, pairs))
        else:
            pairs = [
                (b * groups + m, (b ^ by[m % 2]) * groups + m)
                for b in range(lax.axis_size(axis))
                for m in range(groups)
            ]
            results.append(lax.ppermute(piece, (axis, "member"), pairs))
    return results


def per_device_split(
    runoff,
    route_params,
    unit_shapes,
    level_map,
    down_map,
    gauge_reach,
    gauge_sigma,
    observed,
    obs_noise,
):
    f32, bf16 = jnp.float32, jnp.bfloat16
    parts, groups = lax.axis_size("basin"), lax.axis_size("member")
    reach_count, members_dev, series_len = runoff.shape
    shape_count, block_len = unit_shapes.shape
    gauge_count = observed.shape[0]
    block_count = series_len // block_len
    share = members_dev // parts
    rows = share * block_count
    total = parts * reach_count
    cap = reach_count // 4
    wide = parts * gauge_count * WINDOWS
    members = members_dev * groups
    sent = pltpu.VMEM((reach_count * rows + reach_count, block_len), bf16)
    sent_back = pltpu.VMEM((reach_count * rows + EXTRA, block_len), bf16)
    base = pltpu.VMEM((members_dev, gauge_count * WINDOWS), f32)
    *packed, own_params, tile, own_base = pl.pallas_call(
        pack_body,
        out_shape=[sent] * parts
        + [pltpu.VMEM(route_params.shape, f32), pltpu.VMEM((reach_count, LANES), f32), base],
        in_specs=[smem()] * 4 + [vmem()] * 4,
        out_specs=[vmem()] * (parts + 3),
        scratch_shapes=[
            pltpu.VMEM((block_len // LANES, reach_count * members_dev * block_count, LANES), f32),
            pltpu.VMEM((reach_count, LANES), f32),
        ],
        name="pack",
    )(level_map, down_map, gauge_reach, gauge_sigma, runoff, route_params, observed, obs_noise)
    arrived = swapped(packed, "basin", "basin")
    conv_table, window_table = kernel_table(unit_shapes, series_len // WINDOWS, wide)
    *routed, base_top = pl.pallas_call(
        functools.partial(
            route_body,
            parts=parts,
            reach_count=reach_count,
            shape_count=shape_count,
            gauge_count=gauge_count,
            members_dev=members_dev,
        ),
        out_shape=[sent_back] * parts + [pltpu.VMEM((parts,) + base.shape, f32)],
        in_specs=[vmem()] * (3 + parts),
        out_specs=[vmem()] * (parts + 1),
        scratch_shapes=[
            pltpu.VMEM((total + 2, rows, block_len), f32),
            pltpu.VMEM((total + 1, rows, block_len), bf16),
            pltpu.VMEM((parts * max(cap, gauge_count) * rows, 2 * block_len), bf16),
            pltpu.VMEM((shape_count * share, total, LANES), f32),
            pltpu.SMEM((LEVELS * parts * cap,), jnp.int32),
        ],
        compiler_params=pltpu.CompilerParams(),
        name="route",
    )(kept(conv_table), kept(window_table), kept(own_base), *map(kept, arrived))
    returned = swapped(routed, "basin", "back")
    local, noise_base = pl.pallas_call(
        functools.partial(gather_body, wide=wide),
        out_shape=[
            pltpu.VMEM((members_dev, wide + LANES), f32),
            pltpu.VMEM((parts,) + base.shape, f32),
        ],
        in_specs=[vmem()] * (2 + parts),
        out_specs=[vmem()] * 2,
        name="gather",
    )(kept(tile), kept(base_top), *map(kept, returned))
    everyone = swapped([local] * groups, "member", "member")
    flows = pl.pallas_call(
        functools.partial(unpack_body, parts=parts, reach_count=reach_count),
        out_shape=jax.ShapeDtypeStruct(runoff.shape, bf16),
        in_specs=[vmem()] * parts,
        out_specs=vmem(),
        scratch_shapes=[pltpu.VMEM((block_len // LANES, reach_count * members_dev * block_count, LANES), f32)],
        name="unpack",
    )(*map(kept, returned))
    updated = pl.pallas_call(
        solve_body,
        out_shape=jax.ShapeDtypeStruct(route_params.shape, f32),
        in_specs=[vmem()] * (2 + groups),
        out_specs=vmem(),
        scratch_shapes=[pltpu.VMEM((members, wide), f32), pltpu.VMEM((LANES, wide), f32)],
        name="solve",
    )(kept(noise_base), kept(own_params), *map(kept, everyone))
    return flows, updated


def per_device(*args):
    runoff, route_params, unit_shapes, _, _, _, _, observed, _ = args
    parts, groups = lax.axis_size("basin"), lax.axis_size("member")
    reach_count, members_dev, series_len = runoff.shape
    shape_count, block_len = unit_shapes.shape
    block_count = series_len // block_len
    gauge_count = observed.shape[0]
    wide = parts * gauge_count * WINDOWS
    share = max(members_dev // parts, 1)
    fits = (
        parts == 4
        and groups == 4
        and members_dev == share * parts
        and reach_count == 8
        and members_dev == 8
        and block_count == 8
        and series_len % block_len == 0
        and block_len == 2 * LANES
        and gauge_count * WINDOWS == LANES
        and wide % block_len == 0
        and members_dev // 2 + 3 * share * (wide // block_len) <= EXTRA
        and shape_count * members_dev + reach_count // 4 + 2 <= LANES // parts
        and 2 * reach_count < CODE
        and parts >= 2
        and reach_count == LEVELS
        and shape_count * groups * members_dev <= LANES
        and groups * members_dev + members_dev <= LANES
    )
    if fits:
        return per_device_split(*args)
    return per_device_chain(*args)


def passed_along(x, axis, by):
    length = lax.axis_size(axis)
    pairs = [(i, i + by) for i in range(length) if 0 <= i + by < length]
    return lax.ppermute(x, axis, pairs)


def route_rows(inflow_rows, slot_weights, conv_table):
    block_len = conv_table.shape[0] // 2
    row_count, series_len = inflow_rows.shape
    blocks = inflow_rows.reshape(row_count, series_len // block_len, block_len)
    earlier = jnp.concatenate([jnp.zeros_like(blocks[:, :1]), blocks[:, :-1]], axis=1)
    joined = jnp.concatenate([blocks, earlier], axis=2).reshape(-1, 2 * block_len)
    mixed_blocks = jnp.dot(joined, conv_table, preferred_element_type=jnp.float32)
    mixed_blocks = mixed_blocks.reshape(
        row_count, series_len // block_len, slot_weights.shape[1], block_len
    )
    return jnp.sum(mixed_blocks * slot_weights[:, None, :, None], axis=2).reshape(
        row_count, series_len
    )


def level_select(level_block, down_block, level_now, slot_count):
    entry_count = level_block.shape[0]
    entry_ids = jnp.arange(entry_count, dtype=jnp.int32)
    in_level = level_block == level_now
    before = (entry_ids[None, :] < entry_ids[:, None]) & in_level[None, :]
    rank = jnp.sum(before.astype(jnp.int32), axis=1)
    slot_ids = jnp.arange(slot_count, dtype=jnp.int32)
    select = (rank[None, :] == slot_ids[:, None]) & in_level[None, :]
    slot_valid = slot_ids < jnp.sum(in_level.astype(jnp.int32))
    slot_target = jnp.sum(jnp.where(select, down_block[None, :], 0), axis=1)
    return (select, slot_valid, slot_target)


def per_device_chain(
    runoff,
    route_params,
    unit_shapes,
    level_map,
    down_map,
    gauge_reach,
    gauge_sigma,
    observed,
    obs_noise,
):
    conv_table, _ = kernel_table(unit_shapes, runoff.shape[2] // WINDOWS, LANES)
    reach_count, members_dev, series_len = runoff.shape
    flat_len = members_dev * series_len
    slot_count = reach_count // 4
    shape_count = route_params.shape[0]
    inflow = runoff.astype(jnp.float32).reshape(reach_count, flat_len)
    outflow = jnp.zeros_like(inflow)
    reach_ids = jnp.arange(reach_count, dtype=jnp.int32)[:, None]
    params_rows = jnp.transpose(route_params, (1, 2, 0))
    prev_level, prev_down = passed_along((level_map, down_map), "basin", 1)
    for level_now in range(LEVELS):
        select, slot_valid, slot_target_row = level_select(
            level_map, down_map, level_now, slot_count
        )
        gathered = jnp.dot(
            select.astype(jnp.bfloat16),
            inflow.astype(jnp.bfloat16),
            preferred_element_type=jnp.float32,
        )
        gathered = gathered.astype(jnp.bfloat16).reshape(slot_count * members_dev, series_len)
        slot_weights = jnp.einsum(
            "cr,rms->cms", select.astype(jnp.float32), params_rows, precision=lax.Precision.HIGHEST
        ).reshape(-1, shape_count)
        routed = (
            route_rows(gathered, slot_weights, conv_table)
            .astype(jnp.bfloat16)
            .reshape(slot_count, flat_len)
        )
        slot_target = slot_target_row[None, :]
        slot_mask = slot_valid[None, :]
        local_edges = (slot_target == reach_ids) & slot_mask
        chosen = jnp.transpose(select) & slot_mask
        edge_matrix = jnp.concatenate([local_edges, chosen], axis=0).astype(jnp.bfloat16)
        spread_flows = jnp.dot(edge_matrix, routed, preferred_element_type=jnp.float32)
        inflow = inflow + spread_flows[:reach_count]
        outflow = outflow + spread_flows[reach_count:]
        if level_now + 1 < LEVELS:
            arrived = passed_along(routed, "basin", 1)
            prev_select, prev_valid, prev_target = level_select(
                prev_level, prev_down, level_now, slot_count
            )
            incoming = (prev_target[None, :] == reach_ids + reach_count) & prev_valid[None, :]
            inflow = inflow + jnp.dot(
                incoming.astype(jnp.bfloat16), arrived, preferred_element_type=jnp.float32
            )
    flows = outflow.astype(jnp.bfloat16)
    gauge_pick = (gauge_reach[:, None] == jnp.arange(reach_count, dtype=jnp.int32)[None, :]).astype(
        jnp.bfloat16
    )
    gauged = jnp.dot(gauge_pick, flows, preferred_element_type=jnp.float32)
    predicted = jnp.mean(gauged.reshape(-1, members_dev, WINDOWS, series_len // WINDOWS), axis=3)
    scaled = predicted / gauge_sigma[:, None, None]
    innovation = observed[:, None, :] / gauge_sigma[:, None, None] + obs_noise - scaled
    scaled = jnp.transpose(scaled, (0, 2, 1))
    innovation = jnp.transpose(innovation, (0, 2, 1))
    scaled, innovation = (
        lax.all_gather(scaled, "member", axis=2, tiled=True),
        lax.all_gather(innovation, "member", axis=2, tiled=True),
    )
    members = scaled.shape[2]
    scaled = scaled.reshape(-1, members)
    innovation = innovation.reshape(-1, members)
    spread = (scaled - jnp.mean(scaled, axis=1, keepdims=True)) / jnp.sqrt(members - 1.0)
    gram_part = jnp.dot(spread.T, spread, precision=lax.Precision.HIGHEST)
    cross_part = jnp.dot(spread.T, innovation, precision=lax.Precision.HIGHEST)
    gram_part, cross_part = lax.psum((gram_part, cross_part), "basin")
    gram = jnp.eye(members, dtype=jnp.float32) + gram_part
    factor = jnp.linalg.cholesky(gram)
    kalman_gain = jax.scipy.linalg.cho_solve((factor, True), cross_part)
    col_start = lax.axis_index("member") * members_dev
    all_params = lax.all_gather(route_params, "member", axis=2, tiled=True).reshape(-1, members)
    anomaly = all_params - jnp.mean(all_params, axis=1, keepdims=True)
    columns = lax.dynamic_slice_in_dim(kalman_gain, col_start, members_dev, 1)
    increment = jnp.dot(anomaly, columns, precision=lax.Precision.HIGHEST)
    updated = route_params.reshape(-1, members_dev) + increment / jnp.sqrt(members - 1.0)
    return (
        flows.reshape(reach_count, members_dev, series_len),
        updated.reshape(route_params.shape),
    )


def solution(mesh):
    return jax.shard_map(
        per_device,
        mesh=mesh,
        in_specs=(
            P(("groups", "basin"), "member", None),
            P(None, ("groups", "basin"), "member"),
            P(),
            P(("groups", "basin")),
            P(("groups", "basin")),
            P(("groups", "basin")),
            P(("groups", "basin")),
            P(("groups", "basin"), None),
            P(("groups", "basin"), "member", None),
        ),
        out_specs=(P(("groups", "basin"), "member", None), P(None, ("groups", "basin"), "member")),
        check_vma=False,
    )
```
